32 devices in a mesh: dp: 16 (over z, y, x), rep: 2 (over core).
Axes of the slice: x: 2, y: 2, z: 4, core: 2. Of those that a mesh axis runs over, the one named last changes fastest.
Arguments:
- tokens: bfloat16 [65536, 768], P(('dp', 'rep')), may hold values from -6 to 6
- flags: int32 [65536], P(('dp', 'rep')), may hold values from 0 to 1, as said below
- mask_embed: bfloat16 [768], replicated, may hold values from -6 to 6
- cotangent: bfloat16 [65536, 768], P(('dp', 'rep')), may hold values from -6 to 6
- w_qkv: float32 [768, 2304], P('dp'), may hold values from -0.21875 to 0.21875
- b_qv: float32 [2, 768], P(None, 'dp'), may hold values from -4 to 4
- w_out: float32 [768, 768], P('dp'), may hold values from -1.25 to 1.25
- b_out: float32 [768], P('dp'), may hold values from -4 to 4
- norm_one: float32 [2, 768], P(None, 'dp'), as said below
- w_up: float32 [768, 3072], P('dp'), may hold values from -0.21875 to 0.21875
- b_up: float32 [3072], P('dp'), may hold values from -4 to 4
- w_down: float32 [3072, 768], P('dp'), may hold values from -0.109375 to 0.109375
- b_down: float32 [768], P('dp'), may hold values from -4 to 4
- norm_two: float32 [2, 768], P(None, 'dp'), as said below
Outputs:
- activations: bfloat16 [65536, 768], P(('dp', 'rep'))
- input_grad: float32 [65536, 768], P(('dp', 'rep'))
- grad_w_qkv: float32 [768, 2304], P('dp')
- grad_b_qv: float32 [2, 768], P(None, 'dp')
- grad_w_out: float32 [768, 768], P('dp')
- grad_b_out: float32 [768], P('dp')
- grad_norm_one: float32 [2, 768], P(None, 'dp')
- grad_w_up: float32 [768, 3072], P('dp')
- grad_b_up: float32 [3072], P('dp')
- grad_w_down: float32 [3072, 768], P('dp')
- grad_b_down: float32 [768], P('dp')
- grad_norm_two: float32 [2, 768], P(None, 'dp')
The draws below stay inside these ranges and needn't reach their ends.
Inputs may be any that keep to these rules, and one draw needn't show every extreme that they name: `flags`: within each sequence of 512 tokens the ones form spans; the share of masked tokens differs from sequence to sequence. `norm_one`: row 0 is a gain near 1, row 1 a shift. `norm_two`: row 0 is a gain near 1, row 1 a shift.
All inputs are finite; a program needn't handle non-finite values.
Results may differ from the reference program's by a relative error of at most 0.015.
Values may be sent and summed in bfloat16 or wider, within the bound.
A program may use at most 320 MiB of HBM per device.

```python
import math
import jax
import jax.numpy as jnp
from jax import lax

D = 768
HEADS = 12
HEAD = 64
FF = 3072
SEQ = 512
TOKENS = 65536


def draw_flags(key, part):
    sequences = TOKENS // SEQ
    key_rate, key_start, key_length = jax.random.split(key, 3)
    rate = jax.random.randint(key_rate, (sequences, 1), 15, 60)
    starts = (jax.random.randint(key_start, (sequences, SEQ), 0, 1000) < rate).astype(jnp.int32)
    trials = (jax.random.randint(key_length, (sequences, SEQ, 9), 0, 10) < 8).astype(jnp.int32)
    length = 1 + jnp.sum(jnp.cumprod(trials, axis=-1), axis=-1)
    covered = jnp.zeros((sequences, SEQ), jnp.int32)
    for offset in range(10):
        moved_start = jnp.pad(starts, ((0, 0), (offset, 0)))[:, :SEQ]
        moved_length = jnp.pad(length, ((0, 0), (offset, 0)))[:, :SEQ]
        covered = jnp.maximum(covered, moved_start * (moved_length > offset).astype(jnp.int32))
    return covered.reshape(TOKENS)


def norm_pair(key):
    key_gain, key_shift = jax.random.split(key)
    gain = 1.0 + 0.2 * jax.random.uniform(key_gain, (D,), jnp.float32, -1.0, 1.0)
    shift = 0.3 * jax.random.normal(key_shift, (D,), jnp.float32)
    return jnp.stack([gain, shift]).astype(jnp.float32)


def draw_norm_one(key, part):
    return norm_pair(jax.random.fold_in(key, 11))


def draw_norm_two(key, part):
    return norm_pair(jax.random.fold_in(key, 23))


def block_levels(key, shape, pieces, low, high):
    level = 1.0
    for axis_at, blocks in pieces:
        steps = jax.random.uniform(jax.random.fold_in(jax.random.fold_in(key, 6), axis_at), (blocks,), jnp.float32, low / len(pieces), high / len(pieces))
        level = level * jnp.repeat(jnp.exp(steps), shape[axis_at] // blocks).reshape((-1,) + (1,) * (len(shape) - 1 - axis_at))
    return level


def scatter_about(own_key, dims, scale, bound, shards=(), dtype=jnp.bfloat16):
    values = scale * jax.random.normal(own_key, dims, jnp.float32)
    if shards:
        values = values * block_levels(own_key, dims, shards, -0.22, 0.18)
    return jnp.clip(values, -bound, bound).astype(dtype)


def setup_inputs(seed: int = 0) -> dict:
    key_list = jax.random.split(jax.random.key(seed), 15)
    tokens = scatter_about(key_list[0], (TOKENS, D), 1.0, 6.0, ((0, 32),))
    flags = draw_flags(jax.random.fold_in(key_list[14], 71), 0)
    mask_embed = scatter_about(key_list[2], (D,), 1.0, 6.0)
    cotangent = scatter_about(key_list[3], (TOKENS, D), 1.0, 6.0, ((0, 32),))
    w_qkv = scatter_about(key_list[4], (D, 3 * D), D ** -0.5, 0.21875, ((0, 16),), jnp.float32)
    b_qv = scatter_about(key_list[5], (2, D), 0.3, 4.0, ((1, 16),), jnp.float32)
    w_out = scatter_about(key_list[6], (D, D), (D // 32) ** -0.5, 1.25, ((0, 16),), jnp.float32)
    b_out = scatter_about(key_list[7], (D,), 0.3, 4.0, ((0, 16),), jnp.float32)
    norm_one = draw_norm_one(jax.random.fold_in(key_list[14], 71), 0)
    w_up = scatter_about(key_list[9], (D, FF), D ** -0.5, 0.21875, ((0, 16),), jnp.float32)
    b_up = scatter_about(key_list[10], (FF,), 0.3, 4.0, ((0, 16),), jnp.float32)
    w_down = scatter_about(key_list[11], (FF, D), FF ** -0.5, 0.109375, ((0, 16),), jnp.float32)
    b_down = scatter_about(key_list[12], (D,), 0.3, 4.0, ((0, 16),), jnp.float32)
    norm_two = draw_norm_two(jax.random.fold_in(key_list[14], 71), 0)
    return dict(tokens=tokens, flags=flags, mask_embed=mask_embed, cotangent=cotangent, w_qkv=w_qkv, b_qv=b_qv, w_out=w_out, b_out=b_out, norm_one=norm_one, w_up=w_up, b_up=b_up, w_down=w_down, b_down=b_down, norm_two=norm_two)


@jax.custom_vjp
def low(v):
    return lax.optimization_barrier(v.astype(jnp.bfloat16)).astype(jnp.float32)

@jax.custom_vjp
def low_back(v):
    return v

def low_keep(v):
    return (low(v), None)

def low_pass(kept, grad):
    return (grad,)

def back_keep(v):
    return (v, None)

def back_low(kept, grad):
    return (low(grad),)
low.defvjp(low_keep, low_pass)
low_back.defvjp(back_keep, back_low)

def matmul_high(left, right):
    return jnp.matmul(left, right, precision=lax.Precision.HIGHEST)

def normalize(values, params):
    center = values - lax.optimization_barrier(jnp.mean(values, axis=-1, keepdims=True))
    inverse = lax.rsqrt(lax.optimization_barrier(jnp.mean(center * center, axis=-1, keepdims=True)) + 1e-12)
    return center * inverse * params[0] + params[1]

def layer(inputs, params):
    w_qkv, b_qv, w_out, b_out, norm_one, w_up, b_up, w_down, b_down, norm_two = [low(item) for item in params]
    groups, length, width = inputs.shape
    bias = jnp.concatenate([b_qv[0], jnp.zeros_like(b_qv[0]), b_qv[1]])
    projected = low(low_back(matmul_high(inputs, w_qkv) + bias))
    query = projected[..., :width].reshape(groups, length, HEADS, HEAD)
    keys = projected[..., width:2 * width].reshape(groups, length, HEADS, HEAD)
    vals = projected[..., 2 * width:].reshape(groups, length, HEADS, HEAD)
    scores = jnp.einsum('gqhe,gkhe->ghqk', query, keys, precision=lax.Precision.HIGHEST) * HEAD ** (-0.5)
    scores = low_back(scores)
    top = lax.optimization_barrier(jnp.max(scores, axis=-1, keepdims=True))
    expo = jnp.exp(scores - top)
    probs = low(expo / lax.optimization_barrier(jnp.sum(expo, axis=-1, keepdims=True)))
    mixed = jnp.einsum('ghqk,gkhe->gqhe', probs, vals, precision=lax.Precision.HIGHEST).reshape(groups, length, width)
    mixed = low(low_back(mixed))
    attended = low_back(matmul_high(mixed, w_out) + b_out)
    first = normalize(inputs + attended, norm_one)
    upper = low_back(matmul_high(low(first), w_up) + b_up)
    acts = low(jax.nn.gelu(upper, approximate=False))
    lowered = low_back(matmul_high(acts, w_down) + b_down)
    return normalize(first + lowered, norm_two)

def reference(tokens, flags, mask_embed, cotangent, w_qkv, b_qv, w_out, b_out, norm_one, w_up, b_up, w_down, b_down, norm_two):
    params = tuple((item.astype(jnp.float32) for item in (w_qkv, b_qv, w_out, b_out, norm_one, w_up, b_up, w_down, b_down, norm_two)))
    masked = (flags > 0)[:, None]
    inputs = jnp.where(masked, mask_embed.astype(jnp.float32)[None, :], tokens.astype(jnp.float32))
    out_grad = jnp.where(masked, cotangent.astype(jnp.float32), jnp.float32(0.0))
    sequences = TOKENS // SEQ
    group = math.gcd(sequences, max(1, 4096 // SEQ))
    steps_count = sequences // group
    inputs_grouped = inputs.reshape(steps_count, group, SEQ, D)
    grads_grouped = out_grad.reshape(steps_count, group, SEQ, D)

    def advance(totals, item):
        block_in, block_grad = item
        result, pull = jax.vjp(layer, block_in, params)
        grad_in, grad_params = pull(block_grad)
        totals = jax.tree.map(lambda left, right: left + right, totals, grad_params)
        return (totals, (result, grad_in))
    zeros = tuple((jnp.zeros_like(item) for item in params))
    grads, (results, grad_inputs) = lax.scan(advance, zeros, (inputs_grouped, grads_grouped))
    activations = results.reshape(TOKENS, D).astype(jnp.bfloat16)
    input_grad = jnp.where(masked, jnp.float32(0.0), grad_inputs.reshape(TOKENS, D))
    return (activations, input_grad, grads[0], grads[1], grads[2], grads[3], grads[4], grads[5], grads[6], grads[7], grads[8], grads[9])
```

```python
import functools

import jax
import jax.numpy as jnp
from jax import lax
from jax.experimental import pallas as pl
from jax.experimental.pallas import tpu as pltpu
from jax.sharding import PartitionSpec as P

HEADS = 12
SEQ = 512
EPS = 1e-12
half = jnp.bfloat16
single = jnp.float32
VMEM_LIMIT = 61 * 1024 * 1024


def mm(left, right):
    return jnp.dot(left, right, preferred_element_type=single)


def mm_tb(left, right):
    return lax.dot_general(left, right, (((1,), (1,)), ((), ())), preferred_element_type=single)


def mm_ta(left, right):
    return lax.dot_general(left, right, (((0,), (0,)), ((), ())), preferred_element_type=single)


def row_mean(values):
    return jnp.mean(values, axis=-1, keepdims=True)


def col_sum(values):
    return jnp.sum(values, axis=0, keepdims=True)


def project_body(tok_ref, flag_ref, mask_ref, w_ref, bias_ref, inp_ref, proj_ref):
    masked = flag_ref[...] > 0
    inputs = jnp.where(masked, mask_ref[...].astype(single), tok_ref[...].astype(single))
    low = inputs.astype(half)
    inp_ref[...] = low
    proj_ref[...] = (mm(low, w_ref[...]) + bias_ref[...]).astype(half)


def project(tokens, flags, mask_embed, w_qkv, bias):
    count, width = tokens.shape
    block = 256
    wide = w_qkv.shape[1]
    return pl.pallas_call(
        project_body,
        grid=(count // block,),
        in_specs=[
            pl.BlockSpec((block, width), lambda i: (i, 0)),
            pl.BlockSpec((block, 1), lambda i: (i, 0)),
            pl.BlockSpec((1, width), lambda i: (0, 0)),
            pl.BlockSpec((width, wide), lambda i: (0, 0), pipeline_mode=pl.Buffered(1)),
            pl.BlockSpec((1, wide), lambda i: (0, 0)),
        ],
        out_specs=[
            pl.BlockSpec((block, width), lambda i: (i, 0)),
            pl.BlockSpec((block, wide), lambda i: (i, 0)),
        ],
        out_shape=[
            jax.ShapeDtypeStruct((count, width), half),
            jax.ShapeDtypeStruct((count, wide), half),
        ],
        compiler_params=pltpu.CompilerParams(vmem_limit_bytes=VMEM_LIMIT),
        name="project",
    )(tokens, flags, mask_embed, w_qkv, bias)


def head_masks(width):
    lane = lax.broadcasted_iota(jnp.int32, (1, width), 1)
    return [(lane // 64) == h for h in range(width // 64)]


def attend_pair(query, keys, vals):
    scaled = query * half(0.125)
    turned = vals.T
    outs, logs = [], []
    for h, mask in enumerate(head_masks(128)):
        own = jnp.where(mask, keys, half(0))
        scores = mm_tb(own, scaled)
        top = jnp.max(scores, axis=0, keepdims=True)
        expo = jnp.exp(scores - top)
        total = jnp.sum(expo, axis=0, keepdims=True)
        mixed = mm(turned[64 * h : 64 * h + 64], expo.astype(half))
        outs.append(mixed * (1.0 / total))
        logs.append(top + jnp.log(total))
    return jnp.concatenate(outs, axis=0).astype(half).T, logs


def attend_body(pairs, q_ref, k_ref, v_ref, mixed_ref, log_ref):
    for p in range(pairs):
        cols = pl.ds(128 * p, 128)
        mixed, logs = attend_pair(q_ref[:, cols], k_ref[:, cols], v_ref[:, cols])
        mixed_ref[:, cols] = mixed
        for h in range(2):
            log_ref[0, 0, pl.ds(2 * p + h, 1), :] = logs[h]


def attend(projected, pairs=2):
    count = projected.shape[0]
    width = projected.shape[1] // 3
    groups = count // SEQ
    steps = width // (128 * pairs)
    spec = lambda part: pl.BlockSpec((SEQ, 128 * pairs), lambda g, p: (g, part * steps + p))
    return pl.pallas_call(
        functools.partial(attend_body, pairs),
        grid=(groups, steps),
        in_specs=[spec(0), spec(1), spec(2)],
        out_specs=[
            pl.BlockSpec((SEQ, 128 * pairs), lambda g, p: (g, p)),
            pl.BlockSpec((1, 1, 8, SEQ), lambda g, p: (g, p, 0, 0)),
        ],
        out_shape=[
            jax.ShapeDtypeStruct((count, width), half),
            jax.ShapeDtypeStruct((groups, steps, 8, SEQ), single),
        ],
        compiler_params=pltpu.CompilerParams(vmem_limit_bytes=VMEM_LIMIT),
        name="attend",
    )(projected, projected, projected)


def attend_back_pair(query, keys, vals, grad, mixed, logs):
    scaled = query * half(0.125)
    scaled_keys = keys * half(0.125)
    product = grad.astype(single) * mixed.astype(single)
    grad_turned = grad.T
    scaled_turned = scaled.T
    d_vals, d_keys, d_query = [], [], None
    for h, mask in enumerate(head_masks(128)):
        scores = mm_tb(jnp.where(mask, scaled, half(0)), keys)
        probs = jnp.exp(scores - logs[:, h : h + 1])
        d_probs = mm_tb(jnp.where(mask, grad, half(0)), vals)
        delta = jnp.sum(jnp.where(mask, product, 0.0), axis=1, keepdims=True)
        d_scores = (probs * (d_probs - delta)).astype(half)
        rows = slice(64 * h, 64 * h + 64)
        d_vals.append(mm(grad_turned[rows], probs.astype(half)))
        d_keys.append(mm(scaled_turned[rows], d_scores))
        part = mm(d_scores, jnp.where(mask, scaled_keys, half(0)))
        d_query = part if d_query is None else d_query + part
    turn = lambda parts: jnp.concatenate(parts, axis=0).astype(half).T
    return d_query.astype(half), turn(d_keys), turn(d_vals)


def attend_back_body(pairs, q_ref, k_ref, v_ref, grad_ref, mixed_ref, log_ref, dq_ref, dk_ref, dv_ref):
    logs = log_ref[0, 0].T
    for p in range(pairs):
        cols = pl.ds(128 * p, 128)
        dq, dk, dv = attend_back_pair(
            q_ref[:, cols],
            k_ref[:, cols],
            v_ref[:, cols],
            grad_ref[:, cols],
            mixed_ref[:, cols],
            logs[:, 2 * p : 2 * p + 2],
        )
        dq_ref[:, cols] = dq
        dk_ref[:, cols] = dk
        dv_ref[:, cols] = dv


def attend_back(projected, d_mixed, mixed, logs, pairs=2):
    count, width = mixed.shape
    groups = count // SEQ
    steps = width // (128 * pairs)
    spec = lambda part: pl.BlockSpec((SEQ, 128 * pairs), lambda g, p: (g, part * steps + p))
    out = pl.BlockSpec((SEQ, 128 * pairs), lambda g, p: (g, p))
    return pl.pallas_call(
        functools.partial(attend_back_body, pairs),
        grid=(groups, steps),
        in_specs=[
            spec(0),
            spec(1),
            spec(2),
            out,
            out,
            pl.BlockSpec((1, 1, 8, SEQ), lambda g, p: (g, p, 0, 0)),
        ],
        out_specs=[out] * 3,
        out_shape=[jax.ShapeDtypeStruct((count, width), half)] * 3,
        compiler_params=pltpu.CompilerParams(vmem_limit_bytes=VMEM_LIMIT),
        name="attend_back",
    )(projected, projected, projected, d_mixed, mixed, logs)


def norm(values, gain, shift):
    center = values - row_mean(values)
    inverse = lax.rsqrt(row_mean(center * center) + EPS)
    unit = center * inverse
    return unit * gain + shift, unit, inverse


def norm_back(grad, unit, inverse, gain):
    scaled = grad * gain
    return inverse * (scaled - row_mean(scaled) - unit * row_mean(scaled * unit))


def middle_body(
    mixed_ref,
    inp_ref,
    flag_ref,
    cot_ref,
    vec_ref,
    bup_ref,
    wo_ref,
    wu_ref,
    wd_ref,
    act_out,
    dsum_out,
    dmix_out,
    small_out,
    gbup_out,
    gwo_out,
    gwu_out,
    gwd_out,
    unit1,
    first,
    low,
    acts,
    slope,
    total,
    d_low,
    acc_o,
    acc_u,
    acc_d,
    stage,
    sems,
):
    step = pl.program_id(0)
    last = pl.num_programs(0) - 1
    width = wo_ref.shape[0]
    chunks = wd_ref.shape[0] // width

    @pl.when(step == 0)
    def _():
        small_out[...] = jnp.zeros_like(small_out)
        gbup_out[...] = jnp.zeros_like(gbup_out)
        acc_o[...] = jnp.zeros_like(acc_o)
        acc_u[...] = jnp.zeros_like(acc_u)
        acc_d[...] = jnp.zeros_like(acc_d)

    vec = lambda row: vec_ref[pl.ds(row, 1), :]
    attended = mm(mixed_ref[...], wo_ref[...]) + vec(2)
    value, unit, inv1 = norm(inp_ref[...].astype(single) + attended, vec(3), vec(4))
    unit1[...] = unit
    first[...] = value
    low[...] = value.astype(half)
    total[...] = jnp.zeros_like(total)

    @pl.loop(0, chunks)
    def _(j):
        cols = pl.ds(pl.multiple_of(j * width, width), width)
        upper = mm(low[...], wu_ref[:, cols]) + bup_ref[:, cols]
        phi = 0.5 * (1.0 + lax.erf(upper * 0.7071067811865476))
        act = (upper * phi).astype(half)
        acts[j] = act
        slope[j] = (phi + upper * jnp.exp(-0.5 * upper * upper) * 0.3989422804014327).astype(half)
        total[...] += mm(act, wd_ref[cols, :])

    value, unit, inv2 = norm(first[...] + total[...] + vec(5), vec(6), vec(7))
    act_out[...] = value.astype(half)
    out_grad = jnp.where(flag_ref[...] > 0, cot_ref[...].astype(single), 0.0)
    small_out[pl.ds(6, 1), :] += col_sum(out_grad * unit)
    small_out[pl.ds(7, 1), :] += col_sum(out_grad)
    d_second = norm_back(out_grad, unit, inv2, vec(6))
    lowered = d_second.astype(half)
    d_low[...] = lowered
    small_out[pl.ds(5, 1), :] += col_sum(lowered.astype(single))
    total[...] = d_second

    @pl.loop(0, chunks)
    def _(j):
        cols = pl.ds(pl.multiple_of(j * width, width), width)
        d_acts = mm_tb(d_low[...], wd_ref[cols, :])
        d_upper = (d_acts * slope[j].astype(single)).astype(half)
        gbup_out[:, cols] += col_sum(d_upper.astype(single))
        total[...] += mm_tb(d_upper, wu_ref[:, cols])
        acc_d[j] += mm_ta(acts[j], d_low[...])
        acc_u[j] += mm_ta(low[...], d_upper)

    d_first = total[...]
    unit = unit1[...]
    small_out[pl.ds(3, 1), :] += col_sum(d_first * unit)
    small_out[pl.ds(4, 1), :] += col_sum(d_first)
    d_sum = norm_back(d_first, unit, inv1, vec(3))
    dsum_out[...] = d_sum
    d_att = d_sum.astype(half)
    small_out[pl.ds(2, 1), :] += col_sum(d_att.astype(single))
    dmix_out[...] = mm_tb(d_att, wo_ref[...]).astype(half)
    acc_o[...] += mm_ta(mixed_ref[...], d_att)

    @pl.when(step == last)
    def _():
        copies = []
        todo = [(acc_d.at[j], gwd_out.at[pl.ds(j * width, width), :]) for j in range(chunks)]
        todo += [(acc_u.at[j], gwu_out.at[:, pl.ds(j * width, width)]) for j in range(chunks)]
        todo += [(acc_o, gwo_out)]
        for n, (src, dst) in enumerate(todo):
            slot = n % 2
            if n >= 2:
                copies[n - 2].wait()
            stage[slot] = src[...].astype(half)
            copies.append(pltpu.make_async_copy(stage.at[slot], dst, sems.at[slot]))
            copies[n].start()
        for copy in copies[-2:]:
            copy.wait()


def middle(mixed, inputs, flags, cotangent, vecs, b_up, w_out, w_up, w_down, block=512):
    count, width = mixed.shape
    hidden = w_up.shape[1]
    chunks = hidden // width
    rows = lambda cols: pl.BlockSpec((block, cols), lambda i: (i, 0))
    once = lambda shape: pl.BlockSpec(shape, lambda i: (0, 0), pipeline_mode=pl.Buffered(1))
    keep = lambda shape: pl.BlockSpec(shape, lambda i: (0, 0))
    whole = pl.BlockSpec(memory_space=pl.ANY)
    return pl.pallas_call(
        middle_body,
        grid=(count // block,),
        in_specs=[
            rows(width),
            rows(width),
            rows(1),
            rows(width),
            keep((8, width)),
            keep((1, hidden)),
            once((width, width)),
            once((width, hidden)),
            once((hidden, width)),
        ],
        out_specs=[
            rows(width),
            rows(width),
            rows(width),
            keep((8, width)),
            keep((1, hidden)),
            whole,
            whole,
            whole,
        ],
        out_shape=[
            jax.ShapeDtypeStruct((count, width), half),
            jax.ShapeDtypeStruct((count, width), single),
            jax.ShapeDtypeStruct((count, width), half),
            jax.ShapeDtypeStruct((8, width), single),
            jax.ShapeDtypeStruct((1, hidden), single),
            jax.ShapeDtypeStruct((width, width), half),
            jax.ShapeDtypeStruct((width, hidden), half),
            jax.ShapeDtypeStruct((hidden, width), half),
        ],
        scratch_shapes=[
            pltpu.VMEM((block, width), single),
            pltpu.VMEM((block, width), single),
            pltpu.VMEM((block, width), half),
            pltpu.VMEM((chunks, block, width), half),
            pltpu.VMEM((chunks, block, width), half),
            pltpu.VMEM((block, width), single),
            pltpu.VMEM((block, width), half),
            pltpu.VMEM((width, width), single),
            pltpu.VMEM((chunks, width, width), single),
            pltpu.VMEM((chunks, width, width), single),
            pltpu.VMEM((2, width, width), half),
            pltpu.SemaphoreType.DMA((2,)),
        ],
        compiler_params=pltpu.CompilerParams(vmem_limit_bytes=VMEM_LIMIT),
        name="middle",
    )(mixed, inputs, flags, cotangent, vecs, b_up, w_out, w_up, w_down)


def weight_back_body(inp_ref, dq_ref, dk_ref, dv_ref, out_ref, sum_ref):
    part = pl.program_id(0)

    def work(ref):
        grad = ref[...]
        out_ref[...] = mm_ta(inp_ref[...], grad).astype(half)
        sum_ref[...] = jnp.broadcast_to(col_sum(grad.astype(single)), sum_ref.shape)

    for n, ref in enumerate((dq_ref, dk_ref, dv_ref)):
        pl.when(part == n)(functools.partial(work, ref))


def weight_back(inputs, d_parts, block=256):
    count, width = inputs.shape
    steps = width // block

    def spec(n):
        return pl.BlockSpec(
            (count, block), lambda p, i: (0, jnp.where(p == n, i, jnp.where(p > n, steps - 1, 0)))
        )

    return pl.pallas_call(
        weight_back_body,
        grid=(3, steps),
        in_specs=[pl.BlockSpec((count, width), lambda p, i: (0, 0), pipeline_mode=pl.Buffered(1))]
        + [spec(n) for n in range(3)],
        out_specs=[
            pl.BlockSpec((width, block), lambda p, i: (0, p * steps + i)),
            pl.BlockSpec((8, block), lambda p, i: (0, p * steps + i)),
        ],
        out_shape=[
            jax.ShapeDtypeStruct((width, 3 * width), half),
            jax.ShapeDtypeStruct((8, 3 * width), single),
        ],
        compiler_params=pltpu.CompilerParams(vmem_limit_bytes=VMEM_LIMIT),
        name="weight_back",
    )(inputs, *d_parts)


def input_back_body(dq_ref, dk_ref, dv_ref, w_ref, dsum_ref, flag_ref, out_ref):
    width = dq_ref.shape[1]
    grad = dsum_ref[...]
    for part, ref in enumerate((dq_ref, dk_ref, dv_ref)):
        grad = grad + mm_tb(ref[...], w_ref[:, pl.ds(part * width, width)])
    out_ref[...] = jnp.where(flag_ref[...] > 0, 0.0, grad)


def input_back(d_parts, w_qkv, d_sum, flags, block=256):
    count, width = d_sum.shape
    spec = pl.BlockSpec((block, width), lambda i: (i, 0))
    return pl.pallas_call(
        input_back_body,
        grid=(count // block,),
        in_specs=[spec] * 3
        + [
            pl.BlockSpec(w_qkv.shape, lambda i: (0, 0), pipeline_mode=pl.Buffered(1)),
            spec,
            pl.BlockSpec((block, 1), lambda i: (i, 0)),
        ],
        out_specs=spec,
        out_shape=jax.ShapeDtypeStruct((count, width), single),
        compiler_params=pltpu.CompilerParams(vmem_limit_bytes=VMEM_LIMIT),
        name="input_back",
    )(*d_parts, w_qkv, d_sum, flags)


MESH = pl.DeviceIdType.MESH
ZS = 4


class Place:
    def __init__(self):
        self.me = lax.axis_index("dp")
        self.core = lax.axis_index("rep")
        self.z = self.me // 4
        self.y = (self.me // 2) % 2
        self.x = self.me % 2
        step_x = 1 - 2 * self.x
        step_y = 2 - 4 * self.y
        self.near = self.me + step_x + self.core * (step_y - step_x)
        self.far = self.me + step_y + self.core * (step_x - step_y)
        self.diag = self.me + step_x + step_y
        self.near_bit = self.x + self.core * (self.y - self.x)
        self.far_bit = self.y + self.core * (self.x - self.y)

    def chip(self, z, far, near):
        return z * 4 + far * (2 - self.core) + near * (1 + self.core)

    def partner(self):
        return (self.me, 1 - self.core)

    def barrier(self):
        sem = pltpu.get_barrier_semaphore()
        tell = lambda dev: pl.semaphore_signal(sem, inc=1, device_id=dev, device_id_type=MESH)
        tell(self.partner())
        tell((self.near, self.core))
        tell((self.far, self.core))

        @pl.when(self.z > 0)
        def _():
            tell((self.me - 4, self.core))

        @pl.when(self.z < ZS - 1)
        def _():
            tell((self.me + 4, self.core))

        return sem, 3 + jnp.minimum(self.z, 1) + jnp.minimum(ZS - 1 - self.z, 1)


def send(src, dst, send_sem, recv_sem, dev):
    return pltpu.make_async_remote_copy(
        src_ref=src, dst_ref=dst, send_sem=send_sem, recv_sem=recv_sem, device_id=dev, device_id_type=MESH
    )


class Gather:
    def __init__(self, place, fulls, rows, sends, recvs, passed):
        self.place = place
        self.fulls = fulls
        self.rows = rows
        self.sends, self.recvs, self.passed = sends, recvs, passed

    def piece(self, t, q, h):
        full = self.fulls[t]
        rows = self.rows[t]
        if full.shape[1] == 128:
            part = rows // 2
            return full.at[pl.ds(pl.multiple_of(q * rows + h * part, 8), part), :]
        cols = full.shape[1] // 2
        return full.at[pl.ds(pl.multiple_of(q * rows, 16), rows), pl.ds(pl.multiple_of(h * cols, 128), cols)]

    def events(self):
        p = self.place
        yes = p.z >= 0
        up = ((p.me + 4, p.core), p.z < ZS - 1)
        down = ((p.me - 4, p.core), p.z > 0)
        near = ((p.near, p.core), yes)
        far = ((p.far, p.core), yes)
        other = (p.partner(), None)
        out = [(p.me, yes, [up, down, near, far], True)]
        for r in range(ZS):
            ways = [(-4 * r, p.z >= r, up), (4 * r, p.z + r < ZS, down)] if r else [(0, yes, None)]
            if r:
                for shift, there, onward in ways:
                    out.append((p.me + shift, there, [onward, near, far, other], False))
            for shift, there, _ in ways:
                out.append((p.near + shift, there, [far, other], False))
            for shift, there, _ in ways:
                out.append((p.far + shift, there, [other], False))
            for shift, there, _ in ways:
                out.append((p.diag + shift, there, [other], False))
        return out

    def copies(self, t, event):
        q, _, targets, _ = event
        piece = self.piece(t, q, self.place.core)
        made = []
        for n, (dev, cond) in enumerate(targets):
            recv = self.passed.at[t, q] if cond is None else self.recvs.at[t, q]
            made.append((send(piece, piece, self.sends.at[t, n, q], recv, dev), cond))
        return made

    def run(self, t, event):
        q, there, targets, own = event

        @pl.when(there)
        def _():
            made = self.copies(t, event)
            if not own:
                made[0][0].wait_recv() if made[0][1] is not None else send(
                    self.piece(t, q, self.place.core),
                    self.piece(t, q, self.place.core),
                    self.sends.at[t, 0, q],
                    self.recvs.at[t, q],
                    self.place.partner(),
                ).wait_recv()
            for copy, cond in made:
                if cond is None:
                    copy.start()
                else:
                    pl.when(cond)(copy.start)

    def finish_sends(self, t, event):
        q, there, targets, own = event

        @pl.when(there)
        def _():
            for copy, cond in self.copies(t, event):
                if cond is None:
                    copy.wait_send()
                else:
                    pl.when(cond)(copy.wait_send)

    def finish_partner(self, t):
        p = self.place

        @pl.loop(0, 16)
        def _(q):
            @pl.when(q != p.me)
            def _():
                piece = self.piece(t, q, 1 - p.core)
                send(piece, piece, self.sends.at[t, 0, q], self.passed.at[t, q], p.partner()).wait_recv()


def gather_body(count, *refs):
    shards, fulls = refs[:count], refs[count : 2 * count]
    own = refs[2 * count : 3 * count]
    sends, recvs, passed, local = refs[3 * count :]
    place = Place()
    sem, expect = place.barrier()
    for shard, low in zip(shards, own):
        low[...] = shard[...].astype(low.dtype)
    rows = [shard.shape[0] for shard in shards]
    g = Gather(place, fulls, rows, sends, recvs, passed)
    mine = []
    for t in range(count):
        dst = fulls[t].at[pl.ds(pl.multiple_of(place.me * rows[t], 16), rows[t]), :]
        mine.append(pltpu.make_async_copy(own[t], dst, local.at[t]))
        mine[t].start()
    pl.semaphore_wait(sem, expect)
    events = g.events()
    for t in range(count):
        mine[t].wait()
        g.run(t, events[0])
    for event in events[1:]:
        for t in range(count):
            g.run(t, event)
    for event in events:
        for t in range(count):
            g.finish_sends(t, event)
    for t in range(count):
        g.finish_partner(t)


def gather_all(shards, dtypes, collective_id):
    count = len(shards)
    fulls = [jax.ShapeDtypeStruct((16 * s.shape[0], s.shape[1]), d) for s, d in zip(shards, dtypes)]
    return pl.pallas_call(
        functools.partial(gather_body, count),
        in_specs=[pl.BlockSpec(memory_space=pltpu.VMEM)] * count,
        out_specs=[pl.BlockSpec(memory_space=pl.ANY)] * count,
        out_shape=fulls,
        scratch_shapes=[pltpu.VMEM(s.shape, d) for s, d in zip(shards, dtypes)]
        + [
            pltpu.SemaphoreType.DMA((count, 4, 16)),
            pltpu.SemaphoreType.DMA((count, 16)),
            pltpu.SemaphoreType.DMA((count, 16)),
            pltpu.SemaphoreType.DMA((count,)),
        ],
        compiler_params=pltpu.CompilerParams(
            collective_id=collective_id, has_side_effects=True, vmem_limit_bytes=VMEM_LIMIT
        ),
        name=f"gather_{collective_id}",
    )(*shards)


class Scatter:
    def __init__(self, place, grad, rows, out, mine, pair, far, near, low, high, own, sems):
        self.place = place
        self.grad, self.rows, self.out = grad, rows, out
        self.mine, self.pair, self.far, self.near, self.low, self.high, self.own = mine, pair, far, near, low, high, own
        self.sems = sems
        self.cols = grad.shape[1] // 2

    LOCAL, PAIR_S, PAIR_R, LAST_S, LAST_R, FAR_S, FAR_R = 0, 1, 2, 3, 4, 8, 16
    NEAR_S, NEAR_R, UP_S, UP_R, DOWN_S, DOWN_R = 24, 28, 32, 36, 40, 44
    COUNT = 48

    def columns(self, h):
        return pl.ds(pl.multiple_of(h * self.cols, 128), self.cols)

    def at(self, ref, q):
        return ref.at[pl.ds(pl.multiple_of(q * self.rows, 16), self.rows), :]

    def load(self, ref, q):
        return ref[pl.ds(pl.multiple_of(q * self.rows, 16), self.rows), :].astype(single)

    def store(self, ref, q, value):
        ref[pl.ds(pl.multiple_of(q * self.rows, 16), self.rows), :] = value.astype(ref.dtype)

    def copy_local(self):
        return pltpu.make_async_copy(
            self.grad.at[:, self.columns(self.place.core)], self.mine, self.sems.at[self.LOCAL]
        )

    def copy_pair(self):
        p = self.place
        return send(
            self.grad.at[:, self.columns(1 - p.core)],
            self.pair,
            self.sems.at[self.PAIR_S],
            self.sems.at[self.PAIR_R],
            p.partner(),
        )

    def copy_far(self, k):
        p = self.place
        q = p.chip(k // 2, 1 - p.far_bit, k % 2)
        return send(
            self.at(self.mine, q),
            self.at(self.far, k),
            self.sems.at[self.FAR_S + k],
            self.sems.at[self.FAR_R + k],
            (p.far, p.core),
        )

    def copy_near(self, z):
        p = self.place
        return send(
            self.at(self.far, z * 2 + 1 - p.near_bit),
            self.at(self.near, z),
            self.sems.at[self.NEAR_S + z],
            self.sems.at[self.NEAR_R + z],
            (p.near, p.core),
        )

    def copy_up(self, z):
        p = self.place
        return send(
            self.at(self.near, z),
            self.at(self.low, z),
            self.sems.at[self.UP_S + z],
            self.sems.at[self.UP_R + z],
            (p.me + 4, p.core),
        )

    def copy_down(self, z):
        p = self.place
        return send(
            self.at(self.near, z),
            self.at(self.high, z),
            self.sems.at[self.DOWN_S + z],
            self.sems.at[self.DOWN_R + z],
            (p.me - 4, p.core),
        )

    def copy_last(self):
        p = self.place
        return send(
            self.own,
            self.out.at[:, self.columns(p.core)],
            self.sems.at[self.LAST_S],
            self.sems.at[self.LAST_R],
            p.partner(),
        )

    def start(self):
        self.copy_local().start()
        self.copy_pair().start()

    def to_far(self):
        p = self.place
        self.copy_local().wait()
        self.copy_pair().wait_recv()

        @pl.loop(0, 8)
        def _(k):
            q = p.chip(k // 2, 1 - p.far_bit, k % 2)
            self.store(self.mine, q, self.load(self.mine, q) + self.load(self.pair, q))
            self.copy_far(k).start()

    def to_near(self):
        p = self.place

        def add(k):
            q = p.chip(k // 2, p.far_bit, k % 2)
            self.copy_far(k).wait_recv()
            self.store(
                self.far, k, self.load(self.far, k) + self.load(self.mine, q) + self.load(self.pair, q)
            )

        @pl.loop(0, 4)
        def _(z):
            add(z * 2 + 1 - p.near_bit)
            self.copy_near(z).start()

        @pl.loop(0, 4)
        def _(z):
            add(z * 2 + p.near_bit)

    def to_line(self):
        p = self.place

        @pl.loop(0, 4)
        def _(z):
            self.copy_near(z).wait_recv()
            self.store(self.near, z, self.load(self.near, z) + self.load(self.far, z * 2 + p.near_bit))

        @pl.when(p.z == 0)
        def _():
            for z in (3, 2, 1):
                self.copy_up(z).start()

        @pl.when(p.z == ZS - 1)
        def _():
            for z in (0, 1, 2):
                self.copy_down(z).start()

    def along(self, step):
        p = self.place

        @pl.when(p.z == step)
        def _():
            for z in (3, 2, 1):
                if z >= step:
                    self.copy_up(z).wait_recv()
                if z > step:
                    self.store(self.near, z, self.load(self.near, z) + self.load(self.low, z))
                    self.copy_up(z).start()

        @pl.when(p.z == ZS - 1 - step)
        def _():
            for z in (0, 1, 2):
                if z <= ZS - 1 - step:
                    self.copy_down(z).wait_recv()
                if z < ZS - 1 - step:
                    self.store(self.near, z, self.load(self.near, z) + self.load(self.high, z))
                    self.copy_down(z).start()

    def to_last(self):
        p = self.place
        self.own[...] = self.load(self.near, p.z)

        @pl.when(p.z > 0)
        def _():
            self.own[...] += self.load(self.low, p.z)

        @pl.when(p.z < ZS - 1)
        def _():
            self.own[...] += self.load(self.high, p.z)

        self.copy_last().start()
        self.out[:, self.columns(p.core)] = self.own[...]

    def finish(self):
        p = self.place
        self.copy_pair().wait_send()

        @pl.loop(0, 8)
        def _(k):
            self.copy_far(k).wait_send()

        @pl.loop(0, 4)
        def _(z):
            self.copy_near(z).wait_send()

            @pl.when(z > p.z)
            def _():
                self.copy_up(z).wait_send()

            @pl.when(z < p.z)
            def _():
                self.copy_down(z).wait_send()

        self.copy_last().wait()

    def stages(self):
        return [
            self.start,
            self.to_far,
            self.to_near,
            self.to_line,
            lambda: self.along(1),
            lambda: self.along(2),
            lambda: self.along(3),
            self.to_last,
            self.finish,
        ]

    @staticmethod
    def scratch(shape):
        total, cols = shape[0], shape[1] // 2
        rows = total // 16
        return [
            pltpu.VMEM((total, cols), half),
            pltpu.VMEM((total, cols), half),
            pltpu.VMEM((8 * rows, cols), half),
            pltpu.VMEM((4 * rows, cols), half),
            pltpu.VMEM((4 * rows, cols), half),
            pltpu.VMEM((4 * rows, cols), half),
            pltpu.VMEM((rows, cols), single),
            pltpu.SemaphoreType.DMA((Scatter.COUNT,)),
        ]


def scatter_body(count, *refs):
    grads, outs = refs[:count], refs[count : 2 * count]
    rest = refs[2 * count :]
    place = Place()
    sem, expect = place.barrier()
    runs = []
    for t in range(count):
        rows = grads[t].shape[0] // 16
        runs.append(Scatter(place, grads[t], rows, outs[t], *rest[8 * t : 8 * t + 8]))
    pl.semaphore_wait(sem, expect)
    table = [run.stages() for run in runs]
    for wave in range(count + len(table[0]) - 1):
        for t in range(count):
            if 0 <= wave - t < len(table[t]):
                table[t][wave - t]()


def scatter_sum(grads, collective_id):
    count = len(grads)
    outs = [jax.ShapeDtypeStruct((g.shape[0] // 16, g.shape[1]), single) for g in grads]
    return pl.pallas_call(
        functools.partial(scatter_body, count),
        in_specs=[pl.BlockSpec(memory_space=pl.ANY)] * count,
        out_specs=[pl.BlockSpec(memory_space=pltpu.VMEM)] * count,
        out_shape=outs,
        scratch_shapes=sum([Scatter.scratch(g.shape) for g in grads], []),
        compiler_params=pltpu.CompilerParams(
            collective_id=collective_id, has_side_effects=True, vmem_limit_bytes=VMEM_LIMIT
        ),
        name=f"scatter_{collective_id}",
    )(*grads)


def small_body(blocks_ref, out_ref, got, send_sem, recv_sem):
    me = lax.axis_index("dp")
    core = lax.axis_index("rep")
    sem = pltpu.get_barrier_semaphore()
    total = 32
    mine = me * 2 + core

    @pl.loop(0, total)
    def _(d):
        @pl.when(d != mine)
        def _():
            pl.semaphore_signal(sem, inc=1, device_id=(d // 2, d % 2), device_id_type=MESH)

    pl.semaphore_wait(sem, total - 1)

    def copy(d):
        return send(blocks_ref.at[d // 2], got.at[mine], send_sem.at[d], recv_sem.at[mine], (d // 2, d % 2))

    @pl.loop(0, total)
    def _(d):
        pl.when(d != mine)(lambda: copy(d).start())

    got[mine] = blocks_ref[me]

    @pl.loop(0, total)
    def _(d):
        @pl.when(d != mine)
        def _():
            copy(d).wait_send()
            send(got.at[d], got.at[d], send_sem.at[d], recv_sem.at[d], (d // 2, d % 2)).wait_recv()

    out_ref[...] = jnp.sum(got[...], axis=0)


def small_sum(blocks, collective_id):
    _, rows, lanes = blocks.shape
    return pl.pallas_call(
        small_body,
        in_specs=[pl.BlockSpec(memory_space=pltpu.VMEM)],
        out_specs=pl.BlockSpec(memory_space=pltpu.VMEM),
        out_shape=jax.ShapeDtypeStruct((rows, lanes), single),
        scratch_shapes=[
            pltpu.VMEM((32, rows, lanes), single),
            pltpu.SemaphoreType.DMA((32,)),
            pltpu.SemaphoreType.DMA((32,)),
        ],
        compiler_params=pltpu.CompilerParams(collective_id=collective_id, has_side_effects=True),
        name=f"small_{collective_id}",
    )(blocks)


def pack_small(vectors, b_up, low):
    n = vectors[0].shape[0]
    block = jnp.concatenate([jnp.stack(vectors), b_up.reshape(-1, n)])
    block = lax.reduce_precision(block, 8, 7) if low else block
    return jnp.pad(block, ((0, 16 - block.shape[0]), (0, 128 - n)))


def unpack_small(full, chips, n):
    full = full.reshape(chips, 16, 128)
    vectors = full[:, :8, :n].transpose(1, 0, 2).reshape(8, chips * n)
    return vectors, full[:, 8:12, :n].reshape(1, 4 * chips * n)


def local(chips, twins, tokens, flags, mask_embed, cotangent, w_qkv, b_qv, w_out, b_out, norm_one, w_up, b_up, w_down, b_down, norm_two):
    own_kernels = chips == 16 and twins == 2
    n = b_out.shape[0]
    width = chips * n
    small = pack_small(
        [b_qv[0], b_qv[1], b_out, norm_one[0], norm_one[1], b_down, norm_two[0], norm_two[1]], b_up, True
    )
    shards = [w_qkv, w_out, w_up, w_down]
    if own_kernels:
        *fulls, small_full = gather_all(shards + [small], [half] * 4 + [single], 1)
    else:
        fulls = [lax.all_gather(s.astype(half), "dp", axis=0, tiled=True) for s in shards]
        small_full = lax.all_gather(small, "dp", axis=0, tiled=True)
    qkv_full, out_full, up_full, down_full = fulls
    vecs, bup_full = unpack_small(small_full, chips, n)
    bias = jnp.concatenate([vecs[0], jnp.zeros_like(vecs[0]), vecs[1]])[None]
    flag_col = flags[:, None]
    inputs, projected = project(tokens, flag_col, mask_embed[None], qkv_full, bias)
    mixed, logs = attend(projected)
    activations, d_sum, d_mixed, g_small, g_bup, g_out, g_up, g_down = middle(
        mixed, inputs, flag_col, cotangent, vecs, bup_full, out_full, up_full, down_full
    )
    d_parts = attend_back(projected, d_mixed, mixed, logs)
    g_qkv, sums = weight_back(inputs, d_parts)
    input_grad = input_back(d_parts, qkv_full, d_sum, flag_col)
    g_small = jnp.concatenate([sums[0:1, :width], sums[0:1, 2 * width :], g_small[2:8]])
    g_small = g_small.reshape(8, chips, n).transpose(1, 0, 2)
    g_small = jnp.concatenate([g_small, g_bup.reshape(chips, 4, n)], axis=1)
    g_small = jnp.pad(g_small, ((0, 0), (0, 4), (0, 128 - n)))
    grads = [g_qkv, g_out, g_up, g_down]
    if own_kernels:
        grads = scatter_sum(grads, 2)
        g_small = small_sum(g_small, 3)
    else:
        grads = [lax.psum_scatter(g.astype(single), "dp", scatter_dimension=0, tiled=True) for g in grads]
        grads = [lax.psum(g.astype(half), "rep").astype(single) for g in grads]
        g_small = lax.psum_scatter(g_small, "dp", scatter_dimension=0, tiled=False)
        g_small = lax.psum(g_small, "rep")
    g_qkv, g_out, g_up, g_down = grads
    rows = g_small[:, :n]
    return (
        activations,
        input_grad,
        g_qkv,
        rows[0:2],
        g_out,
        rows[2],
        rows[3:5],
        g_up,
        rows[8:12].reshape(4 * n),
        g_down,
        rows[5],
        rows[6:8],
    )


def solution(mesh):
    rows = P(("dp", "rep"), None)
    first = P("dp", None)
    second = P(None, "dp")
    return jax.shard_map(
        functools.partial(local, mesh.shape["dp"], mesh.shape["rep"]),
        mesh=mesh,
        in_specs=(rows, P(("dp", "rep")), P(), rows, first, second, first, P("dp"), second, first, P("dp"), first, P("dp"), second),
        out_specs=(rows, rows, first, second, first, P("dp"), second, first, P("dp"), first, P("dp"), second),
        check_vma=False,
    )
```

```python
import functools

import jax
import jax.numpy as jnp
from jax import lax
from jax.experimental import pallas as pl
from jax.experimental.pallas import tpu as pltpu
from jax.sharding import PartitionSpec as P

HEADS = 12
SEQ = 512
EPS = 1e-12
half = jnp.bfloat16
single = jnp.float32
VMEM_LIMIT = 61 * 1024 * 1024


def mm(left, right):
    return jnp.dot(left, right, preferred_element_type=single)


def mm_tb(left, right):
    return lax.dot_general(left, right, (((1,), (1,)), ((), ())), preferred_element_type=single)


def mm_ta(left, right):
    return lax.dot_general(left, right, (((0,), (0,)), ((), ())), preferred_element_type=single)


def row_mean(values):
    return jnp.mean(values, axis=-1, keepdims=True)


def col_sum(values):
    return jnp.sum(values, axis=0, keepdims=True)


def project_body(tok_ref, flag_ref, mask_ref, w_ref, bias_ref, inp_ref, proj_ref):
    masked = flag_ref[...] > 0
    inputs = jnp.where(masked, mask_ref[...].astype(single), tok_ref[...].astype(single))
    low = inputs.astype(half)
    inp_ref[...] = low
    proj_ref[...] = (mm(low, w_ref[...]) + bias_ref[...]).astype(half)


def project(tokens, flags, mask_embed, w_qkv, bias):
    count, width = tokens.shape
    block = 256
    wide = w_qkv.shape[1]
    return pl.pallas_call(
        project_body,
        grid=(count // block,),
        in_specs=[
            pl.BlockSpec((block, width), lambda i: (i, 0)),
            pl.BlockSpec((block, 1), lambda i: (i, 0)),
            pl.BlockSpec((1, width), lambda i: (0, 0)),
            pl.BlockSpec((width, wide), lambda i: (0, 0), pipeline_mode=pl.Buffered(1)),
            pl.BlockSpec((1, wide), lambda i: (0, 0)),
        ],
        out_specs=[
            pl.BlockSpec((block, width), lambda i: (i, 0)),
            pl.BlockSpec((block, wide), lambda i: (i, 0)),
        ],
        out_shape=[
            jax.ShapeDtypeStruct((count, width), half),
            jax.ShapeDtypeStruct((count, wide), half),
        ],
        compiler_params=pltpu.CompilerParams(vmem_limit_bytes=VMEM_LIMIT),
        name="project",
    )(tokens, flags, mask_embed, w_qkv, bias)


def head_masks(width):
    lane = lax.broadcasted_iota(jnp.int32, (1, width), 1)
    return [(lane // 64) == h for h in range(width // 64)]


def attend_pair(query, keys, vals):
    scaled = query * half(0.125)
    turned = vals.T
    outs, logs = [], []
    for h, mask in enumerate(head_masks(128)):
        own = jnp.where(mask, keys, half(0))
        scores = mm_tb(own, scaled)
        top = jnp.max(scores, axis=0, keepdims=True)
        expo = jnp.exp(scores - top)
        total = jnp.sum(expo, axis=0, keepdims=True)
        mixed = mm(turned[64 * h : 64 * h + 64], expo.astype(half))
        outs.append(mixed * (1.0 / total))
        logs.append(top + jnp.log(total))
    return jnp.concatenate(outs, axis=0).astype(half).T, logs


def attend_body(pairs, q_ref, k_ref, v_ref, mixed_ref, log_ref):
    for p in range(pairs):
        cols = pl.ds(128 * p, 128)
        mixed, logs = attend_pair(q_ref[:, cols], k_ref[:, cols], v_ref[:, cols])
        mixed_ref[:, cols] = mixed
        for h in range(2):
            log_ref[0, 0, pl.ds(2 * p + h, 1), :] = logs[h]


def attend(projected, pairs=2):
    count = projected.shape[0]
    width = projected.shape[1] // 3
    groups = count // SEQ
    steps = width // (128 * pairs)
    spec = lambda part: pl.BlockSpec((SEQ, 128 * pairs), lambda g, p: (g, part * steps + p))
    return pl.pallas_call(
        functools.partial(attend_body, pairs),
        grid=(groups, steps),
        in_specs=[spec(0), spec(1), spec(2)],
        out_specs=[
            pl.BlockSpec((SEQ, 128 * pairs), lambda g, p: (g, p)),
            pl.BlockSpec((1, 1, 8, SEQ), lambda g, p: (g, p, 0, 0)),
        ],
        out_shape=[
            jax.ShapeDtypeStruct((count, width), half),
            jax.ShapeDtypeStruct((groups, steps, 8, SEQ), single),
        ],
        compiler_params=pltpu.CompilerParams(vmem_limit_bytes=VMEM_LIMIT),
        name="attend",
    )(projected, projected, projected)


def attend_back_pair(query, keys, vals, grad, mixed, logs):
    scaled = query * half(0.125)
    scaled_keys = keys * half(0.125)
    product = grad.astype(single) * mixed.astype(single)
    grad_turned = grad.T
    scaled_turned = scaled.T
    d_vals, d_keys, d_query = [], [], None
    for h, mask in enumerate(head_masks(128)):
        scores = mm_tb(jnp.where(mask, scaled, half(0)), keys)
        probs = jnp.exp(scores - logs[:, h : h + 1])
        d_probs = mm_tb(jnp.where(mask, grad, half(0)), vals)
        delta = jnp.sum(jnp.where(mask, product, 0.0), axis=1, keepdims=True)
        d_scores = (probs * (d_probs - delta)).astype(half)
        rows = slice(64 * h, 64 * h + 64)
        d_vals.append(mm(grad_turned[rows], probs.astype(half)))
        d_keys.append(mm(scaled_turned[rows], d_scores))
        part = mm(d_scores, jnp.where(mask, scaled_keys, half(0)))
        d_query = part if d_query is None else d_query + part
    turn = lambda parts: jnp.concatenate(parts, axis=0).astype(half).T
    return d_query.astype(half), turn(d_keys), turn(d_vals)


def norm(values, gain, shift):
    center = values - row_mean(values)
    inverse = lax.rsqrt(row_mean(center * center) + EPS)
    unit = center * inverse
    return unit * gain + shift, unit, inverse


def norm_back(grad, unit, inverse, gain):
    scaled = grad * gain
    return inverse * (scaled - row_mean(scaled) - unit * row_mean(scaled * unit))


def middle_body(
    mixed_ref,
    inp_ref,
    flag_ref,
    cot_ref,
    vec_ref,
    bup_ref,
    wo_ref,
    wu_ref,
    wd_ref,
    act_out,
    dsum_out,
    dmix_out,
    small_out,
    gwo_out,
    gwu_out,
    gwd_out,
    unit1,
    first,
    low,
    acts,
    slope,
    total,
    d_low,
    acc_o,
    acc_u,
    acc_d,
    stage,
    sems,
):
    step = pl.program_id(0)
    last = pl.num_programs(0) - 1
    width = wo_ref.shape[0]
    chunks = wd_ref.shape[0] // width

    @pl.when(step == 0)
    def _():
        small_out[...] = jnp.zeros_like(small_out)
        acc_o[...] = jnp.zeros_like(acc_o)
        acc_u[...] = jnp.zeros_like(acc_u)
        acc_d[...] = jnp.zeros_like(acc_d)

    vec = lambda row: vec_ref[pl.ds(row, 1), :]
    attended = mm(mixed_ref[...], wo_ref[...]) + vec(2)
    value, unit, inv1 = norm(inp_ref[...].astype(single) + attended, vec(3), vec(4))
    unit1[...] = unit
    first[...] = value
    low[...] = value.astype(half)
    total[...] = jnp.zeros_like(total)

    @pl.loop(0, chunks)
    def _(j):
        cols = pl.ds(pl.multiple_of(j * width, width), width)
        upper = mm(low[...], wu_ref[:, cols]) + bup_ref[:, cols]
        phi = 0.5 * (1.0 + lax.erf(upper * 0.7071067811865476))
        act = (upper * phi).astype(half)
        acts[j] = act
        slope[j] = (phi + upper * jnp.exp(-0.5 * upper * upper) * 0.3989422804014327).astype(half)
        total[...] += mm(act, wd_ref[cols, :])

    value, unit, inv2 = norm(first[...] + total[...] + vec(5), vec(6), vec(7))
    act_out[...] = value.astype(half)
    out_grad = jnp.where(flag_ref[...] > 0, cot_ref[...].astype(single), 0.0)
    small_out[pl.ds(6, 1), :] += col_sum(out_grad * unit)
    small_out[pl.ds(7, 1), :] += col_sum(out_grad)
    d_second = norm_back(out_grad, unit, inv2, vec(6))
    lowered = d_second.astype(half)
    d_low[...] = lowered
    small_out[pl.ds(5, 1), :] += col_sum(lowered.astype(single))
    total[...] = d_second

    @pl.loop(0, chunks)
    def _(j):
        cols = pl.ds(pl.multiple_of(j * width, width), width)
        d_acts = mm_tb(d_low[...], wd_ref[cols, :])
        d_upper = (d_acts * slope[j].astype(single)).astype(half)
        small_out[pl.ds(8 + j, 1), :] += col_sum(d_upper.astype(single))
        total[...] += mm_tb(d_upper, wu_ref[:, cols])
        acc_d[j] += mm_ta(acts[j], d_low[...])
        acc_u[j] += mm_ta(low[...], d_upper)

    d_first = total[...]
    unit = unit1[...]
    small_out[pl.ds(3, 1), :] += col_sum(d_first * unit)
    small_out[pl.ds(4, 1), :] += col_sum(d_first)
    d_sum = norm_back(d_first, unit, inv1, vec(3))
    dsum_out[...] = d_sum
    d_att = d_sum.astype(half)
    small_out[pl.ds(2, 1), :] += col_sum(d_att.astype(single))
    dmix_out[...] = mm_tb(d_att, wo_ref[...]).astype(half)
    acc_o[...] += mm_ta(mixed_ref[...], d_att)

    @pl.when(step == last)
    def _():
        copies = []
        todo = [(acc_d.at[j], gwd_out.at[pl.ds(j * width, width), :]) for j in range(chunks)]
        todo += [(acc_u.at[j], gwu_out.at[:, pl.ds(j * width, width)]) for j in range(chunks)]
        todo += [(acc_o, gwo_out)]
        for n, (src, dst) in enumerate(todo):
            slot = n % 2
            if n >= 2:
                copies[n - 2].wait()
            stage[slot] = src[...].astype(half)
            copies.append(pltpu.make_async_copy(stage.at[slot], dst, sems.at[slot]))
            copies[n].start()
        for copy in copies[-2:]:
            copy.wait()


def middle(mixed, inputs, flags, cotangent, vecs, b_up, w_out, w_up, w_down, block=512):
    count, width = mixed.shape
    hidden = w_up.shape[1]
    chunks = hidden // width
    rows = lambda cols: pl.BlockSpec((block, cols), lambda i: (i, 0))
    once = lambda shape: pl.BlockSpec(shape, lambda i: (0, 0), pipeline_mode=pl.Buffered(1))
    keep = lambda shape: pl.BlockSpec(shape, lambda i: (0, 0))
    whole = pl.BlockSpec(memory_space=pl.ANY)
    return pl.pallas_call(
        middle_body,
        grid=(count // block,),
        in_specs=[
            rows(width),
            rows(width),
            rows(1),
            rows(width),
            keep((8, width)),
            keep((1, hidden)),
            once((width, width)),
            once((width, hidden)),
            once((hidden, width)),
        ],
        out_specs=[
            rows(width),
            rows(width),
            rows(width),
            keep((16, width)),
            whole,
            whole,
            whole,
        ],
        out_shape=[
            jax.ShapeDtypeStruct((count, width), half),
            jax.ShapeDtypeStruct((count, width), single),
            jax.ShapeDtypeStruct((count, width), half),
            jax.ShapeDtypeStruct((16, width), single),
            jax.ShapeDtypeStruct((width, width), half),
            jax.ShapeDtypeStruct((width, hidden), half),
            jax.ShapeDtypeStruct((hidden, width), half),
        ],
        scratch_shapes=[
            pltpu.VMEM((block, width), single),
            pltpu.VMEM((block, width), single),
            pltpu.VMEM((block, width), half),
            pltpu.VMEM((chunks, block, width), half),
            pltpu.VMEM((chunks, block, width), half),
            pltpu.VMEM((block, width), single),
            pltpu.VMEM((block, width), half),
            pltpu.VMEM((width, width), single),
            pltpu.VMEM((chunks, width, width), single),
            pltpu.VMEM((chunks, width, width), single),
            pltpu.VMEM((2, width, width), half),
            pltpu.SemaphoreType.DMA((2,)),
        ],
        compiler_params=pltpu.CompilerParams(vmem_limit_bytes=VMEM_LIMIT),
        name="middle",
    )(mixed, inputs, flags, cotangent, vecs, b_up, w_out, w_up, w_down)


MESH = pl.DeviceIdType.MESH
ZS = 4


class Place:
    def __init__(self):
        self.me = lax.axis_index("dp")
        self.core = lax.axis_index("rep")
        self.z = self.me // 4
        self.y = (self.me // 2) % 2
        self.x = self.me % 2
        step_x = 1 - 2 * self.x
        step_y = 2 - 4 * self.y
        self.near = self.me + step_x + self.core * (step_y - step_x)
        self.far = self.me + step_y + self.core * (step_x - step_y)
        self.diag = self.me + step_x + step_y
        self.near_bit = self.x + self.core * (self.y - self.x)
        self.far_bit = self.y + self.core * (self.x - self.y)

    def chip(self, z, far, near):
        return z * 4 + far * (2 - self.core) + near * (1 + self.core)

    def partner(self):
        return (self.me, 1 - self.core)

    def barrier(self):
        sem = pltpu.get_barrier_semaphore()
        tell = lambda dev: pl.semaphore_signal(sem, inc=1, device_id=dev, device_id_type=MESH)
        tell(self.partner())
        tell((self.near, self.core))
        tell((self.far, self.core))

        for k in range(1, ZS):
            tell(((self.me + 4 * k) % (4 * ZS), self.core))
        return sem, 3 + ZS - 1


def send(src, dst, send_sem, recv_sem, dev):
    return pltpu.make_async_remote_copy(
        src_ref=src, dst_ref=dst, send_sem=send_sem, recv_sem=recv_sem, device_id=dev, device_id_type=MESH
    )


class Gather:
    def __init__(self, place, fulls, rows, sends, recvs, passed):
        self.place = place
        self.fulls = fulls
        self.rows = rows
        self.sends, self.recvs, self.passed = sends, recvs, passed

    def piece(self, t, q, h):
        full = self.fulls[t]
        rows = self.rows[t]
        if full.shape[1] == 128:
            part = rows // 2
            return full.at[pl.ds(pl.multiple_of(q * rows + h * part, 8), part), :]
        cols = full.shape[1] // 2
        return full.at[pl.ds(pl.multiple_of(q * rows, 16), rows), pl.ds(pl.multiple_of(h * cols, 128), cols)]

    def events(self):
        p = self.place
        yes = p.z >= 0
        up = ((p.me + 4, p.core), p.z < ZS - 1)
        down = ((p.me - 4, p.core), p.z > 0)
        near = ((p.near, p.core), yes)
        far = ((p.far, p.core), yes)
        other = (p.partner(), None)
        out = [(p.me, yes, [up, down, near, far], True)]
        for r in range(ZS):
            ways = [(-4 * r, p.z >= r, up), (4 * r, p.z + r < ZS, down)] if r else [(0, yes, None)]
            if r:
                for shift, there, onward in ways:
                    out.append((p.me + shift, there, [onward, near, far, other], False))
            for shift, there, _ in ways:
                out.append((p.near + shift, there, [far, other], False))
            for shift, there, _ in ways:
                out.append((p.far + shift, there, [other], False))
            for shift, there, _ in ways:
                out.append((p.diag + shift, there, [other], False))
        return out

    def copies(self, t, event):
        q, _, targets, _ = event
        piece = self.piece(t, q, self.place.core)
        made = []
        for n, (dev, cond) in enumerate(targets):
            recv = self.passed.at[t, q] if cond is None else self.recvs.at[t, q]
            made.append((send(piece, piece, self.sends.at[t, n, q], recv, dev), cond))
        return made

    def run(self, t, event):
        q, there, targets, own = event

        @pl.when(there)
        def _():
            made = self.copies(t, event)
            if not own:
                made[0][0].wait_recv() if made[0][1] is not None else send(
                    self.piece(t, q, self.place.core),
                    self.piece(t, q, self.place.core),
                    self.sends.at[t, 0, q],
                    self.recvs.at[t, q],
                    self.place.partner(),
                ).wait_recv()
            for copy, cond in made:
                if cond is None:
                    copy.start()
                else:
                    pl.when(cond)(copy.start)

    def finish_sends(self, t, event):
        q, there, targets, own = event

        @pl.when(there)
        def _():
            for copy, cond in self.copies(t, event):
                if cond is None:
                    copy.wait_send()
                else:
                    pl.when(cond)(copy.wait_send)

    def finish_partner(self, t):
        p = self.place

        @pl.loop(0, 16)
        def _(q):
            @pl.when(q != p.me)
            def _():
                piece = self.piece(t, q, 1 - p.core)
                send(piece, piece, self.sends.at[t, 0, q], self.passed.at[t, q], p.partner()).wait_recv()


def gather_body(count, *refs):
    shards, fulls = refs[:count], refs[count : 2 * count]
    own = refs[2 * count : 3 * count]
    sends, recvs, passed, local = refs[3 * count :]
    place = Place()
    sem, expect = place.barrier()
    for shard, low in zip(shards, own):
        low[...] = shard[...].astype(low.dtype)
    rows = [shard.shape[0] for shard in shards]
    g = Gather(place, fulls, rows, sends, recvs, passed)
    mine = []
    for t in range(count):
        dst = fulls[t].at[pl.ds(pl.multiple_of(place.me * rows[t], 16), rows[t]), :]
        mine.append(pltpu.make_async_copy(own[t], dst, local.at[t]))
        mine[t].start()
    pl.semaphore_wait(sem, expect)
    events = g.events()
    for t in range(count):
        mine[t].wait()
        g.run(t, events[0])
    for event in events[1:]:
        for t in range(count):
            g.run(t, event)
    for event in events:
        for t in range(count):
            g.finish_sends(t, event)
    for t in range(count):
        g.finish_partner(t)


def gather_all(shards, dtypes, collective_id):
    count = len(shards)
    fulls = [jax.ShapeDtypeStruct((16 * s.shape[0], s.shape[1]), d) for s, d in zip(shards, dtypes)]
    return pl.pallas_call(
        functools.partial(gather_body, count),
        in_specs=[pl.BlockSpec(memory_space=pltpu.VMEM)] * count,
        out_specs=[pl.BlockSpec(memory_space=pl.ANY)] * count,
        out_shape=fulls,
        scratch_shapes=[pltpu.VMEM(s.shape, d) for s, d in zip(shards, dtypes)]
        + [
            pltpu.SemaphoreType.DMA((count, 4, 16)),
            pltpu.SemaphoreType.DMA((count, 16)),
            pltpu.SemaphoreType.DMA((count, 16)),
            pltpu.SemaphoreType.DMA((count,)),
        ],
        compiler_params=pltpu.CompilerParams(
            collective_id=collective_id, has_side_effects=True, vmem_limit_bytes=VMEM_LIMIT
        ),
        name=f"gather_{collective_id}",
    )(*shards)


class Scatter:
    def __init__(self, place, grad, rows, out, mine, pair, far, near, low, high, own, got, sems):
        self.place = place
        self.grad, self.rows, self.out = grad, rows, out
        self.mine, self.pair, self.far, self.near, self.low, self.high, self.own, self.got = mine, pair, far, near, low, high, own, got
        self.sems = sems
        self.cols = grad.shape[1] // 2

    LOCAL, PAIR_S, PAIR_R, LAST_S, LAST_R, FAR_S, FAR_R = 0, 1, 2, 3, 4, 8, 16
    NEAR_S, NEAR_R, UP_S, UP_R, DOWN_S, DOWN_R = 24, 28, 32, 36, 40, 44
    COUNT = 48

    def columns(self, h):
        return pl.ds(pl.multiple_of(h * self.cols, 128), self.cols)

    def at(self, ref, q):
        return ref.at[pl.ds(pl.multiple_of(q * self.rows, 16), self.rows), :]

    def load(self, ref, q):
        return ref[pl.ds(pl.multiple_of(q * self.rows, 16), self.rows), :].astype(single)

    def store(self, ref, q, value):
        ref[pl.ds(pl.multiple_of(q * self.rows, 16), self.rows), :] = value.astype(ref.dtype)

    def copy_local(self):
        return pltpu.make_async_copy(
            self.grad.at[:, self.columns(self.place.core)], self.mine, self.sems.at[self.LOCAL]
        )

    def copy_pair(self):
        p = self.place
        return send(
            self.grad.at[:, self.columns(1 - p.core)],
            self.pair,
            self.sems.at[self.PAIR_S],
            self.sems.at[self.PAIR_R],
            p.partner(),
        )

    def copy_far(self, k):
        p = self.place
        q = p.chip(k // 2, 1 - p.far_bit, k % 2)
        return send(
            self.at(self.mine, q),
            self.at(self.far, k),
            self.sems.at[self.FAR_S + k],
            self.sems.at[self.FAR_R + k],
            (p.far, p.core),
        )

    def copy_near(self, z):
        p = self.place
        return send(
            self.at(self.far, z * 2 + 1 - p.near_bit),
            self.at(self.near, z),
            self.sems.at[self.NEAR_S + z],
            self.sems.at[self.NEAR_R + z],
            (p.near, p.core),
        )

    def copy_up(self, z):
        p = self.place
        return send(
            self.at(self.near, z),
            self.at(self.low, z),
            self.sems.at[self.UP_S + z],
            self.sems.at[self.UP_R + z],
            (p.me + 4, p.core),
        )

    def copy_down(self, z):
        p = self.place
        return send(
            self.at(self.near, z),
            self.at(self.high, z),
            self.sems.at[self.DOWN_S + z],
            self.sems.at[self.DOWN_R + z],
            (p.me - 4, p.core),
        )

    def copy_last(self):
        p = self.place
        return send(
            self.own,
            self.got,
            self.sems.at[self.LAST_S],
            self.sems.at[self.LAST_R],
            p.partner(),
        )

    def start(self):
        self.copy_local().start()
        self.copy_pair().start()

    def to_far(self):
        p = self.place
        self.copy_local().wait()
        self.copy_pair().wait_recv()

        @pl.loop(0, 8)
        def _(k):
            q = p.chip(k // 2, 1 - p.far_bit, k % 2)
            self.store(self.mine, q, self.load(self.mine, q) + self.load(self.pair, q))
            self.copy_far(k).start()

    def to_near(self):
        p = self.place

        def add(k):
            q = p.chip(k // 2, p.far_bit, k % 2)
            self.copy_far(k).wait_recv()
            self.store(
                self.far, k, self.load(self.far, k) + self.load(self.mine, q) + self.load(self.pair, q)
            )

        @pl.loop(0, 4)
        def _(z):
            add(z * 2 + 1 - p.near_bit)
            self.copy_near(z).start()

        @pl.loop(0, 4)
        def _(z):
            add(z * 2 + p.near_bit)

    def to_line(self):
        p = self.place

        @pl.loop(0, 4)
        def _(z):
            self.copy_near(z).wait_recv()
            self.store(self.near, z, self.load(self.near, z) + self.load(self.far, z * 2 + p.near_bit))

        @pl.when(p.z == 0)
        def _():
            for z in (3, 2, 1):
                self.copy_up(z).start()

        @pl.when(p.z == ZS - 1)
        def _():
            for z in (0, 1, 2):
                self.copy_down(z).start()

    def along(self, step):
        p = self.place

        @pl.when(p.z == step)
        def _():
            for z in (3, 2, 1):
                if z >= step:
                    self.copy_up(z).wait_recv()
                if z > step:
                    self.store(self.near, z, self.load(self.near, z) + self.load(self.low, z))
                    self.copy_up(z).start()

        @pl.when(p.z == ZS - 1 - step)
        def _():
            for z in (0, 1, 2):
                if z <= ZS - 1 - step:
                    self.copy_down(z).wait_recv()
                if z < ZS - 1 - step:
                    self.store(self.near, z, self.load(self.near, z) + self.load(self.high, z))
                    self.copy_down(z).start()

    def to_last(self):
        p = self.place
        self.own[...] = self.load(self.near, p.z)

        @pl.when(p.z > 0)
        def _():
            self.own[...] += self.load(self.low, p.z)

        @pl.when(p.z < ZS - 1)
        def _():
            self.own[...] += self.load(self.high, p.z)

        self.copy_last().start()
        self.out[:, self.columns(p.core)] = self.own[...]

    def finish(self):
        p = self.place
        self.copy_pair().wait_send()

        @pl.loop(0, 8)
        def _(k):
            self.copy_far(k).wait_send()

        @pl.loop(0, 4)
        def _(z):
            self.copy_near(z).wait_send()

            @pl.when(z > p.z)
            def _():
                self.copy_up(z).wait_send()

            @pl.when(z < p.z)
            def _():
                self.copy_down(z).wait_send()

        self.copy_last().wait()
        self.out[:, self.columns(1 - p.core)] = self.got[...]

    def stages(self):
        return [
            self.start,
            self.to_far,
            self.to_near,
            self.to_line,
            lambda: self.along(1),
            lambda: self.along(2),
            lambda: self.along(3),
            self.to_last,
            self.finish,
        ]

    @staticmethod
    def scratch(shape):
        total, cols = shape[0], shape[1] // 2
        rows = total // 16
        return [
            pltpu.VMEM((total, cols), half),
            pltpu.VMEM((total, cols), half),
            pltpu.VMEM((8 * rows, cols), half),
            pltpu.VMEM((4 * rows, cols), half),
            pltpu.VMEM((4 * rows, cols), half),
            pltpu.VMEM((4 * rows, cols), half),
            pltpu.VMEM((rows, cols), single),
            pltpu.VMEM((rows, cols), single),
            pltpu.SemaphoreType.DMA((Scatter.COUNT,)),
        ]


class Total:
    COUNT = 12

    def __init__(self, place, start, pair, result, parts, held, sems):
        self.place, self.first, self.pair, self.result = place, start, pair, result
        self.parts, self.held, self.sems = parts, held, sems

    def copy(self, n):
        p = self.place
        if n == 0:
            src, dev = self.first, p.partner()
        elif n <= 3:
            src, dev = self.held.at[0], ((p.me + 4 * n) % (4 * ZS), p.core)
        elif n == 4:
            src, dev = self.held.at[1], (p.near, p.core)
        else:
            src, dev = self.held.at[2], (p.far, p.core)
        return send(src, self.parts.at[n], self.sems.at[n], self.sems.at[6 + n], dev)

    def stages(self):
        def begin():
            if self.pair:
                self.copy(0).start()

        def column():
            value = self.first[...]
            if self.pair:
                self.copy(0).wait_recv()
                value = value + self.parts[0]
            self.held[0] = value
            for n in (1, 2, 3):
                self.copy(n).start()

        def near():
            value = self.held[0]
            for n in (1, 2, 3):
                self.copy(n).wait_recv()
                value = value + self.parts[n]
            self.held[1] = value
            self.copy(4).start()

        def far():
            self.copy(4).wait_recv()
            self.held[2] = self.held[1] + self.parts[4]
            self.copy(5).start()

        def finish():
            self.copy(5).wait_recv()
            self.result[...] = self.held[2] + self.parts[5]
            for n in range(0 if self.pair else 1, 6):
                self.copy(n).wait_send()

        return [begin, column, near, far, finish]

    @staticmethod
    def scratch(shape):
        return [
            pltpu.VMEM((6,) + shape, single),
            pltpu.VMEM((3,) + shape, single),
            pltpu.SemaphoreType.DMA((Total.COUNT,)),
        ]


PAIRS = 2


def back_body(links, plan, *refs):
    q_ref, k_ref, v_ref, grad_ref, mixed_ref, log_ref, inp_ref, w_ref, dsum_ref, flag_ref, small_ref = refs[:11]
    rest = refs[11:]
    step = pl.program_id(0)
    width = inp_ref.shape[1]
    count = inp_ref.shape[0]
    wide = 128 * PAIRS
    per_group = width // wide
    attends = (count // SEQ) * per_group
    weights = 3 * (width // 256)
    actions = {}

    if links:
        grads, (out_ref, g_qkv, g_out, g_up, g_down, total_ref) = rest[:3], rest[3:9]
        parts_ref, made, sums, fixed = rest[9], rest[10], rest[11], rest[12:]
        place = Place()
        runs = []
        sources = [(grads[2], g_down), (grads[1], g_up), (grads[0], g_out)]
        sources += [(made.at[n], g_qkv.at[:, pl.ds(n * width, width)]) for n in range(3)]
        for n, (src, dst) in enumerate(sources):
            runs.append(Scatter(place, src, src.shape[0] // 16, dst, *fixed[9 * n : 9 * n + 9]))
        runs.append(Total(place, sums, True, total_ref, *fixed[9 * len(sources) :]))

        def enter():
            sem, expect = place.barrier()
            pl.semaphore_wait(sem, expect)

        actions.setdefault((0, 0), []).append(enter)
        for n, run in enumerate(runs):
            for stage, when in zip(run.stages(), plan[n]):
                actions.setdefault(when, []).append(stage)
    else:
        out_ref, made, total_ref = rest[:3]
        parts_ref, sums = rest[3:]

    def talk(point):
        for (at, where), todo in sorted(actions.items(), key=lambda item: item[0]):
            if where == point:

                def run_all(todo=todo):
                    for action in todo:
                        action()

                pl.when(step == at)(run_all)

    @pl.when(step == 0)
    def _():
        sums[...] = small_ref[...]

    talk(0)

    @pl.when(step < attends)
    def _():
        group = step // per_group
        column = step % per_group
        rows = pl.ds(pl.multiple_of(group * SEQ, SEQ), SEQ)
        logs = log_ref[0, 0].T
        for p in range(PAIRS):
            cols = pl.ds(128 * p, 128)
            done = attend_back_pair(
                q_ref[:, cols],
                k_ref[:, cols],
                v_ref[:, cols],
                grad_ref[:, cols],
                mixed_ref[:, cols],
                logs[:, 2 * p : 2 * p + 2],
            )
            where = pl.ds(pl.multiple_of(column * wide + 128 * p, 128), 128)
            for n in range(3):
                parts_ref[n, rows, where] = done[n]
            if p + 1 < PAIRS:
                talk(1)

    @pl.when((step >= attends) & (step < attends + weights))
    def _():
        part = (step - attends) // (width // 256)
        cols = pl.ds(pl.multiple_of((step - attends) % (width // 256) * 256, 256), 256)
        grad = parts_ref[part, :, cols]
        made[part, :, cols] = mm_ta(inp_ref[...], grad).astype(half)
        column = col_sum(grad.astype(single))

        @pl.when(part == 0)
        def _():
            sums[pl.ds(0, 1), cols] = column

        @pl.when(part == 2)
        def _():
            sums[pl.ds(1, 1), cols] = column

    @pl.when(step >= attends + weights)
    def _():
        block = out_ref.shape[0]
        rows = pl.ds(pl.multiple_of((step - attends - weights) * block, block), block)
        grad = dsum_ref[...]
        for n in range(3):
            grad = grad + mm_tb(parts_ref[n, rows, :], w_ref[:, pl.ds(n * width, width)])
        out_ref[...] = jnp.where(flag_ref[...] > 0, 0.0, grad)

    talk(2)
    if not links:
        total_ref[...] = sums[...]


def back(links, projected, d_mixed, mixed, logs, inputs, w_qkv, d_sum, flags, small, grads):
    count, width = mixed.shape
    groups = count // SEQ
    wide = 128 * PAIRS
    per_group = width // wide
    attends = groups * per_group
    weights = 3 * (width // 256)
    block = 256
    last = attends - 1

    def group_of(s):
        return jnp.minimum(s, last) // per_group

    def column_of(s):
        return jnp.minimum(s, last) % per_group

    def late(s):
        return jnp.maximum(s - attends - weights, 0)

    spec = lambda part: pl.BlockSpec((SEQ, wide), lambda s: (group_of(s), part * per_group + column_of(s)))
    whole = lambda shape: pl.BlockSpec(shape, lambda s: (0,) * len(shape), pipeline_mode=pl.Buffered(1))
    anywhere = pl.BlockSpec(memory_space=pl.ANY)
    in_specs = [
        spec(0),
        spec(1),
        spec(2),
        spec(0),
        spec(0),
        pl.BlockSpec((1, 1, 8, SEQ), lambda s: (group_of(s), column_of(s), 0, 0)),
        whole(inputs.shape),
        whole(w_qkv.shape),
        pl.BlockSpec((block, width), lambda s: (late(s), 0)),
        pl.BlockSpec((block, 1), lambda s: (late(s), 0)),
        whole(small.shape),
    ]
    out_specs = [pl.BlockSpec((block, width), lambda s: (late(s), 0))]
    out_shape = [jax.ShapeDtypeStruct((count, width), single)]
    operands = [projected, projected, projected, d_mixed, mixed, logs, inputs, w_qkv, d_sum, flags, small]
    dparts = pltpu.VMEM((3, count, width), half)
    sums = pltpu.VMEM(small.shape, single)
    plan = None
    if links:
        in_specs += [anywhere] * 3
        operands += grads
        shapes = [(width // 16, 3 * width)] + [(g.shape[0] // 16, g.shape[1]) for g in grads] + [small.shape]
        out_specs += [whole(shape) for shape in shapes]
        out_shape += [jax.ShapeDtypeStruct(shape, single) for shape in shapes]
        scratch = [dparts, pltpu.VMEM((3, width, width), half), sums]
        for shape in [grads[2].shape, grads[1].shape, grads[0].shape] + [(width, width)] * 3:
            scratch += Scatter.scratch(shape)
        scratch += Total.scratch(small.shape)
        params = pltpu.CompilerParams(collective_id=2, has_side_effects=True, vmem_limit_bytes=VMEM_LIMIT)
        plan = back_plan(attends, weights, count // block)
    else:
        out_specs += [whole((3, width, width)), whole(small.shape)]
        out_shape += [jax.ShapeDtypeStruct((3, width, width), half), jax.ShapeDtypeStruct(small.shape, single)]
        scratch = [dparts, sums]
        params = pltpu.CompilerParams(vmem_limit_bytes=VMEM_LIMIT)
    return pl.pallas_call(
        functools.partial(back_body, links, plan),
        grid=(attends + weights + count // block,),
        in_specs=in_specs,
        out_specs=out_specs,
        out_shape=out_shape,
        scratch_shapes=scratch,
        compiler_params=params,
        name="back",
    )(*operands)


def back_plan(attends, weights, inputs):
    def at(n):
        if n < 2 * attends:
            return n // 2, n % 2
        n -= 2 * attends
        return (attends + n, 0) if n < weights + inputs else (attends + weights + inputs - 1, 2)

    down = [0, 3, 11, 18, 20, 22, 23, 24, 25]
    up = [0, 5, 19, 25, 27, 28, 29, 30, 31]
    out = [0, 6, 21, 26, 28, 29, 30, 31, 32]
    third = lambda n: [n, n + 1, n + 4, n + 6, n + 8, n + 9, n + 10, n + 11, 99]
    small = [33, 34, 36, 38, 40]
    after = 2 * attends
    table = [down, up, out, third(after + 3), third(after + 6), third(after + 9), small]
    return [[at(n) for n in row] for row in table]


def pack_small(vectors, b_up, low):
    n = vectors[0].shape[0]
    block = jnp.concatenate([jnp.stack(vectors), b_up.reshape(-1, n)])
    block = lax.reduce_precision(block, 8, 7) if low else block
    return jnp.pad(block, ((0, 16 - block.shape[0]), (0, 128 - n)))


def unpack_small(full, chips, n):
    full = full.reshape(chips, 16, 128)
    vectors = full[:, :8, :n].transpose(1, 0, 2).reshape(8, chips * n)
    return vectors, full[:, 8:12, :n].reshape(1, 4 * chips * n)


def local(chips, twins, tokens, flags, mask_embed, cotangent, w_qkv, b_qv, w_out, b_out, norm_one, w_up, b_up, w_down, b_down, norm_two):
    own_kernels = chips == 16 and twins == 2
    n = b_out.shape[0]
    width = chips * n
    small = pack_small(
        [b_qv[0], b_qv[1], b_out, norm_one[0], norm_one[1], b_down, norm_two[0], norm_two[1]], b_up, True
    )
    shards = [w_qkv, w_out, w_up, w_down]
    if own_kernels:
        *fulls, small_full = gather_all(shards + [small], [half] * 4 + [single], 1)
    else:
        fulls = [lax.all_gather(s.astype(half), "dp", axis=0, tiled=True) for s in shards]
        small_full = lax.all_gather(small, "dp", axis=0, tiled=True)
    qkv_full, out_full, up_full, down_full = fulls
    vecs, bup_full = unpack_small(small_full, chips, n)
    bias = jnp.concatenate([vecs[0], jnp.zeros_like(vecs[0]), vecs[1]])[None]
    flag_col = flags[:, None]
    inputs, projected = project(tokens, flag_col, mask_embed[None], qkv_full, bias)
    mixed, logs = attend(projected)
    activations, d_sum, d_mixed, g_small, g_out, g_up, g_down = middle(
        mixed, inputs, flag_col, cotangent, vecs, bup_full, out_full, up_full, down_full
    )
    grads = [g_out, g_up, g_down]
    input_grad, g_qkv, *summed = back(
        own_kernels, projected, d_mixed, mixed, logs, inputs, qkv_full, d_sum, flag_col, g_small, grads
    )
    if own_kernels:
        g_out, g_up, g_down, g_small = summed
    else:
        g_small = summed[0]
        grads = [jnp.concatenate([g_qkv[0], g_qkv[1], g_qkv[2]], axis=1)] + grads
        grads = [lax.psum_scatter(g.astype(single), "dp", scatter_dimension=0, tiled=True) for g in grads]
        g_qkv, g_out, g_up, g_down = [lax.psum(g.astype(half), "rep").astype(single) for g in grads]
        g_small = lax.psum(g_small, ("dp", "rep"))
    me = lax.axis_index("dp")
    rows = lax.dynamic_slice_in_dim(g_small[:8], me * n, n, axis=1)
    g_bup = lax.dynamic_slice_in_dim(g_small[8:12].reshape(4 * width), me * 4 * n, 4 * n)
    return (
        activations,
        input_grad,
        g_qkv,
        rows[0:2],
        g_out,
        rows[2],
        rows[3:5],
        g_up,
        g_bup,
        g_down,
        rows[5],
        rows[6:8],
    )


def solution(mesh):
    rows = P(("dp", "rep"), None)
    first = P("dp", None)
    second = P(None, "dp")
    return jax.shard_map(
        functools.partial(local, mesh.shape["dp"], mesh.shape["rep"]),
        mesh=mesh,
        in_specs=(rows, P(("dp", "rep")), P(), rows, first, second, first, P("dp"), second, first, P("dp"), first, P("dp"), second),
        out_specs=(rows, rows, first, second, first, P("dp"), second, first, P("dp"), first, P("dp"), second),
        check_vma=False,
    )
```

```python
import functools

import jax
import jax.numpy as jnp
from jax import lax
from jax.experimental import pallas as pl
from jax.experimental.pallas import tpu as pltpu
from jax.sharding import PartitionSpec as P

HEADS = 12
SEQ = 512
EPS = 1e-12
half = jnp.bfloat16
single = jnp.float32
VMEM_LIMIT = 61 * 1024 * 1024


def mm(left, right):
    return jnp.dot(left, right, preferred_element_type=single)


def mm_tb(left, right):
    return lax.dot_general(left, right, (((1,), (1,)), ((), ())), preferred_element_type=single)


def mm_ta(left, right):
    return lax.dot_general(left, right, (((0,), (0,)), ((), ())), preferred_element_type=single)


def row_mean(values):
    return jnp.mean(values, axis=-1, keepdims=True)


def col_sum(values):
    return jnp.sum(values, axis=0, keepdims=True)


def head_masks(width):
    lane = lax.broadcasted_iota(jnp.int32, (1, width), 1)
    return [(lane // 64) == h for h in range(width // 64)]


def attend_pair(query, keys, vals):
    scaled = query * half(0.125)
    turned = vals.T
    outs, logs = [], []
    for h, mask in enumerate(head_masks(128)):
        own = jnp.where(mask, keys, half(0))
        scores = mm_tb(own, scaled)
        top = jnp.max(scores, axis=0, keepdims=True)
        expo = jnp.exp(scores - top)
        total = jnp.sum(expo, axis=0, keepdims=True)
        mixed = mm(turned[64 * h : 64 * h + 64], expo.astype(half))
        outs.append(mixed * (1.0 / total))
        logs.append(top + jnp.log(total))
    return jnp.concatenate(outs, axis=0).astype(half).T, logs


def attend_back_pair(query, keys, vals, grad, mixed, logs):
    scaled = query * half(0.125)
    scaled_keys = keys * half(0.125)
    product = grad.astype(single) * mixed.astype(single)
    grad_turned = grad.T
    scaled_turned = scaled.T
    d_vals, d_keys, d_query = [], [], None
    for h, mask in enumerate(head_masks(128)):
        scores = mm_tb(jnp.where(mask, scaled, half(0)), keys)
        probs = jnp.exp(scores - logs[:, h : h + 1])
        d_probs = mm_tb(jnp.where(mask, grad, half(0)), vals)
        delta = jnp.sum(jnp.where(mask, product, 0.0), axis=1, keepdims=True)
        d_scores = (probs * (d_probs - delta)).astype(half)
        rows = slice(64 * h, 64 * h + 64)
        d_vals.append(mm(grad_turned[rows], probs.astype(half)))
        d_keys.append(mm(scaled_turned[rows], d_scores))
        part = mm(d_scores, jnp.where(mask, scaled_keys, half(0)))
        d_query = part if d_query is None else d_query + part
    turn = lambda parts: jnp.concatenate(parts, axis=0).astype(half).T
    return d_query.astype(half), turn(d_keys), turn(d_vals)


def norm(values, gain, shift):
    center = values - row_mean(values)
    inverse = lax.rsqrt(row_mean(center * center) + EPS)
    unit = center * inverse
    return unit * gain + shift, unit, inverse


def norm_back(grad, unit, inverse, gain):
    scaled = grad * gain
    return inverse * (scaled - row_mean(scaled) - unit * row_mean(scaled * unit))


def middle_body(
    mixed_ref,
    inp_ref,
    flag_ref,
    cot_ref,
    vec_ref,
    wo_ref,
    wu_ref,
    wd_ref,
    act_out,
    dsum_out,
    dmix_out,
    small_out,
    gwo_out,
    gwu_out,
    gwd_out,
    unit1,
    first,
    low,
    acts,
    slope,
    total,
    d_low,
    acc_o,
    acc_u,
    acc_d,
    stage,
    sems,
):
    step = pl.program_id(0)
    last = pl.num_programs(0) - 1
    width = wo_ref.shape[0]
    chunks = wd_ref.shape[0] // width

    @pl.when(step == 0)
    def _():
        small_out[...] = jnp.zeros_like(small_out)
        acc_o[...] = jnp.zeros_like(acc_o)
        acc_u[...] = jnp.zeros_like(acc_u)
        acc_d[...] = jnp.zeros_like(acc_d)

    vec = lambda row: vec_ref[pl.ds(row, 1), :]
    attended = mm(mixed_ref[...], wo_ref[...]) + vec(2)
    value, unit, inv1 = norm(inp_ref[...].astype(single) + attended, vec(3), vec(4))
    unit1[...] = unit
    first[...] = value
    low[...] = value.astype(half)
    total[...] = jnp.zeros_like(total)

    @pl.loop(0, chunks)
    def _(j):
        cols = pl.ds(pl.multiple_of(j * width, width), width)
        upper = mm(low[...], wu_ref[:, cols]) + vec(8 + j)
        phi = 0.5 * (1.0 + lax.erf(upper * 0.7071067811865476))
        act = (upper * phi).astype(half)
        acts[j] = act
        slope[j] = (phi + upper * jnp.exp(-0.5 * upper * upper) * 0.3989422804014327).astype(half)
        total[...] += mm(act, wd_ref[cols, :])

    value, unit, inv2 = norm(first[...] + total[...] + vec(5), vec(6), vec(7))
    act_out[...] = value.astype(half)
    out_grad = jnp.where(flag_ref[...] > 0, cot_ref[...].astype(single), 0.0)
    small_out[pl.ds(6, 1), :] += col_sum(out_grad * unit)
    small_out[pl.ds(7, 1), :] += col_sum(out_grad)
    d_second = norm_back(out_grad, unit, inv2, vec(6))
    lowered = d_second.astype(half)
    d_low[...] = lowered
    small_out[pl.ds(5, 1), :] += col_sum(lowered.astype(single))
    total[...] = d_second

    @pl.loop(0, chunks)
    def _(j):
        cols = pl.ds(pl.multiple_of(j * width, width), width)
        d_acts = mm_tb(d_low[...], wd_ref[cols, :])
        d_upper = (d_acts * slope[j].astype(single)).astype(half)
        small_out[pl.ds(8 + j, 1), :] += col_sum(d_upper.astype(single))
        total[...] += mm_tb(d_upper, wu_ref[:, cols])
        acc_d[j] += mm_ta(acts[j], d_low[...])
        acc_u[j] += mm_ta(low[...], d_upper)

    d_first = total[...]
    unit = unit1[...]
    small_out[pl.ds(3, 1), :] += col_sum(d_first * unit)
    small_out[pl.ds(4, 1), :] += col_sum(d_first)
    d_sum = norm_back(d_first, unit, inv1, vec(3))
    dsum_out[...] = d_sum
    d_att = d_sum.astype(half)
    small_out[pl.ds(2, 1), :] += col_sum(d_att.astype(single))
    dmix_out[...] = mm_tb(d_att, wo_ref[...]).astype(half)
    acc_o[...] += mm_ta(mixed_ref[...], d_att)

    @pl.when(step == last)
    def _():
        copies = []
        todo = [(acc_d.at[j], gwd_out.at[pl.ds(j * width, width), :]) for j in range(chunks)]
        todo += [(acc_u.at[j], gwu_out.at[:, pl.ds(j * width, width)]) for j in range(chunks)]
        todo += [(acc_o, gwo_out)]
        for n, (src, dst) in enumerate(todo):
            slot = n % 2
            if n >= 2:
                copies[n - 2].wait()
            stage[slot] = src[...].astype(half)
            copies.append(pltpu.make_async_copy(stage.at[slot], dst, sems.at[slot]))
            copies[n].start()
        for copy in copies[-2:]:
            copy.wait()


def middle(mixed, inputs, flags, cotangent, vecs, w_out, w_up, w_down, block=512):
    count, width = mixed.shape
    hidden = w_up.shape[1]
    chunks = hidden // width
    rows = lambda cols: pl.BlockSpec((block, cols), lambda i: (i, 0))
    once = lambda shape: pl.BlockSpec(shape, lambda i: (0, 0), pipeline_mode=pl.Buffered(1))
    keep = lambda shape: pl.BlockSpec(shape, lambda i: (0, 0))
    whole = pl.BlockSpec(memory_space=pl.ANY)
    return pl.pallas_call(
        middle_body,
        grid=(count // block,),
        in_specs=[
            rows(width),
            rows(width),
            rows(1),
            rows(width),
            keep((16, width)),
            once((width, width)),
            once((width, hidden)),
            once((hidden, width)),
        ],
        out_specs=[
            rows(width),
            rows(width),
            rows(width),
            keep((16, width)),
            whole,
            whole,
            whole,
        ],
        out_shape=[
            jax.ShapeDtypeStruct((count, width), half),
            jax.ShapeDtypeStruct((count, width), single),
            jax.ShapeDtypeStruct((count, width), half),
            jax.ShapeDtypeStruct((16, width), single),
            jax.ShapeDtypeStruct((width, width), half),
            jax.ShapeDtypeStruct((width, hidden), half),
            jax.ShapeDtypeStruct((hidden, width), half),
        ],
        scratch_shapes=[
            pltpu.VMEM((block, width), single),
            pltpu.VMEM((block, width), single),
            pltpu.VMEM((block, width), half),
            pltpu.VMEM((chunks, block, width), half),
            pltpu.VMEM((chunks, block, width), half),
            pltpu.VMEM((block, width), single),
            pltpu.VMEM((block, width), half),
            pltpu.VMEM((width, width), single),
            pltpu.VMEM((chunks, width, width), single),
            pltpu.VMEM((chunks, width, width), single),
            pltpu.VMEM((2, width, width), half),
            pltpu.SemaphoreType.DMA((2,)),
        ],
        compiler_params=pltpu.CompilerParams(vmem_limit_bytes=VMEM_LIMIT),
        name="middle",
    )(mixed, inputs, flags, cotangent, vecs, w_out, w_up, w_down)


MESH = pl.DeviceIdType.MESH
ZS = 4


class Place:
    def __init__(self):
        self.me = lax.axis_index("dp")
        self.core = lax.axis_index("rep")
        self.z = self.me // 4
        self.y = (self.me // 2) % 2
        self.x = self.me % 2
        step_x = 1 - 2 * self.x
        step_y = 2 - 4 * self.y
        self.near = self.me + step_x + self.core * (step_y - step_x)
        self.far = self.me + step_y + self.core * (step_x - step_y)
        self.diag = self.me + step_x + step_y
        self.near_bit = self.x + self.core * (self.y - self.x)
        self.far_bit = self.y + self.core * (self.x - self.y)

    def chip(self, z, far, near):
        return z * 4 + far * (2 - self.core) + near * (1 + self.core)

    def partner(self):
        return (self.me, 1 - self.core)

    def barrier(self):
        sem = pltpu.get_barrier_semaphore()
        tell = lambda dev: pl.semaphore_signal(sem, inc=1, device_id=dev, device_id_type=MESH)
        tell(self.partner())
        tell((self.near, self.core))
        tell((self.far, self.core))

        for k in range(1, ZS):
            tell(((self.me + 4 * k) % (4 * ZS), self.core))
        return sem, 3 + ZS - 1


def send(src, dst, send_sem, recv_sem, dev):
    return pltpu.make_async_remote_copy(
        src_ref=src, dst_ref=dst, send_sem=send_sem, recv_sem=recv_sem, device_id=dev, device_id_type=MESH
    )


OWN, COLUMN, NEAR, FAR, DIAG, END = range(6)


class Gather:
    def __init__(self, place, own, full, rows, offset, cols, sends, recvs, passed):
        self.place, self.own, self.full = place, own, full
        self.rows, self.offset, self.cols = rows, offset, cols
        self.stride = full.shape[1] // 2
        self.sends, self.recvs, self.passed = sends, recvs, passed

    def window(self, h):
        return pl.ds(pl.multiple_of(h * self.stride + self.offset, 128), self.cols)

    def piece(self, q, h):
        return self.full.at[pl.ds(pl.multiple_of(q * self.rows, 16), self.rows), self.window(h)]

    def stage(self, kind, r):
        p = self.place
        yes = p.z >= 0
        up = ((p.me + 4, p.core), p.z < ZS - 1)
        down = ((p.me - 4, p.core), p.z > 0)
        near = ((p.near, p.core), yes)
        far = ((p.far, p.core), yes)
        other = (p.partner(), None)
        if kind == OWN:
            return [(p.me, yes, [up, down, near, far])]
        base = {COLUMN: p.me, NEAR: p.near, FAR: p.far, DIAG: p.diag}[kind]
        ways = [(-4 * r, p.z >= r, up), (4 * r, p.z + r < ZS, down)] if r else [(0, yes, None)]
        onward = {COLUMN: [near, far, other], NEAR: [far, other], FAR: [other], DIAG: [other]}[kind]
        return [(base + shift, there, ([way] if kind == COLUMN else []) + onward) for shift, there, way in ways]

    def copies(self, kind, q, targets):
        p = self.place
        dst = self.piece(q, p.core)
        src = self.own.at[:, self.window(p.core)] if kind == OWN else dst
        made = []
        for n, (dev, cond) in enumerate(targets):
            recv = self.passed.at[q] if cond is None else self.recvs.at[q]
            made.append((send(src, dst, self.sends.at[n, q], recv, dev), cond))
        return made

    def run(self, kind, r):
        if kind == END:
            return self.finish_partner()
        for q, there, targets in self.stage(kind, r):

            def go(q=q, targets=targets):
                if kind != OWN:
                    piece = self.piece(q, self.place.core)
                    send(piece, piece, self.sends.at[0, q], self.recvs.at[q], self.place.partner()).wait_recv()
                for copy, cond in self.copies(kind, q, targets):
                    copy.start() if cond is None else pl.when(cond)(copy.start)

            pl.when(there)(go)

    def finish_sends(self, kind, r):
        if kind == END:
            return
        for q, there, targets in self.stage(kind, r):

            def go(q=q, targets=targets):
                for copy, cond in self.copies(kind, q, targets):
                    copy.wait_send() if cond is None else pl.when(cond)(copy.wait_send)

            pl.when(there)(go)

    def finish_partner(self):
        p = self.place

        @pl.loop(0, 4 * ZS)
        def _(q):
            @pl.when(q != p.me)
            def _():
                piece = self.piece(q, 1 - p.core)
                send(piece, piece, self.sends.at[0, q], self.passed.at[q], p.partner()).wait_recv()


class Scatter:
    def __init__(self, place, grad, rows, out, mine, pair, far, near, low, high, own, got, sems):
        self.place = place
        self.grad, self.rows, self.out = grad, rows, out
        self.mine, self.pair, self.far, self.near, self.low, self.high, self.own, self.got = mine, pair, far, near, low, high, own, got
        self.sems = sems
        self.cols = grad.shape[1] // 2

    LOCAL, PAIR_S, PAIR_R, LAST_S, LAST_R, FAR_S, FAR_R = 0, 1, 2, 3, 4, 8, 16
    NEAR_S, NEAR_R, UP_S, UP_R, DOWN_S, DOWN_R = 24, 28, 32, 36, 40, 44
    COUNT = 48

    def columns(self, h):
        return pl.ds(pl.multiple_of(h * self.cols, 128), self.cols)

    def at(self, ref, q):
        return ref.at[pl.ds(pl.multiple_of(q * self.rows, 16), self.rows), :]

    def load(self, ref, q):
        return ref[pl.ds(pl.multiple_of(q * self.rows, 16), self.rows), :]

    def store(self, ref, q, value):
        ref[pl.ds(pl.multiple_of(q * self.rows, 16), self.rows), :] = value.astype(ref.dtype)

    def copy_local(self):
        return pltpu.make_async_copy(
            self.grad.at[:, self.columns(self.place.core)], self.mine, self.sems.at[self.LOCAL]
        )

    def copy_pair(self):
        p = self.place
        return send(
            self.grad.at[:, self.columns(1 - p.core)],
            self.pair,
            self.sems.at[self.PAIR_S],
            self.sems.at[self.PAIR_R],
            p.partner(),
        )

    def copy_far(self, k):
        p = self.place
        q = p.chip(k // 2, 1 - p.far_bit, k % 2)
        return send(
            self.at(self.mine, q),
            self.at(self.far, k),
            self.sems.at[self.FAR_S + k],
            self.sems.at[self.FAR_R + k],
            (p.far, p.core),
        )

    def copy_near(self, z):
        p = self.place
        return send(
            self.at(self.far, z * 2 + 1 - p.near_bit),
            self.at(self.near, z),
            self.sems.at[self.NEAR_S + z],
            self.sems.at[self.NEAR_R + z],
            (p.near, p.core),
        )

    def copy_up(self, z):
        p = self.place
        return send(
            self.at(self.near, z),
            self.at(self.low, z),
            self.sems.at[self.UP_S + z],
            self.sems.at[self.UP_R + z],
            (p.me + 4, p.core),
        )

    def copy_down(self, z):
        p = self.place
        return send(
            self.at(self.near, z),
            self.at(self.high, z),
            self.sems.at[self.DOWN_S + z],
            self.sems.at[self.DOWN_R + z],
            (p.me - 4, p.core),
        )

    def copy_last(self):
        p = self.place
        return send(
            self.own,
            self.got,
            self.sems.at[self.LAST_S],
            self.sems.at[self.LAST_R],
            p.partner(),
        )

    def start(self):
        self.copy_local().start()
        self.copy_pair().start()

    def to_far(self):
        p = self.place
        self.copy_local().wait()
        self.copy_pair().wait_recv()

        @pl.loop(0, 8)
        def _(k):
            q = p.chip(k // 2, 1 - p.far_bit, k % 2)
            self.store(self.mine, q, self.load(self.mine, q) + self.load(self.pair, q))
            self.copy_far(k).start()

    def to_near(self):
        p = self.place

        def add(k):
            q = p.chip(k // 2, p.far_bit, k % 2)
            self.copy_far(k).wait_recv()
            self.store(
                self.far, k, self.load(self.far, k) + self.load(self.mine, q) + self.load(self.pair, q)
            )

        @pl.loop(0, 4)
        def _(z):
            add(z * 2 + 1 - p.near_bit)
            self.copy_near(z).start()

        @pl.loop(0, 4)
        def _(z):
            add(z * 2 + p.near_bit)

    def to_line(self):
        p = self.place

        @pl.loop(0, 4)
        def _(z):
            self.copy_near(z).wait_recv()
            self.store(self.near, z, self.load(self.near, z) + self.load(self.far, z * 2 + p.near_bit))

        @pl.when(p.z == 0)
        def _():
            for z in (3, 2, 1):
                self.copy_up(z).start()

        @pl.when(p.z == ZS - 1)
        def _():
            for z in (0, 1, 2):
                self.copy_down(z).start()

    def along(self, step):
        p = self.place

        @pl.when(p.z == step)
        def _():
            for z in (3, 2, 1):
                if z >= step:
                    self.copy_up(z).wait_recv()
                if z > step:
                    self.store(self.near, z, self.load(self.near, z) + self.load(self.low, z))
                    self.copy_up(z).start()

        @pl.when(p.z == ZS - 1 - step)
        def _():
            for z in (0, 1, 2):
                if z <= ZS - 1 - step:
                    self.copy_down(z).wait_recv()
                if z < ZS - 1 - step:
                    self.store(self.near, z, self.load(self.near, z) + self.load(self.high, z))
                    self.copy_down(z).start()

    def to_last(self):
        p = self.place
        self.own[...] = self.load(self.near, p.z).astype(single)

        @pl.when(p.z > 0)
        def _():
            self.own[...] += self.load(self.low, p.z).astype(single)

        @pl.when(p.z < ZS - 1)
        def _():
            self.own[...] += self.load(self.high, p.z).astype(single)

        self.copy_last().start()
        self.out[:, self.columns(p.core)] = self.own[...]

    def finish(self):
        p = self.place
        self.copy_pair().wait_send()

        @pl.loop(0, 8)
        def _(k):
            self.copy_far(k).wait_send()

        @pl.loop(0, 4)
        def _(z):
            self.copy_near(z).wait_send()

            @pl.when(z > p.z)
            def _():
                self.copy_up(z).wait_send()

            @pl.when(z < p.z)
            def _():
                self.copy_down(z).wait_send()

        self.copy_last().wait()
        self.out[:, self.columns(1 - p.core)] = self.got[...]

    def stages(self):
        return [
            self.start,
            self.to_far,
            self.to_near,
            self.to_line,
            lambda: self.along(1),
            lambda: self.along(2),
            lambda: self.along(3),
            self.to_last,
            self.finish,
        ]

    @staticmethod
    def scratch(shape):
        total, cols = shape[0], shape[1] // 2
        rows = total // 16
        return [
            pltpu.VMEM((total, cols), half),
            pltpu.VMEM((total, cols), half),
            pltpu.VMEM((8 * rows, cols), half),
            pltpu.VMEM((4 * rows, cols), half),
            pltpu.VMEM((4 * rows, cols), half),
            pltpu.VMEM((4 * rows, cols), half),
            pltpu.VMEM((rows, cols), single),
            pltpu.VMEM((rows, cols), single),
            pltpu.SemaphoreType.DMA((Scatter.COUNT,)),
        ]


class Total:
    COUNT = 12

    def __init__(self, place, start, pair, result, parts, held, sems):
        self.place, self.first, self.pair, self.result = place, start, pair, result
        self.parts, self.held, self.sems = parts, held, sems

    def copy(self, n):
        p = self.place
        if n == 0:
            src, dev = self.first, p.partner()
        elif n <= 3:
            src, dev = self.held.at[0], ((p.me + 4 * n) % (4 * ZS), p.core)
        elif n == 4:
            src, dev = self.held.at[1], (p.near, p.core)
        else:
            src, dev = self.held.at[2], (p.far, p.core)
        return send(src, self.parts.at[n], self.sems.at[n], self.sems.at[6 + n], dev)

    def stages(self):
        def begin():
            if self.pair:
                self.copy(0).start()

        def column():
            value = self.first[...]
            if self.pair:
                self.copy(0).wait_recv()
                value = value + self.parts[0]
            self.held[0] = value
            for n in (1, 2, 3):
                self.copy(n).start()

        def near():
            value = self.held[0]
            for n in (1, 2, 3):
                self.copy(n).wait_recv()
                value = value + self.parts[n]
            self.held[1] = value
            self.copy(4).start()

        def far():
            self.copy(4).wait_recv()
            self.held[2] = self.held[1] + self.parts[4]
            self.copy(5).start()

        def finish():
            self.copy(5).wait_recv()
            self.result[...] = self.held[2] + self.parts[5]
            for n in range(0 if self.pair else 1, 6):
                self.copy(n).wait_send()

        return [begin, column, near, far, finish]

    @staticmethod
    def scratch(shape):
        return [
            pltpu.VMEM((6,) + shape, single),
            pltpu.VMEM((3,) + shape, single),
            pltpu.SemaphoreType.DMA((Total.COUNT,)),
        ]


PAIRS = 2


FRONT_PLAN = [
    (-1, 0, 0, 0), (-1, 1, 0, 0), (-1, 0, 2, 0), (-1, 0, 3, 0), (-1, 0, 1, 1), (-1, 1, 2, 0),
    (-1, 1, 3, 0), (-1, 1, 1, 1), (-1, 0, 4, 0), (-1, 0, 1, 2), (-1, 1, 1, 2), (-1, 0, 2, 1),
    (-1, 0, 3, 1), (-1, 1, 4, 0), (-1, 1, 2, 1), (-1, 0, 1, 3), (-1, 0, 2, 2), (-1, 1, 1, 3),
    (-1, 1, 3, 1), (-1, 1, 2, 2), (-1, 0, 3, 2), (-1, 1, 3, 2), (-1, 0, 2, 3), (-1, 0, 3, 3),
    (-1, 0, 4, 1), (-1, 1, 2, 3), (-1, 2, 0, 0), (-1, 3, 0, 0), (-1, 4, 0, 0), (-1, 1, 4, 1),
    (-1, 1, 3, 3), (-1, 0, 4, 2), (-1, 1, 4, 2), (-1, 0, 4, 3), (-1, 1, 4, 3), (-1, 2, 2, 0),
    (-1, 2, 1, 1), (-1, 0, 5, 0), (-1, 2, 3, 0), (-1, 1, 5, 0), (1, 3, 2, 0), (1, 3, 3, 0),
    (1, 3, 1, 1), (3, 4, 2, 0), (3, 4, 1, 1), (3, 2, 1, 2), (3, 4, 3, 0), (4, 2, 4, 0),
    (4, 2, 2, 1), (5, 2, 3, 1), (6, 3, 1, 2), (7, 3, 4, 0), (8, 2, 1, 3), (8, 3, 2, 1),
    (8, 4, 1, 2), (10, 3, 1, 3), (11, 2, 2, 3), (11, 3, 3, 1), (13, 2, 2, 2), (13, 4, 4, 0),
    (13, 4, 2, 1), (13, 4, 1, 3), (15, 3, 2, 2), (15, 3, 2, 3), (16, 2, 3, 3), (17, 2, 3, 2),
    (17, 4, 3, 1), (17, 4, 2, 2), (17, 4, 2, 3), (18, 2, 4, 1), (19, 3, 3, 2), (20, 3, 3, 3),
    (21, 2, 4, 3), (21, 3, 4, 1), (22, 2, 4, 2), (22, 4, 3, 2), (22, 4, 3, 3), (24, 2, 5, 0),
    (24, 4, 4, 1), (25, 3, 4, 3), (26, 3, 4, 2), (27, 4, 4, 2), (27, 4, 4, 3), (28, 3, 5, 0),
    (31, 4, 5, 0),
]
SMALL_AT = (0, 8, 14, 23)


def front_body(links, *refs):
    tok_ref, flag_ref, mask_ref, small_ref = refs[:4]
    step = pl.program_id(0)
    count = pl.num_programs(0)
    per_group = 1 + HEADS // (2 * PAIRS)
    actions = {}
    if links:
        shards, (inp_ref, proj_ref, mixed_ref, log_ref, vec_ref) = refs[4:8], refs[8:13]
        fulls, w_ref, own, rest = refs[13:17], refs[17], refs[18:21], refs[21:]
        place = Place()
        local = rest[0]
        sets = [rest[1 + 3 * n : 4 + 3 * n] for n in range(5)]
        total = Total(place, small_ref, False, vec_ref, *rest[16:19])
        rows = [shard.shape[0] for shard in shards]
        mine = pl.ds(pl.multiple_of(place.me * rows[0], 16), rows[0])
        cut = w_ref.shape[1] // 2
        first = cut // 2 // 128 * 128 + 128
        parts = [
            Gather(place, w_ref.at[mine], w_ref, rows[0], 0, first, *sets[0]),
            Gather(place, w_ref.at[mine], w_ref, rows[0], first, cut - first, *sets[1]),
        ]
        parts += [Gather(place, own[t], fulls[t + 1], rows[t + 1], 0, fulls[t + 1].shape[1] // 2, *sets[t + 2]) for t in range(3)]
        keep = pltpu.make_async_copy(w_ref, fulls[0], local.at[0])
        mine_to = [
            pltpu.make_async_copy(
                own[t], fulls[t + 1].at[pl.ds(pl.multiple_of(place.me * rows[t + 1], 16), rows[t + 1]), :], local.at[t + 1]
            )
            for t in range(3)
        ]

        def enter():
            sem, expect = place.barrier()
            w_ref[mine, :] = shards[0][...].astype(half)
            for t in range(3):
                own[t][...] = shards[t + 1][...].astype(half)
            pl.semaphore_wait(sem, expect)
            for copy in mine_to:
                copy.start()

        stages = total.stages()
        todo = [(-1, enter), (-1, stages[1])]
        seen = 0
        for n, part, kind, r in FRONT_PLAN:
            if seen in SMALL_AT[1:]:
                todo.append((-1, stages[1 + SMALL_AT.index(seen)]))
            todo.append((n, functools.partial(parts[part].run, kind, r)))
            seen += 1
        todo.append((0, keep.start))

        def leave():
            keep.wait()
            for copy in mine_to:
                copy.wait()
            for _, part, kind, r in FRONT_PLAN:
                parts[part].finish_sends(kind, r)

        for n, action in sorted(todo, key=lambda item: item[0]):
            actions.setdefault(front_point(per_group, n), []).append(action)
        actions.setdefault((4 * per_group - 1, 2), []).append(leave)
    else:
        w_ref, (inp_ref, proj_ref, mixed_ref, log_ref, vec_ref) = refs[4], refs[5:]
        vec_ref[...] = small_ref[...]

    def talk(point):
        for (at, where), todo in sorted(actions.items(), key=lambda item: item[0]):
            if where == point:

                def run_all(todo=todo):
                    for action in todo:
                        action()

                pl.when(step == at)(run_all)

    talk(0)
    column = step % per_group - 1
    wide = 128 * PAIRS
    width = inp_ref.shape[1]

    @pl.when(column < 0)
    def _():
        masked = flag_ref[...] > 0
        low = jnp.where(masked, mask_ref[...].astype(single), tok_ref[...].astype(single)).astype(half)
        inp_ref[...] = low
        for n in range(3):
            cols = pl.ds(n * width, width)
            value = mm(low, w_ref[:, cols])
            if n != 1:
                value = value + vec_ref[pl.ds(n // 2, 1), :]
            proj_ref[:, cols] = value.astype(half)

    @pl.when(column >= 0)
    def _():
        for p in range(PAIRS):
            start = column * wide + 128 * p
            q, k, v = (proj_ref[:, pl.ds(pl.multiple_of(start + n * width, 128), 128)] for n in range(3))
            mixed, logs = attend_pair(q, k, v)
            mixed_ref[:, pl.ds(128 * p, 128)] = mixed
            for h in range(2):
                log_ref[0, 0, pl.ds(2 * p + h, 1), :] = logs[h]
            if p + 1 < PAIRS:
                talk(1)

    talk(2)


def front_point(per_group, n):
    points = 1 + (per_group - 1) * PAIRS
    if n < 0:
        return (0, 0)
    if n >= 4 * points:
        return (4 * per_group - 1, 2)
    group, n = n // points, n % points
    if n == 0:
        return (group * per_group, 0)
    return (group * per_group + 1 + (n - 1) // PAIRS, (n - 1) % PAIRS)


def front(links, tokens, flags, mask_embed, small, shards):
    count, width = tokens.shape
    groups = count // SEQ
    wide = 128 * PAIRS
    steps = width // wide
    per_group = steps + 1
    group = lambda cols: pl.BlockSpec((SEQ, cols), lambda s: (s // per_group, 0))
    whole = lambda shape: pl.BlockSpec(shape, lambda s: (0,) * len(shape), pipeline_mode=pl.Buffered(1))
    column = lambda s: jnp.maximum(s % per_group - 1, 0)
    anywhere = pl.BlockSpec(memory_space=pl.ANY)
    in_specs = [group(width), group(1), whole((1, width)), whole(small.shape)] + [whole(s.shape) for s in shards]
    out_specs = [
        group(width),
        group(3 * width),
        pl.BlockSpec((SEQ, wide), lambda s: (s // per_group, column(s))),
        pl.BlockSpec((1, 1, 8, SEQ), lambda s: (s // per_group, column(s), 0, 0)),
        whole(small.shape),
    ]
    out_shape = [
        jax.ShapeDtypeStruct((count, width), half),
        jax.ShapeDtypeStruct((count, 3 * width), half),
        jax.ShapeDtypeStruct((count, width), half),
        jax.ShapeDtypeStruct((groups, steps, 8, SEQ), single),
        jax.ShapeDtypeStruct(small.shape, single),
    ]
    scratch = []
    params = pltpu.CompilerParams(vmem_limit_bytes=VMEM_LIMIT)
    if links:
        full = [(4 * ZS * s.shape[0], s.shape[1]) for s in shards]
        out_specs += [anywhere] * 4
        out_shape += [jax.ShapeDtypeStruct(shape, half) for shape in full]
        scratch += [pltpu.VMEM(full[0], half)] + [pltpu.VMEM(s.shape, half) for s in shards[1:]]
        scratch.append(pltpu.SemaphoreType.DMA((4,)))
        for _ in range(5):
            scratch += [pltpu.SemaphoreType.DMA((4, 4 * ZS))] + [pltpu.SemaphoreType.DMA((4 * ZS,))] * 2
        scratch += Total.scratch(small.shape)
        params = pltpu.CompilerParams(collective_id=1, has_side_effects=True, vmem_limit_bytes=VMEM_LIMIT)
    return pl.pallas_call(
        functools.partial(front_body, links),
        grid=(groups * per_group,),
        in_specs=in_specs,
        out_specs=out_specs,
        out_shape=out_shape,
        scratch_shapes=scratch,
        compiler_params=params,
        name="front",
    )(tokens, flags, mask_embed, small, *shards)


def back_body(links, steps, *refs):
    q_ref, k_ref, v_ref, grad_ref, mixed_ref, log_ref, inp_ref, w_ref, dsum_ref, flag_ref, small_ref = refs[:11]
    rest = refs[11:]
    step = pl.program_id(0)
    width = inp_ref.shape[1]
    count = inp_ref.shape[0]
    wide = 128 * PAIRS
    per_group = width // wide
    attends = (count // SEQ) * per_group
    weights = 3 * (width // 256)
    actions = {}

    if links:
        grads, (out_ref, g_qkv, g_out, g_up, g_down, total_ref) = rest[:3], rest[3:9]
        parts_ref, made, sums, fixed = rest[9], rest[10], rest[11], rest[12:]
        place = Place()
        runs = []
        sources = [(grads[2], g_down), (grads[1], g_up), (grads[0], g_out)]
        sources += [(made.at[n], g_qkv.at[:, pl.ds(n * width, width)]) for n in range(3)]
        for n, (src, dst) in enumerate(sources):
            runs.append(Scatter(place, src, src.shape[0] // 16, dst, *fixed[9 * n : 9 * n + 9]))
        runs.append(Total(place, sums, True, total_ref, *fixed[9 * len(sources) :]))

        def enter():
            sem, expect = place.barrier()
            pl.semaphore_wait(sem, expect)

        actions[(0, 0)] = [enter]
        order = [(n, which, stage) for which, row in enumerate(BACK_PLAN) for stage, n in enumerate(row)]
        for n, which, stage in sorted(order):
            actions.setdefault(back_point(attends, steps, n), []).append(runs[which].stages()[stage])
    else:
        out_ref, made, total_ref = rest[:3]
        parts_ref, sums = rest[3:]

    def talk(point):
        for (at, where), todo in sorted(actions.items(), key=lambda item: item[0]):
            if where == point:

                def run_all(todo=todo):
                    for action in todo:
                        action()

                pl.when(step == at)(run_all)

    @pl.when(step == 0)
    def _():
        sums[...] = small_ref[...]

    talk(0)

    @pl.when(step < attends)
    def _():
        group = step // per_group
        column = step % per_group
        rows = pl.ds(pl.multiple_of(group * SEQ, SEQ), SEQ)
        logs = log_ref[0, 0].T
        for p in range(PAIRS):
            cols = pl.ds(128 * p, 128)
            done = attend_back_pair(
                q_ref[:, cols],
                k_ref[:, cols],
                v_ref[:, cols],
                grad_ref[:, cols],
                mixed_ref[:, cols],
                logs[:, 2 * p : 2 * p + 2],
            )
            where = pl.ds(pl.multiple_of(column * wide + 128 * p, 128), 128)
            for n in range(3):
                parts_ref[n, rows, where] = done[n]
            if p + 1 < PAIRS:
                talk(1)

    @pl.when((step >= attends) & (step < attends + weights))
    def _():
        part = (step - attends) // (width // 256)
        cols = pl.ds(pl.multiple_of((step - attends) % (width // 256) * 256, 256), 256)
        grad = parts_ref[part, :, cols]
        made[part, :, cols] = mm_ta(inp_ref[...], grad).astype(half)
        column = col_sum(grad.astype(single))

        @pl.when(part == 0)
        def _():
            sums[pl.ds(0, 1), cols] = column

        @pl.when(part == 2)
        def _():
            sums[pl.ds(1, 1), cols] = column

    @pl.when(step >= attends + weights)
    def _():
        block = out_ref.shape[0]
        rows = pl.ds(pl.multiple_of((step - attends - weights) * block, block), block)
        grad = dsum_ref[...]
        for n in range(3):
            grad = grad + mm_tb(parts_ref[n, rows, :], w_ref[:, pl.ds(n * width, width)])
        out_ref[...] = jnp.where(flag_ref[...] > 0, 0.0, grad)

    talk(2)
    if not links:
        total_ref[...] = sums[...]


def back(links, projected, d_mixed, mixed, logs, inputs, w_qkv, d_sum, flags, small, grads):
    count, width = mixed.shape
    groups = count // SEQ
    wide = 128 * PAIRS
    per_group = width // wide
    attends = groups * per_group
    weights = 3 * (width // 256)
    block = 256
    steps = attends + weights + count // block
    last = attends - 1

    def group_of(s):
        return jnp.minimum(s, last) // per_group

    def column_of(s):
        return jnp.minimum(s, last) % per_group

    def late(s):
        return jnp.maximum(s - attends - weights, 0)

    spec = lambda part: pl.BlockSpec((SEQ, wide), lambda s: (group_of(s), part * per_group + column_of(s)))
    whole = lambda shape: pl.BlockSpec(shape, lambda s: (0,) * len(shape), pipeline_mode=pl.Buffered(1))
    anywhere = pl.BlockSpec(memory_space=pl.ANY)
    in_specs = [
        spec(0),
        spec(1),
        spec(2),
        spec(0),
        spec(0),
        pl.BlockSpec((1, 1, 8, SEQ), lambda s: (group_of(s), column_of(s), 0, 0)),
        whole(inputs.shape),
        whole(w_qkv.shape),
        pl.BlockSpec((block, width), lambda s: (late(s), 0)),
        pl.BlockSpec((block, 1), lambda s: (late(s), 0)),
        whole(small.shape),
    ]
    out_specs = [pl.BlockSpec((block, width), lambda s: (late(s), 0))]
    out_shape = [jax.ShapeDtypeStruct((count, width), single)]
    operands = [projected, projected, projected, d_mixed, mixed, logs, inputs, w_qkv, d_sum, flags, small]
    dparts = pltpu.VMEM((3, count, width), half)
    sums = pltpu.VMEM(small.shape, single)
    if links:
        in_specs += [anywhere] * 3
        operands += grads
        shapes = [(width // 16, 3 * width)] + [(g.shape[0] // 16, g.shape[1]) for g in grads] + [small.shape]
        out_specs += [whole(shape) for shape in shapes]
        out_shape += [jax.ShapeDtypeStruct(shape, single) for shape in shapes]
        scratch = [dparts, pltpu.VMEM((3, width, width), half), sums]
        for shape in [grads[2].shape, grads[1].shape, grads[0].shape] + [(width, width)] * 3:
            scratch += Scatter.scratch(shape)
        scratch += Total.scratch(small.shape)
        params = pltpu.CompilerParams(collective_id=2, has_side_effects=True, vmem_limit_bytes=VMEM_LIMIT)
    else:
        out_specs += [whole((3, width, width)), whole(small.shape)]
        out_shape += [jax.ShapeDtypeStruct((3, width, width), half), jax.ShapeDtypeStruct(small.shape, single)]
        scratch = [dparts, sums]
        params = pltpu.CompilerParams(vmem_limit_bytes=VMEM_LIMIT)
    return pl.pallas_call(
        functools.partial(back_body, links, steps),
        grid=(steps,),
        in_specs=in_specs,
        out_specs=out_specs,
        out_shape=out_shape,
        scratch_shapes=scratch,
        compiler_params=params,
        name="back",
    )(*operands)


BACK_PLAN = [
    [0, 4, 13, 22, 29, 34, 36, 36, 37],
    [0, 6, 23, 28, 34, 38, 41, 41, 45],
    [0, 6, 24, 29, 35, 38, 41, 41, 45],
    [27, 29, 33, 35, 37, 39, 41, 41, 45],
    [30, 32, 35, 37, 39, 41, 50, 50, 55],
    [33, 34, 37, 39, 41, 52, 62, 62, 67],
    [33, 35, 37, 39, 42],
]


def back_point(attends, steps, n):
    if n < 2 * attends:
        return n // 2, n % 2
    n -= attends
    return (n, 0) if n < steps else (steps - 1, 2)


def local(chips, twins, tokens, flags, mask_embed, cotangent, w_qkv, b_qv, w_out, b_out, norm_one, w_up, b_up, w_down, b_down, norm_two):
    links = chips == 4 * ZS and twins == 2
    n = b_out.shape[0]
    width = chips * n
    me = lax.axis_index("dp")
    vectors = jnp.stack([b_qv[0], b_qv[1], b_out, norm_one[0], norm_one[1], b_down, norm_two[0], norm_two[1]])
    vectors = lax.dynamic_update_slice(jnp.zeros((8, width), single), vectors, (0, me * n))
    hidden = lax.dynamic_update_slice(jnp.zeros((4 * width,), single), b_up, (me * 4 * n,)).reshape(4, width)
    small = jnp.concatenate([vectors, hidden, jnp.zeros_like(hidden)])
    small = lax.reduce_precision(small, 8, 7)
    shards = [w_qkv, w_out, w_up, w_down]
    flag_col = flags[:, None]
    if links:
        inputs, projected, mixed, logs, vecs, qkv_full, out_full, up_full, down_full = front(
            True, tokens, flag_col, mask_embed[None], small, shards
        )
    else:
        qkv_full, out_full, up_full, down_full = [
            lax.all_gather(s.astype(half), "dp", axis=0, tiled=True) for s in shards
        ]
        small = lax.psum(small, "dp")
        inputs, projected, mixed, logs, vecs = front(False, tokens, flag_col, mask_embed[None], small, [qkv_full])
    activations, d_sum, d_mixed, g_small, g_out, g_up, g_down = middle(
        mixed, inputs, flag_col, cotangent, vecs, out_full, up_full, down_full
    )
    grads = [g_out, g_up, g_down]
    input_grad, g_qkv, *summed = back(
        links, projected, d_mixed, mixed, logs, inputs, qkv_full, d_sum, flag_col, g_small, grads
    )
    if links:
        g_out, g_up, g_down, g_small = summed
    else:
        g_small = summed[0]
        grads = [jnp.concatenate([g_qkv[0], g_qkv[1], g_qkv[2]], axis=1)] + grads
        grads = [lax.psum_scatter(g.astype(single), "dp", scatter_dimension=0, tiled=True) for g in grads]
        g_qkv, g_out, g_up, g_down = [lax.psum(g.astype(half), "rep").astype(single) for g in grads]
        g_small = lax.psum(g_small, ("dp", "rep"))
    rows = lax.dynamic_slice_in_dim(g_small[:8], me * n, n, axis=1)
    g_bup = lax.dynamic_slice_in_dim(g_small[8:12].reshape(4 * width), me * 4 * n, 4 * n)
    return (
        activations,
        input_grad,
        g_qkv,
        rows[0:2],
        g_out,
        rows[2],
        rows[3:5],
        g_up,
        g_bup,
        g_down,
        rows[5],
        rows[6:8],
    )


def solution(mesh):
    rows = P(("dp", "rep"), None)
    first = P("dp", None)
    second = P(None, "dp")
    return jax.shard_map(
        functools.partial(local, mesh.shape["dp"], mesh.shape["rep"]),
        mesh=mesh,
        in_specs=(rows, P(("dp", "rep")), P(), rows, first, second, first, P("dp"), second, first, P("dp"), first, P("dp"), second),
        out_specs=(rows, rows, first, second, first, P("dp"), second, first, P("dp"), first, P("dp"), second),
        check_vma=False,
    )
```

```python
import functools

import jax
import jax.numpy as jnp
from jax import lax
from jax.experimental import pallas as pl
from jax.experimental.pallas import tpu as pltpu
from jax.sharding import PartitionSpec as P

HEADS = 12
SEQ = 512
EPS = 1e-12
half = jnp.bfloat16
single = jnp.float32
VMEM_LIMIT = 61 * 1024 * 1024


def mm(left, right):
    return jnp.dot(left, right, preferred_element_type=single)


def mm_tb(left, right):
    return lax.dot_general(left, right, (((1,), (1,)), ((), ())), preferred_element_type=single)


def mm_ta(left, right):
    return lax.dot_general(left, right, (((0,), (0,)), ((), ())), preferred_element_type=single)


def row_mean(values):
    return jnp.mean(values, axis=-1, keepdims=True)


def col_sum(values):
    return jnp.sum(values, axis=0, keepdims=True)


def head_masks(width):
    lane = lax.broadcasted_iota(jnp.int32, (1, width), 1)
    return [(lane // 64) == h for h in range(width // 64)]


def attend_pair(query, keys, vals):
    scaled = query * half(0.125)
    turned = vals.T
    outs, logs = [], []
    for h, mask in enumerate(head_masks(128)):
        own = jnp.where(mask, keys, half(0))
        scores = mm_tb(own, scaled)
        top = jnp.max(scores, axis=0, keepdims=True)
        expo = jnp.exp(scores - top)
        total = jnp.sum(expo, axis=0, keepdims=True)
        mixed = mm(turned[64 * h : 64 * h + 64], expo.astype(half))
        outs.append(mixed * (1.0 / total))
        logs.append(top + jnp.log(total))
    return jnp.concatenate(outs, axis=0).astype(half).T, logs


def attend_back_pair(query, keys, vals, grad, mixed, logs):
    scaled = query * half(0.125)
    scaled_keys = keys * half(0.125)
    product = grad.astype(single) * mixed.astype(single)
    grad_turned = grad.T
    scaled_turned = scaled.T
    d_vals, d_keys, d_query = [], [], None
    for h, mask in enumerate(head_masks(128)):
        scores = mm_tb(jnp.where(mask, scaled, half(0)), keys)
        probs = jnp.exp(scores - logs[:, h : h + 1])
        d_probs = mm_tb(jnp.where(mask, grad, half(0)), vals)
        delta = jnp.sum(jnp.where(mask, product, 0.0), axis=1, keepdims=True)
        d_scores = (probs * (d_probs - delta)).astype(half)
        rows = slice(64 * h, 64 * h + 64)
        d_vals.append(mm(grad_turned[rows], probs.astype(half)))
        d_keys.append(mm(scaled_turned[rows], d_scores))
        part = mm(d_scores, jnp.where(mask, scaled_keys, half(0)))
        d_query = part if d_query is None else d_query + part
    turn = lambda parts: jnp.concatenate(parts, axis=0).astype(half).T
    return d_query.astype(half), turn(d_keys), turn(d_vals)


def norm(values, gain, shift):
    center = values - row_mean(values)
    inverse = lax.rsqrt(row_mean(center * center) + EPS)
    unit = center * inverse
    return unit * gain + shift, unit, inverse


def norm_back(grad, unit, inverse, gain):
    scaled = grad * gain
    return inverse * (scaled - row_mean(scaled) - unit * row_mean(scaled * unit))


def middle_body(
    mixed_ref,
    inp_ref,
    flag_ref,
    cot_ref,
    vec_ref,
    wo_all,
    wu_all,
    wd_all,
    act_out,
    dsum_out,
    dmix_out,
    small_out,
    gwo_out,
    gwu_out,
    gwd_out,
    wo_ref,
    wu_ref,
    wd_ref,
    unit1,
    scale1,
    low,
    upper_ref,
    acts,
    slope,
    d_low,
    acc_o,
    acc_u,
    acc_d,
    stage,
    sems,
    loads,
):
    step = pl.program_id(0)
    last = pl.num_programs(0) - 1
    width = wo_ref.shape[0]
    chunks = wd_ref.shape[0] // width
    block = low.shape[0]
    total = dsum_out
    parts = [pl.ds(n * (block // SPLIT), block // SPLIT) for n in range(SPLIT)]

    @pl.when(step == 0)
    def _():
        weights = [(wo_all, wo_ref), (wu_all, wu_ref), (wd_all, wd_ref)]
        copies = [pltpu.make_async_copy(src, dst, loads.at[n]) for n, (src, dst) in enumerate(weights)]
        for copy in copies:
            copy.start()
        small_out[...] = jnp.zeros_like(small_out)
        acc_o[...] = jnp.zeros_like(acc_o)
        acc_u[...] = jnp.zeros_like(acc_u)
        acc_d[...] = jnp.zeros_like(acc_d)
        for copy in copies:
            copy.wait()

    vec = lambda row: vec_ref[pl.ds(row, 1), :]
    for rows in parts:
        attended = mm(mixed_ref[rows, :], wo_ref[...]) + vec(2)
        value, unit, inverse = norm(inp_ref[rows, :].astype(single) + attended, vec(3), vec(4))
        unit1[rows, :] = unit
        scale1[rows, :] = inverse
        total[rows, :] = value + vec(5)
        low[rows, :] = value.astype(half)

    def to_upper(j):
        upper_ref[j % 2] = mm(low[...], wu_ref[:, j * width : (j + 1) * width]) + vec(8 + j)

    to_upper(0)
    for j in range(chunks):
        if j + 1 < chunks:
            to_upper(j + 1)
        upper = upper_ref[j % 2]
        scaled = upper * 0.7071067811865476
        phi = 0.5 * (1.0 + lax.erf(scaled))
        acts[j] = (upper * phi).astype(half)
        bell = jnp.exp2(scaled * scaled * -1.4426950408889634)
        slope[j] = (phi + upper * bell * 0.3989422804014327).astype(half)
        total[...] += mm(acts[j], wd_ref[j * width : (j + 1) * width, :])

    for rows in parts:
        value, unit, inv2 = norm(total[rows, :], vec(6), vec(7))
        act_out[rows, :] = value.astype(half)
        out_grad = jnp.where(flag_ref[rows, :] > 0, cot_ref[rows, :].astype(single), 0.0)
        small_out[pl.ds(6, 1), :] += col_sum(out_grad * unit)
        small_out[pl.ds(7, 1), :] += col_sum(out_grad)
        d_second = norm_back(out_grad, unit, inv2, vec(6))
        lowered = d_second.astype(half)
        d_low[rows, :] = lowered
        small_out[pl.ds(5, 1), :] += col_sum(lowered.astype(single))
        total[rows, :] = d_second

    def copy_out(j):
        cols = pl.ds(pl.multiple_of(j * width, width), width)
        return [
            pltpu.make_async_copy(stage.at[0], gwd_out.at[cols, :], sems.at[0]),
            pltpu.make_async_copy(stage.at[1], gwu_out.at[:, cols], sems.at[1]),
        ]

    @pl.loop(0, chunks)
    def _(j):
        cols = pl.ds(pl.multiple_of(j * width, width), width)
        d_acts = mm_tb(d_low[...], wd_ref[cols, :])
        d_upper = (d_acts * slope[j].astype(single)).astype(half)
        small_out[pl.ds(8 + j, 1), :] += col_sum(d_upper.astype(single))
        total[...] += mm_tb(d_upper, wu_ref[:, cols])
        acc_d[j] += mm_ta(acts[j], d_low[...])
        acc_u[j] += mm_ta(low[...], d_upper)

        @pl.when(step == last)
        def _():
            @pl.when(j > 0)
            def _():
                for copy in copy_out(j - 1):
                    copy.wait()

            for n, acc in enumerate((acc_d, acc_u)):
                stage[n] = acc[j].astype(half)
                copy_out(j)[n].start()

    d_first = total[...]
    unit = unit1[...]
    small_out[pl.ds(3, 1), :] += col_sum(d_first * unit)
    small_out[pl.ds(4, 1), :] += col_sum(d_first)
    d_sum = norm_back(d_first, unit, scale1[...], vec(3))
    dsum_out[...] = d_sum
    d_low[...] = d_sum.astype(half)
    small_out[pl.ds(2, 1), :] += col_sum(d_low[...].astype(single))
    dmix_out[...] = mm_tb(d_low[...], wo_ref[...]).astype(half)
    acc_o[...] += mm_ta(mixed_ref[...], d_low[...])

    @pl.when(step == last)
    def _():
        for copy in copy_out(chunks - 1):
            copy.wait()
        stage[0] = acc_o[...].astype(half)
        copy = pltpu.make_async_copy(stage.at[0], gwo_out, sems.at[0])
        copy.start()
        copy.wait()


SPLIT = 2


def middle(mixed, inputs, flags, cotangent, vecs, w_out, w_up, w_down, block=512):
    count, width = mixed.shape
    hidden = w_up.shape[1]
    chunks = hidden // width
    rows = lambda cols: pl.BlockSpec((block, cols), lambda i: (i, 0))
    keep = lambda shape: pl.BlockSpec(shape, lambda i: (0, 0))
    whole = pl.BlockSpec(memory_space=pl.ANY)
    return pl.pallas_call(
        middle_body,
        grid=(count // block,),
        in_specs=[
            rows(width),
            rows(width),
            rows(1),
            rows(width),
            keep((16, width)),
            whole,
            whole,
            whole,
        ],
        out_specs=[
            rows(width),
            rows(width),
            rows(width),
            keep((16, width)),
            whole,
            whole,
            whole,
        ],
        out_shape=[
            jax.ShapeDtypeStruct((count, width), half),
            jax.ShapeDtypeStruct((count, width), single),
            jax.ShapeDtypeStruct((count, width), half),
            jax.ShapeDtypeStruct((16, width), single),
            jax.ShapeDtypeStruct((width, width), half),
            jax.ShapeDtypeStruct((width, hidden), half),
            jax.ShapeDtypeStruct((hidden, width), half),
        ],
        scratch_shapes=[
            pltpu.VMEM((width, width), half),
            pltpu.VMEM((width, hidden), half),
            pltpu.VMEM((hidden, width), half),
            pltpu.VMEM((block, width), single),
            pltpu.VMEM((block, 1), single),
            pltpu.VMEM((block, width), half),
            pltpu.VMEM((2, block, width), single),
            pltpu.VMEM((chunks, block, width), half),
            pltpu.VMEM((chunks, block, width), half),
            pltpu.VMEM((block, width), half),
            pltpu.VMEM((width, width), single),
            pltpu.VMEM((chunks, width, width), single),
            pltpu.VMEM((chunks, width, width), single),
            pltpu.VMEM((2, width, width), half),
            pltpu.SemaphoreType.DMA((2,)),
            pltpu.SemaphoreType.DMA((3,)),
        ],
        compiler_params=pltpu.CompilerParams(vmem_limit_bytes=VMEM_LIMIT),
        name="middle",
    )(mixed, inputs, flags, cotangent, vecs, w_out, w_up, w_down)


MESH = pl.DeviceIdType.MESH
ZS = 4


class Place:
    def __init__(self):
        self.me = lax.axis_index("dp")
        self.core = lax.axis_index("rep")
        self.z = self.me // 4
        self.y = (self.me // 2) % 2
        self.x = self.me % 2
        step_x = 1 - 2 * self.x
        step_y = 2 - 4 * self.y
        self.near = self.me + step_x + self.core * (step_y - step_x)
        self.far = self.me + step_y + self.core * (step_x - step_y)
        self.diag = self.me + step_x + step_y
        self.near_bit = self.x + self.core * (self.y - self.x)
        self.far_bit = self.y + self.core * (self.x - self.y)

    def chip(self, z, far, near):
        return z * 4 + far * (2 - self.core) + near * (1 + self.core)

    def partner(self):
        return (self.me, 1 - self.core)

    def barrier(self):
        sem = pltpu.get_barrier_semaphore()
        tell = lambda dev: pl.semaphore_signal(sem, inc=1, device_id=dev, device_id_type=MESH)
        tell(self.partner())
        tell((self.near, self.core))
        tell((self.far, self.core))

        for k in range(1, ZS):
            tell(((self.me + 4 * k) % (4 * ZS), self.core))
        return sem, 3 + ZS - 1


def send(src, dst, send_sem, recv_sem, dev):
    return pltpu.make_async_remote_copy(
        src_ref=src, dst_ref=dst, send_sem=send_sem, recv_sem=recv_sem, device_id=dev, device_id_type=MESH
    )


OWN, COLUMN, NEAR, FAR, DIAG, END = range(6)


class Gather:
    def __init__(self, place, own, full, rows, offset, cols, sends, recvs, passed):
        self.place, self.own, self.full = place, own, full
        self.rows, self.offset, self.cols = rows, offset, cols
        self.stride = full.shape[1] // 2
        self.sends, self.recvs, self.passed = sends, recvs, passed

    def window(self, h):
        return pl.ds(pl.multiple_of(h * self.stride + self.offset, 128), self.cols)

    def piece(self, q, h):
        return self.full.at[pl.ds(pl.multiple_of(q * self.rows, 16), self.rows), self.window(h)]

    def stage(self, kind, r):
        p = self.place
        yes = p.z >= 0
        up = ((p.me + 4, p.core), p.z < ZS - 1)
        down = ((p.me - 4, p.core), p.z > 0)
        near = ((p.near, p.core), yes)
        far = ((p.far, p.core), yes)
        other = (p.partner(), None)
        if kind == OWN:
            return [(p.me, yes, [up, down, near, far])]
        base = {COLUMN: p.me, NEAR: p.near, FAR: p.far, DIAG: p.diag}[kind]
        ways = [(-4 * r, p.z >= r, up), (4 * r, p.z + r < ZS, down)] if r else [(0, yes, None)]
        onward = {COLUMN: [near, far, other], NEAR: [far, other], FAR: [other], DIAG: [other]}[kind]
        return [(base + shift, there, ([way] if kind == COLUMN else []) + onward) for shift, there, way in ways]

    def copies(self, kind, q, targets):
        p = self.place
        dst = self.piece(q, p.core)
        src = self.own.at[:, self.window(p.core)] if kind == OWN else dst
        made = []
        for n, (dev, cond) in enumerate(targets):
            recv = self.passed.at[q] if cond is None else self.recvs.at[q]
            made.append((send(src, dst, self.sends.at[n, q], recv, dev), cond))
        return made

    def run(self, kind, r):
        if kind == END:
            return self.finish_partner()
        for q, there, targets in self.stage(kind, r):

            def go(q=q, targets=targets):
                if kind != OWN:
                    piece = self.piece(q, self.place.core)
                    send(piece, piece, self.sends.at[0, q], self.recvs.at[q], self.place.partner()).wait_recv()
                for copy, cond in self.copies(kind, q, targets):
                    copy.start() if cond is None else pl.when(cond)(copy.start)

            pl.when(there)(go)

    def finish_sends(self, kind, r):
        if kind == END:
            return
        for q, there, targets in self.stage(kind, r):

            def go(q=q, targets=targets):
                for copy, cond in self.copies(kind, q, targets):
                    copy.wait_send() if cond is None else pl.when(cond)(copy.wait_send)

            pl.when(there)(go)

    def finish_partner(self):
        p = self.place

        @pl.loop(0, 4 * ZS)
        def _(q):
            @pl.when(q != p.me)
            def _():
                piece = self.piece(q, 1 - p.core)
                send(piece, piece, self.sends.at[0, q], self.passed.at[q], p.partner()).wait_recv()


class Scatter:
    def __init__(self, place, grad, rows, out, mine, pair, far, near, low, high, own, got, sems):
        self.place = place
        self.grad, self.rows, self.out = grad, rows, out
        self.mine, self.pair, self.far, self.near, self.low, self.high, self.own, self.got = mine, pair, far, near, low, high, own, got
        self.sems = sems
        self.cols = grad.shape[1] // 2

    LOCAL, PAIR_S, PAIR_R, LAST_S, LAST_R, FAR_S, FAR_R = 0, 1, 2, 3, 4, 8, 16
    NEAR_S, NEAR_R, UP_S, UP_R, DOWN_S, DOWN_R = 24, 28, 32, 36, 40, 44
    COUNT = 48

    def columns(self, h):
        return pl.ds(pl.multiple_of(h * self.cols, 128), self.cols)

    def at(self, ref, q):
        return ref.at[pl.ds(pl.multiple_of(q * self.rows, 16), self.rows), :]

    def load(self, ref, q):
        return ref[pl.ds(pl.multiple_of(q * self.rows, 16), self.rows), :]

    def store(self, ref, q, value):
        ref[pl.ds(pl.multiple_of(q * self.rows, 16), self.rows), :] = value.astype(ref.dtype)

    def copy_local(self):
        return pltpu.make_async_copy(
            self.grad.at[:, self.columns(self.place.core)], self.mine, self.sems.at[self.LOCAL]
        )

    def copy_pair(self):
        p = self.place
        return send(
            self.grad.at[:, self.columns(1 - p.core)],
            self.pair,
            self.sems.at[self.PAIR_S],
            self.sems.at[self.PAIR_R],
            p.partner(),
        )

    def copy_far(self, k):
        p = self.place
        q = p.chip(k // 2, 1 - p.far_bit, k % 2)
        return send(
            self.at(self.mine, q),
            self.at(self.far, k),
            self.sems.at[self.FAR_S + k],
            self.sems.at[self.FAR_R + k],
            (p.far, p.core),
        )

    def copy_near(self, z):
        p = self.place
        return send(
            self.at(self.far, z * 2 + 1 - p.near_bit),
            self.at(self.near, z),
            self.sems.at[self.NEAR_S + z],
            self.sems.at[self.NEAR_R + z],
            (p.near, p.core),
        )

    def copy_up(self, z):
        p = self.place
        return send(
            self.at(self.near, z),
            self.at(self.low, z),
            self.sems.at[self.UP_S + z],
            self.sems.at[self.UP_R + z],
            (p.me + 4, p.core),
        )

    def copy_down(self, z):
        p = self.place
        return send(
            self.at(self.near, z),
            self.at(self.high, z),
            self.sems.at[self.DOWN_S + z],
            self.sems.at[self.DOWN_R + z],
            (p.me - 4, p.core),
        )

    def copy_last(self):
        p = self.place
        return send(
            self.own,
            self.got,
            self.sems.at[self.LAST_S],
            self.sems.at[self.LAST_R],
            p.partner(),
        )

    def start(self):
        self.copy_local().start()
        self.copy_pair().start()

    def to_far(self):
        p = self.place
        self.copy_local().wait()
        self.copy_pair().wait_recv()

        @pl.loop(0, 8)
        def _(k):
            q = p.chip(k // 2, 1 - p.far_bit, k % 2)
            self.store(self.mine, q, self.load(self.mine, q) + self.load(self.pair, q))
            self.copy_far(k).start()

    def to_near(self):
        p = self.place

        def add(k):
            q = p.chip(k // 2, p.far_bit, k % 2)
            self.copy_far(k).wait_recv()
            self.store(
                self.far, k, self.load(self.far, k) + self.load(self.mine, q) + self.load(self.pair, q)
            )

        @pl.loop(0, 4)
        def _(z):
            add(z * 2 + 1 - p.near_bit)
            self.copy_near(z).start()

        @pl.loop(0, 4)
        def _(z):
            add(z * 2 + p.near_bit)

    def to_line(self):
        p = self.place

        @pl.loop(0, 4)
        def _(z):
            self.copy_near(z).wait_recv()
            self.store(self.near, z, self.load(self.near, z) + self.load(self.far, z * 2 + p.near_bit))

        @pl.when(p.z == 0)
        def _():
            for z in (3, 2, 1):
                self.copy_up(z).start()

        @pl.when(p.z == ZS - 1)
        def _():
            for z in (0, 1, 2):
                self.copy_down(z).start()

    def along(self, step):
        p = self.place

        @pl.when(p.z == step)
        def _():
            for z in (3, 2, 1):
                if z >= step:
                    self.copy_up(z).wait_recv()
                if z > step:
                    self.store(self.near, z, self.load(self.near, z) + self.load(self.low, z))
                    self.copy_up(z).start()

        @pl.when(p.z == ZS - 1 - step)
        def _():
            for z in (0, 1, 2):
                if z <= ZS - 1 - step:
                    self.copy_down(z).wait_recv()
                if z < ZS - 1 - step:
                    self.store(self.near, z, self.load(self.near, z) + self.load(self.high, z))
                    self.copy_down(z).start()

    def to_last(self):
        p = self.place
        self.own[...] = self.load(self.near, p.z).astype(single)

        @pl.when(p.z > 0)
        def _():
            self.own[...] += self.load(self.low, p.z).astype(single)

        @pl.when(p.z < ZS - 1)
        def _():
            self.own[...] += self.load(self.high, p.z).astype(single)

        self.copy_last().start()
        self.out[:, self.columns(p.core)] = self.own[...]

    def finish(self):
        p = self.place
        self.copy_pair().wait_send()

        @pl.loop(0, 8)
        def _(k):
            self.copy_far(k).wait_send()

        @pl.loop(0, 4)
        def _(z):
            self.copy_near(z).wait_send()

            @pl.when(z > p.z)
            def _():
                self.copy_up(z).wait_send()

            @pl.when(z < p.z)
            def _():
                self.copy_down(z).wait_send()

        self.copy_last().wait()
        self.out[:, self.columns(1 - p.core)] = self.got[...]

    def stages(self):
        return [
            self.start,
            self.to_far,
            self.to_near,
            self.to_line,
            lambda: self.along(1),
            lambda: self.along(2),
            lambda: self.along(3),
            self.to_last,
            self.finish,
        ]

    @staticmethod
    def scratch(shape):
        total, cols = shape[0], shape[1] // 2
        rows = total // 16
        return [
            pltpu.VMEM((total, cols), half),
            pltpu.VMEM((total, cols), half),
            pltpu.VMEM((8 * rows, cols), half),
            pltpu.VMEM((4 * rows, cols), half),
            pltpu.VMEM((4 * rows, cols), half),
            pltpu.VMEM((4 * rows, cols), half),
            pltpu.VMEM((rows, cols), single),
            pltpu.VMEM((rows, cols), single),
            pltpu.SemaphoreType.DMA((Scatter.COUNT,)),
        ]


class Total:
    COUNT = 12

    def __init__(self, place, start, pair, result, parts, held, sems):
        self.place, self.first, self.pair, self.result = place, start, pair, result
        self.parts, self.held, self.sems = parts, held, sems

    def copy(self, n):
        p = self.place
        if n == 0:
            src, dev = self.first, p.partner()
        elif n <= 3:
            src, dev = self.held.at[0], ((p.me + 4 * n) % (4 * ZS), p.core)
        elif n == 4:
            src, dev = self.held.at[1], (p.near, p.core)
        else:
            src, dev = self.held.at[2], (p.far, p.core)
        return send(src, self.parts.at[n], self.sems.at[n], self.sems.at[6 + n], dev)

    def stages(self):
        def begin():
            if self.pair:
                self.copy(0).start()

        def column():
            value = self.first[...]
            if self.pair:
                self.copy(0).wait_recv()
                value = value + self.parts[0]
            self.held[0] = value
            for n in (1, 2, 3):
                self.copy(n).start()

        def near():
            value = self.held[0]
            for n in (1, 2, 3):
                self.copy(n).wait_recv()
                value = value + self.parts[n]
            self.held[1] = value
            self.copy(4).start()

        def far():
            self.copy(4).wait_recv()
            self.held[2] = self.held[1] + self.parts[4]
            self.copy(5).start()

        def finish():
            self.copy(5).wait_recv()
            self.result[...] = self.held[2] + self.parts[5]
            for n in range(0 if self.pair else 1, 6):
                self.copy(n).wait_send()

        return [begin, column, near, far, finish]

    @staticmethod
    def scratch(shape):
        return [
            pltpu.VMEM((6,) + shape, single),
            pltpu.VMEM((3,) + shape, single),
            pltpu.SemaphoreType.DMA((Total.COUNT,)),
        ]


PAIRS = 2


FRONT_PLAN = [
    (-1, 0, 0, 0), (-1, 1, 0, 0), (-1, 0, 2, 0), (-1, 0, 3, 0), (-1, 0, 1, 1), (-1, 1, 2, 0),
    (-1, 1, 3, 0), (-1, 1, 1, 1), (-1, 0, 4, 0), (-1, 0, 1, 2), (-1, 1, 1, 2), (-1, 0, 2, 1),
    (-1, 0, 3, 1), (-1, 1, 4, 0), (-1, 1, 2, 1), (-1, 0, 1, 3), (-1, 0, 2, 2), (-1, 1, 1, 3),
    (-1, 1, 3, 1), (-1, 1, 2, 2), (-1, 0, 3, 2), (-1, 1, 3, 2), (-1, 0, 2, 3), (-1, 0, 3, 3),
    (-1, 0, 4, 1), (-1, 1, 2, 3), (-1, 2, 0, 0), (-1, 3, 0, 0), (-1, 4, 0, 0), (-1, 1, 4, 1),
    (-1, 1, 3, 3), (-1, 0, 4, 2), (-1, 1, 4, 2), (-1, 0, 4, 3), (-1, 1, 4, 3), (-1, 2, 2, 0),
    (-1, 2, 1, 1), (-1, 0, 5, 0), (-1, 2, 3, 0), (-1, 1, 5, 0), (1, 3, 2, 0), (1, 3, 3, 0),
    (1, 3, 1, 1), (3, 4, 2, 0), (3, 4, 1, 1), (3, 2, 1, 2), (3, 4, 3, 0), (4, 2, 4, 0),
    (4, 2, 2, 1), (5, 2, 3, 1), (6, 3, 1, 2), (7, 3, 4, 0), (8, 2, 1, 3), (8, 3, 2, 1),
    (8, 4, 1, 2), (10, 3, 1, 3), (11, 2, 2, 3), (11, 3, 3, 1), (13, 2, 2, 2), (13, 4, 4, 0),
    (13, 4, 2, 1), (13, 4, 1, 3), (15, 3, 2, 2), (15, 3, 2, 3), (16, 2, 3, 3), (17, 2, 3, 2),
    (17, 4, 3, 1), (17, 4, 2, 2), (17, 4, 2, 3), (18, 2, 4, 1), (19, 3, 3, 2), (20, 3, 3, 3),
    (21, 2, 4, 3), (21, 3, 4, 1), (22, 2, 4, 2), (22, 4, 3, 2), (22, 4, 3, 3), (24, 2, 5, 0),
    (24, 4, 4, 1), (25, 3, 4, 3), (26, 3, 4, 2), (27, 4, 4, 2), (27, 4, 4, 3), (28, 3, 5, 0),
    (31, 4, 5, 0),
]
SMALL_AT = (0, 8, 14, 23)


def front_body(links, *refs):
    tok_ref, flag_ref, mask_ref, small_ref = refs[:4]
    step = pl.program_id(0)
    count = pl.num_programs(0)
    per_group = 1 + HEADS // (2 * PAIRS)
    actions = {}
    if links:
        shards, (inp_ref, proj_ref, mixed_ref, log_ref, vec_ref) = refs[4:8], refs[8:13]
        fulls, w_ref, own, rest = refs[13:17], refs[17], refs[18:21], refs[21:]
        place = Place()
        local = rest[0]
        sets = [rest[1 + 3 * n : 4 + 3 * n] for n in range(5)]
        total = Total(place, small_ref, False, vec_ref, *rest[16:19])
        rows = [shard.shape[0] for shard in shards]
        mine = pl.ds(pl.multiple_of(place.me * rows[0], 16), rows[0])
        cut = w_ref.shape[1] // 2
        first = cut // 2 // 128 * 128 + 128
        parts = [
            Gather(place, w_ref.at[mine], w_ref, rows[0], 0, first, *sets[0]),
            Gather(place, w_ref.at[mine], w_ref, rows[0], first, cut - first, *sets[1]),
        ]
        parts += [Gather(place, own[t], fulls[t + 1], rows[t + 1], 0, fulls[t + 1].shape[1] // 2, *sets[t + 2]) for t in range(3)]
        keep = pltpu.make_async_copy(w_ref, fulls[0], local.at[0])
        mine_to = [
            pltpu.make_async_copy(
                own[t], fulls[t + 1].at[pl.ds(pl.multiple_of(place.me * rows[t + 1], 16), rows[t + 1]), :], local.at[t + 1]
            )
            for t in range(3)
        ]

        def enter():
            sem, expect = place.barrier()
            w_ref[mine, :] = shards[0][...].astype(half)
            for t in range(3):
                own[t][...] = shards[t + 1][...].astype(half)
            pl.semaphore_wait(sem, expect)
            for copy in mine_to:
                copy.start()

        stages = total.stages()
        todo = [(-1, enter), (-1, stages[1])]
        seen = 0
        for n, part, kind, r in FRONT_PLAN:
            if seen in SMALL_AT[1:]:
                todo.append((-1, stages[1 + SMALL_AT.index(seen)]))
            todo.append((n, functools.partial(parts[part].run, kind, r)))
            seen += 1
        todo.append((0, keep.start))

        def leave():
            keep.wait()
            for copy in mine_to:
                copy.wait()
            for _, part, kind, r in FRONT_PLAN:
                parts[part].finish_sends(kind, r)

        for n, action in sorted(todo, key=lambda item: item[0]):
            actions.setdefault(front_point(per_group, n), []).append(action)
        actions.setdefault((4 * per_group - 1, 2), []).append(leave)
    else:
        w_ref, (inp_ref, proj_ref, mixed_ref, log_ref, vec_ref) = refs[4], refs[5:]
        vec_ref[...] = small_ref[...]

    def talk(point):
        for (at, where), todo in sorted(actions.items(), key=lambda item: item[0]):
            if where == point:

                def run_all(todo=todo):
                    for action in todo:
                        action()

                pl.when(step == at)(run_all)

    talk(0)
    column = step % per_group - 1
    wide = 128 * PAIRS
    width = inp_ref.shape[1]

    @pl.when(column < 0)
    def _():
        masked = flag_ref[...] > 0
        low = jnp.where(masked, mask_ref[...].astype(single), tok_ref[...].astype(single)).astype(half)
        inp_ref[...] = low
        for n in range(3):
            cols = pl.ds(n * width, width)
            value = mm(low, w_ref[:, cols])
            if n != 1:
                value = value + vec_ref[pl.ds(n // 2, 1), :]
            proj_ref[:, cols] = value.astype(half)

    @pl.when(column >= 0)
    def _():
        for p in range(PAIRS):
            start = column * wide + 128 * p
            q, k, v = (proj_ref[:, pl.ds(pl.multiple_of(start + n * width, 128), 128)] for n in range(3))
            mixed, logs = attend_pair(q, k, v)
            mixed_ref[:, pl.ds(128 * p, 128)] = mixed
            for h in range(2):
                log_ref[0, 0, pl.ds(2 * p + h, 1), :] = logs[h]
            if p + 1 < PAIRS:
                talk(1)

    talk(2)


def front_point(per_group, n):
    points = 1 + (per_group - 1) * PAIRS
    if n < 0:
        return (0, 0)
    if n >= 4 * points:
        return (4 * per_group - 1, 2)
    group, n = n // points, n % points
    if n == 0:
        return (group * per_group, 0)
    return (group * per_group + 1 + (n - 1) // PAIRS, (n - 1) % PAIRS)


def front(links, tokens, flags, mask_embed, small, shards):
    count, width = tokens.shape
    groups = count // SEQ
    wide = 128 * PAIRS
    steps = width // wide
    per_group = steps + 1
    group = lambda cols: pl.BlockSpec((SEQ, cols), lambda s: (s // per_group, 0))
    whole = lambda shape: pl.BlockSpec(shape, lambda s: (0,) * len(shape), pipeline_mode=pl.Buffered(1))
    column = lambda s: jnp.maximum(s % per_group - 1, 0)
    anywhere = pl.BlockSpec(memory_space=pl.ANY)
    in_specs = [group(width), group(1), whole((1, width)), whole(small.shape)] + [whole(s.shape) for s in shards]
    out_specs = [
        group(width),
        group(3 * width),
        pl.BlockSpec((SEQ, wide), lambda s: (s // per_group, column(s))),
        pl.BlockSpec((1, 1, 8, SEQ), lambda s: (s // per_group, column(s), 0, 0)),
        whole(small.shape),
    ]
    out_shape = [
        jax.ShapeDtypeStruct((count, width), half),
        jax.ShapeDtypeStruct((count, 3 * width), half),
        jax.ShapeDtypeStruct((count, width), half),
        jax.ShapeDtypeStruct((groups, steps, 8, SEQ), single),
        jax.ShapeDtypeStruct(small.shape, single),
    ]
    scratch = []
    params = pltpu.CompilerParams(vmem_limit_bytes=VMEM_LIMIT)
    if links:
        full = [(4 * ZS * s.shape[0], s.shape[1]) for s in shards]
        out_specs += [anywhere] * 4
        out_shape += [jax.ShapeDtypeStruct(shape, half) for shape in full]
        scratch += [pltpu.VMEM(full[0], half)] + [pltpu.VMEM(s.shape, half) for s in shards[1:]]
        scratch.append(pltpu.SemaphoreType.DMA((4,)))
        for _ in range(5):
            scratch += [pltpu.SemaphoreType.DMA((4, 4 * ZS))] + [pltpu.SemaphoreType.DMA((4 * ZS,))] * 2
        scratch += Total.scratch(small.shape)
        params = pltpu.CompilerParams(collective_id=1, has_side_effects=True, vmem_limit_bytes=VMEM_LIMIT)
    return pl.pallas_call(
        functools.partial(front_body, links),
        grid=(groups * per_group,),
        in_specs=in_specs,
        out_specs=out_specs,
        out_shape=out_shape,
        scratch_shapes=scratch,
        compiler_params=params,
        name="front",
    )(tokens, flags, mask_embed, small, *shards)


def back_body(links, steps, *refs):
    q_ref, k_ref, v_ref, grad_ref, mixed_ref, log_ref, inp_ref, w_ref, dsum_ref, flag_ref, small_ref = refs[:11]
    rest = refs[11:]
    step = pl.program_id(0)
    width = inp_ref.shape[1]
    count = inp_ref.shape[0]
    wide = 128 * PAIRS
    per_group = width // wide
    attends = (count // SEQ) * per_group
    weights = 3 * (width // 256)
    actions = {}

    if links:
        grads, (out_ref, g_qkv, g_out, g_up, g_down, total_ref) = rest[:3], rest[3:9]
        parts_ref, made, sums, fixed = rest[9], rest[10], rest[11], rest[12:]
        place = Place()
        runs = []
        sources = [(grads[2], g_down), (grads[1], g_up), (grads[0], g_out)]
        sources += [(made.at[n], g_qkv.at[:, pl.ds(n * width, width)]) for n in range(3)]
        for n, (src, dst) in enumerate(sources):
            runs.append(Scatter(place, src, src.shape[0] // 16, dst, *fixed[9 * n : 9 * n + 9]))
        runs.append(Total(place, sums, True, total_ref, *fixed[9 * len(sources) :]))

        def enter():
            sem, expect = place.barrier()
            pl.semaphore_wait(sem, expect)

        actions[(0, 0)] = [enter]
        order = [(n, which, stage) for which, row in enumerate(BACK_PLAN) for stage, n in enumerate(row)]
        for n, which, stage in sorted(order):
            actions.setdefault(back_point(attends, steps, n), []).append(runs[which].stages()[stage])
    else:
        out_ref, made, total_ref = rest[:3]
        parts_ref, sums = rest[3:]

    def talk(point):
        for (at, where), todo in sorted(actions.items(), key=lambda item: item[0]):
            if where == point:

                def run_all(todo=todo):
                    for action in todo:
                        action()

                pl.when(step == at)(run_all)

    @pl.when(step == 0)
    def _():
        sums[...] = small_ref[...]

    talk(0)

    @pl.when(step < attends)
    def _():
        group = step // per_group
        column = step % per_group
        rows = pl.ds(pl.multiple_of(group * SEQ, SEQ), SEQ)
        logs = log_ref[0, 0].T
        for p in range(PAIRS):
            cols = pl.ds(128 * p, 128)
            done = attend_back_pair(
                q_ref[:, cols],
                k_ref[:, cols],
                v_ref[:, cols],
                grad_ref[:, cols],
                mixed_ref[:, cols],
                logs[:, 2 * p : 2 * p + 2],
            )
            where = pl.ds(pl.multiple_of(column * wide + 128 * p, 128), 128)
            for n in range(3):
                parts_ref[n, rows, where] = done[n]
            if p + 1 < PAIRS:
                talk(1)

    @pl.when((step >= attends) & (step < attends + weights))
    def _():
        part = (step - attends) // (width // 256)
        cols = pl.ds(pl.multiple_of((step - attends) % (width // 256) * 256, 256), 256)
        grad = parts_ref[part, :, cols]
        made[part, :, cols] = mm_ta(inp_ref[...], grad).astype(half)
        column = col_sum(grad.astype(single))

        @pl.when(part == 0)
        def _():
            sums[pl.ds(0, 1), cols] = column

        @pl.when(part == 2)
        def _():
            sums[pl.ds(1, 1), cols] = column

    @pl.when(step >= attends + weights)
    def _():
        block = out_ref.shape[0]
        rows = pl.ds(pl.multiple_of((step - attends - weights) * block, block), block)
        grad = dsum_ref[...]
        for n in range(3):
            grad = grad + mm_tb(parts_ref[n, rows, :], w_ref[:, pl.ds(n * width, width)])
        out_ref[...] = jnp.where(flag_ref[...] > 0, 0.0, grad)

    talk(2)
    if not links:
        total_ref[...] = sums[...]


def back(links, projected, d_mixed, mixed, logs, inputs, w_qkv, d_sum, flags, small, grads):
    count, width = mixed.shape
    groups = count // SEQ
    wide = 128 * PAIRS
    per_group = width // wide
    attends = groups * per_group
    weights = 3 * (width // 256)
    block = 256
    steps = attends + weights + count // block
    last = attends - 1

    def group_of(s):
        return jnp.minimum(s, last) // per_group

    def column_of(s):
        return jnp.minimum(s, last) % per_group

    def late(s):
        return jnp.maximum(s - attends - weights, 0)

    spec = lambda part: pl.BlockSpec((SEQ, wide), lambda s: (group_of(s), part * per_group + column_of(s)))
    whole = lambda shape: pl.BlockSpec(shape, lambda s: (0,) * len(shape), pipeline_mode=pl.Buffered(1))
    anywhere = pl.BlockSpec(memory_space=pl.ANY)
    in_specs = [
        spec(0),
        spec(1),
        spec(2),
        spec(0),
        spec(0),
        pl.BlockSpec((1, 1, 8, SEQ), lambda s: (group_of(s), column_of(s), 0, 0)),
        whole(inputs.shape),
        whole(w_qkv.shape),
        pl.BlockSpec((block, width), lambda s: (late(s), 0)),
        pl.BlockSpec((block, 1), lambda s: (late(s), 0)),
        whole(small.shape),
    ]
    out_specs = [pl.BlockSpec((block, width), lambda s: (late(s), 0))]
    out_shape = [jax.ShapeDtypeStruct((count, width), single)]
    operands = [projected, projected, projected, d_mixed, mixed, logs, inputs, w_qkv, d_sum, flags, small]
    dparts = pltpu.VMEM((3, count, width), half)
    sums = pltpu.VMEM(small.shape, single)
    if links:
        in_specs += [anywhere] * 3
        operands += grads
        shapes = [(width // 16, 3 * width)] + [(g.shape[0] // 16, g.shape[1]) for g in grads] + [small.shape]
        out_specs += [whole(shape) for shape in shapes]
        out_shape += [jax.ShapeDtypeStruct(shape, single) for shape in shapes]
        scratch = [dparts, pltpu.VMEM((3, width, width), half), sums]
        for shape in [grads[2].shape, grads[1].shape, grads[0].shape] + [(width, width)] * 3:
            scratch += Scatter.scratch(shape)
        scratch += Total.scratch(small.shape)
        params = pltpu.CompilerParams(collective_id=2, has_side_effects=True, vmem_limit_bytes=VMEM_LIMIT)
    else:
        out_specs += [whole((3, width, width)), whole(small.shape)]
        out_shape += [jax.ShapeDtypeStruct((3, width, width), half), jax.ShapeDtypeStruct(small.shape, single)]
        scratch = [dparts, sums]
        params = pltpu.CompilerParams(vmem_limit_bytes=VMEM_LIMIT)
    return pl.pallas_call(
        functools.partial(back_body, links, steps),
        grid=(steps,),
        in_specs=in_specs,
        out_specs=out_specs,
        out_shape=out_shape,
        scratch_shapes=scratch,
        compiler_params=params,
        name="back",
    )(*operands)


BACK_PLAN = [
    [0, 4, 13, 22, 29, 34, 36, 36, 37],
    [0, 6, 23, 28, 34, 38, 41, 41, 45],
    [0, 6, 24, 29, 35, 38, 41, 41, 45],
    [27, 29, 33, 35, 37, 39, 41, 41, 45],
    [30, 32, 35, 37, 39, 41, 50, 50, 55],
    [33, 34, 37, 39, 41, 52, 62, 62, 67],
    [33, 35, 37, 39, 42],
]


def back_point(attends, steps, n):
    if n < 2 * attends:
        return n // 2, n % 2
    n -= attends
    return (n, 0) if n < steps else (steps - 1, 2)


def local(chips, twins, tokens, flags, mask_embed, cotangent, w_qkv, b_qv, w_out, b_out, norm_one, w_up, b_up, w_down, b_down, norm_two):
    links = chips == 4 * ZS and twins == 2
    n = b_out.shape[0]
    width = chips * n
    me = lax.axis_index("dp")
    vectors = jnp.stack([b_qv[0], b_qv[1], b_out, norm_one[0], norm_one[1], b_down, norm_two[0], norm_two[1]])
    vectors = lax.dynamic_update_slice(jnp.zeros((8, width), single), vectors, (0, me * n))
    hidden = lax.dynamic_update_slice(jnp.zeros((4 * width,), single), b_up, (me * 4 * n,)).reshape(4, width)
    small = jnp.concatenate([vectors, hidden, jnp.zeros_like(hidden)])
    small = lax.reduce_precision(small, 8, 7)
    shards = [w_qkv, w_out, w_up, w_down]
    flag_col = flags[:, None]
    if links:
        inputs, projected, mixed, logs, vecs, qkv_full, out_full, up_full, down_full = front(
            True, tokens, flag_col, mask_embed[None], small, shards
        )
    else:
        qkv_full, out_full, up_full, down_full = [
            lax.all_gather(s.astype(half), "dp", axis=0, tiled=True) for s in shards
        ]
        small = lax.psum(small, "dp")
        inputs, projected, mixed, logs, vecs = front(False, tokens, flag_col, mask_embed[None], small, [qkv_full])
    activations, d_sum, d_mixed, g_small, g_out, g_up, g_down = middle(
        mixed, inputs, flag_col, cotangent, vecs, out_full, up_full, down_full
    )
    grads = [g_out, g_up, g_down]
    input_grad, g_qkv, *summed = back(
        links, projected, d_mixed, mixed, logs, inputs, qkv_full, d_sum, flag_col, g_small, grads
    )
    if links:
        g_out, g_up, g_down, g_small = summed
    else:
        g_small = summed[0]
        grads = [jnp.concatenate([g_qkv[0], g_qkv[1], g_qkv[2]], axis=1)] + grads
        grads = [lax.psum_scatter(g.astype(single), "dp", scatter_dimension=0, tiled=True) for g in grads]
        g_qkv, g_out, g_up, g_down = [lax.psum(g.astype(half), "rep").astype(single) for g in grads]
        g_small = lax.psum(g_small, ("dp", "rep"))
    rows = lax.dynamic_slice_in_dim(g_small[:8], me * n, n, axis=1)
    g_bup = lax.dynamic_slice_in_dim(g_small[8:12].reshape(4 * width), me * 4 * n, 4 * n)
    return (
        activations,
        input_grad,
        g_qkv,
        rows[0:2],
        g_out,
        rows[2],
        rows[3:5],
        g_up,
        g_bup,
        g_down,
        rows[5],
        rows[6:8],
    )


def solution(mesh):
    rows = P(("dp", "rep"), None)
    first = P("dp", None)
    second = P(None, "dp")
    return jax.shard_map(
        functools.partial(local, mesh.shape["dp"], mesh.shape["rep"]),
        mesh=mesh,
        in_specs=(rows, P(("dp", "rep")), P(), rows, first, second, first, P("dp"), second, first, P("dp"), first, P("dp"), second),
        out_specs=(rows, rows, first, second, first, P("dp"), second, first, P("dp"), first, P("dp"), second),
        check_vma=False,
    )
```

```python
import functools

import jax
import jax.numpy as jnp
from jax import lax
from jax.experimental import pallas as pl
from jax.experimental.pallas import tpu as pltpu
from jax.sharding import PartitionSpec as P

HEADS = 12
SEQ = 512
EPS = 1e-12
half = jnp.bfloat16
single = jnp.float32
VMEM_LIMIT = 61 * 1024 * 1024


def mm(left, right):
    return jnp.dot(left, right, preferred_element_type=single)


def mm_tb(left, right):
    return lax.dot_general(left, right, (((1,), (1,)), ((), ())), preferred_element_type=single)


def mm_ta(left, right):
    return lax.dot_general(left, right, (((0,), (0,)), ((), ())), preferred_element_type=single)


def row_mean(values):
    return jnp.mean(values, axis=-1, keepdims=True)


def col_sum(values):
    return jnp.sum(values, axis=0, keepdims=True)


def head_masks(width):
    lane = lax.broadcasted_iota(jnp.int32, (1, width), 1)
    return [(lane // 64) == h for h in range(width // 64)]


def attend_pair(query, keys, vals):
    scaled = query * half(0.125)
    turned = vals.T
    outs, logs = [], []
    for h, mask in enumerate(head_masks(128)):
        own = jnp.where(mask, keys, half(0))
        scores = mm_tb(own, scaled)
        top = jnp.max(scores, axis=0, keepdims=True)
        expo = jnp.exp(scores - top)
        total = jnp.sum(expo, axis=0, keepdims=True)
        mixed = mm(turned[64 * h : 64 * h + 64], expo.astype(half))
        outs.append(mixed * (1.0 / total))
        logs.append(top + jnp.log(total))
    return jnp.concatenate(outs, axis=0).astype(half).T, logs


def attend_back_pair(query, keys, vals, grad, mixed, logs):
    scaled = query * half(0.125)
    scaled_keys = keys * half(0.125)
    product = grad.astype(single) * mixed.astype(single)
    grad_turned = grad.T
    scaled_turned = scaled.T
    d_vals, d_keys, d_query = [], [], None
    for h, mask in enumerate(head_masks(128)):
        scores = mm_tb(jnp.where(mask, scaled, half(0)), keys)
        probs = jnp.exp(scores - logs[:, h : h + 1])
        d_probs = mm_tb(jnp.where(mask, grad, half(0)), vals)
        delta = jnp.sum(jnp.where(mask, product, 0.0), axis=1, keepdims=True)
        d_scores = (probs * (d_probs - delta)).astype(half)
        rows = slice(64 * h, 64 * h + 64)
        d_vals.append(mm(grad_turned[rows], probs.astype(half)))
        d_keys.append(mm(scaled_turned[rows], d_scores))
        part = mm(d_scores, jnp.where(mask, scaled_keys, half(0)))
        d_query = part if d_query is None else d_query + part
    turn = lambda parts: jnp.concatenate(parts, axis=0).astype(half).T
    return d_query.astype(half), turn(d_keys), turn(d_vals)


def norm(values, gain, shift):
    center = values - row_mean(values)
    inverse = lax.rsqrt(row_mean(center * center) + EPS)
    unit = center * inverse
    return unit * gain + shift, unit, inverse


def norm_back(grad, unit, inverse, gain):
    scaled = grad * gain
    return inverse * (scaled - row_mean(scaled) - unit * row_mean(scaled * unit))


def middle_body(
    mixed_ref,
    inp_ref,
    flag_ref,
    cot_ref,
    vec_ref,
    wo_all,
    wu_all,
    wd_all,
    act_out,
    dsum_out,
    dmix_out,
    small_out,
    gwo_out,
    gwu_out,
    gwd_out,
    wo_ref,
    wu_ref,
    wd_ref,
    unit1,
    scale1,
    low,
    upper_ref,
    acts,
    slope,
    d_low,
    acc_o,
    acc_u,
    acc_d,
    stage,
    sems,
    loads,
):
    step = pl.program_id(0)
    last = pl.num_programs(0) - 1
    width = wo_ref.shape[0]
    chunks = wd_ref.shape[0] // width
    block = low.shape[0]
    total = dsum_out
    parts = [pl.ds(n * (block // SPLIT), block // SPLIT) for n in range(SPLIT)]

    @pl.when(step == 0)
    def _():
        weights = [(wo_all, wo_ref), (wu_all, wu_ref), (wd_all, wd_ref)]
        copies = [pltpu.make_async_copy(src, dst, loads.at[n]) for n, (src, dst) in enumerate(weights)]
        for copy in copies:
            copy.start()
        small_out[...] = jnp.zeros_like(small_out)
        acc_o[...] = jnp.zeros_like(acc_o)
        acc_u[...] = jnp.zeros_like(acc_u)
        acc_d[...] = jnp.zeros_like(acc_d)
        for copy in copies:
            copy.wait()

    vec = lambda row: vec_ref[pl.ds(row, 1), :]
    for rows in parts:
        attended = mm(mixed_ref[rows, :], wo_ref[...]) + vec(2)
        value, unit, inverse = norm(inp_ref[rows, :].astype(single) + attended, vec(3), vec(4))
        unit1[rows, :] = unit
        scale1[rows, :] = inverse
        total[rows, :] = value + vec(5)
        low[rows, :] = value.astype(half)

    def to_upper(j):
        upper_ref[j % 2] = mm(low[...], wu_ref[:, j * width : (j + 1) * width]) + vec(8 + j)

    to_upper(0)
    for j in range(chunks):
        if j + 1 < chunks:
            to_upper(j + 1)
        upper = upper_ref[j % 2]
        scaled = upper * 0.7071067811865476
        phi = 0.5 * (1.0 + lax.erf(scaled))
        acts[j] = (upper * phi).astype(half)
        bell = jnp.exp2(scaled * scaled * -1.4426950408889634)
        slope[j] = (phi + upper * bell * 0.3989422804014327).astype(half)
        total[...] += mm(acts[j], wd_ref[j * width : (j + 1) * width, :])

    for rows in parts:
        value, unit, inv2 = norm(total[rows, :], vec(6), vec(7))
        act_out[rows, :] = value.astype(half)
        out_grad = jnp.where(flag_ref[rows, :] > 0, cot_ref[rows, :].astype(single), 0.0)
        small_out[pl.ds(6, 1), :] += col_sum(out_grad * unit)
        small_out[pl.ds(7, 1), :] += col_sum(out_grad)
        d_second = norm_back(out_grad, unit, inv2, vec(6))
        lowered = d_second.astype(half)
        d_low[rows, :] = lowered
        small_out[pl.ds(5, 1), :] += col_sum(lowered.astype(single))
        total[rows, :] = d_second

    def copy_out(j):
        cols = pl.ds(pl.multiple_of(j * width, width), width)
        return [
            pltpu.make_async_copy(stage.at[0], gwd_out.at[cols, :], sems.at[0]),
            pltpu.make_async_copy(stage.at[1], gwu_out.at[:, cols], sems.at[1]),
        ]

    @pl.loop(0, chunks)
    def _(j):
        cols = pl.ds(pl.multiple_of(j * width, width), width)
        d_acts = mm_tb(d_low[...], wd_ref[cols, :])
        d_upper = (d_acts * slope[j].astype(single)).astype(half)
        small_out[pl.ds(8 + j, 1), :] += col_sum(d_upper.astype(single))
        total[...] += mm_tb(d_upper, wu_ref[:, cols])
        acc_d[j] += mm_ta(acts[j], d_low[...])
        acc_u[j] += mm_ta(low[...], d_upper)

        @pl.when(step == last)
        def _():
            @pl.when(j > 0)
            def _():
                for copy in copy_out(j - 1):
                    copy.wait()

            for n, acc in enumerate((acc_d, acc_u)):
                stage[n] = acc[j].astype(half)
                copy_out(j)[n].start()

    d_first = total[...]
    unit = unit1[...]
    small_out[pl.ds(3, 1), :] += col_sum(d_first * unit)
    small_out[pl.ds(4, 1), :] += col_sum(d_first)
    d_sum = norm_back(d_first, unit, scale1[...], vec(3))
    dsum_out[...] = d_sum
    d_low[...] = d_sum.astype(half)
    small_out[pl.ds(2, 1), :] += col_sum(d_low[...].astype(single))
    dmix_out[...] = mm_tb(d_low[...], wo_ref[...]).astype(half)
    acc_o[...] += mm_ta(mixed_ref[...], d_low[...])

    @pl.when(step == last)
    def _():
        for copy in copy_out(chunks - 1):
            copy.wait()
        stage[0] = acc_o[...].astype(half)
        copy = pltpu.make_async_copy(stage.at[0], gwo_out, sems.at[0])
        copy.start()
        copy.wait()


SPLIT = 2


def middle(mixed, inputs, flags, cotangent, vecs, w_out, w_up, w_down, block=512):
    count, width = mixed.shape
    hidden = w_up.shape[1]
    chunks = hidden // width
    rows = lambda cols: pl.BlockSpec((block, cols), lambda i: (i, 0))
    keep = lambda shape: pl.BlockSpec(shape, lambda i: (0, 0))
    whole = pl.BlockSpec(memory_space=pl.ANY)
    return pl.pallas_call(
        middle_body,
        grid=(count // block,),
        in_specs=[
            rows(width),
            rows(width),
            rows(1),
            rows(width),
            keep((16, width)),
            whole,
            whole,
            whole,
        ],
        out_specs=[
            rows(width),
            rows(width),
            rows(width),
            keep((16, width)),
            whole,
            whole,
            whole,
        ],
        out_shape=[
            jax.ShapeDtypeStruct((count, width), half),
            jax.ShapeDtypeStruct((count, width), single),
            jax.ShapeDtypeStruct((count, width), half),
            jax.ShapeDtypeStruct((16, width), single),
            jax.ShapeDtypeStruct((width, width), half),
            jax.ShapeDtypeStruct((width, hidden), half),
            jax.ShapeDtypeStruct((hidden, width), half),
        ],
        scratch_shapes=[
            pltpu.VMEM((width, width), half),
            pltpu.VMEM((width, hidden), half),
            pltpu.VMEM((hidden, width), half),
            pltpu.VMEM((block, width), single),
            pltpu.VMEM((block, 1), single),
            pltpu.VMEM((block, width), half),
            pltpu.VMEM((2, block, width), single),
            pltpu.VMEM((chunks, block, width), half),
            pltpu.VMEM((chunks, block, width), half),
            pltpu.VMEM((block, width), half),
            pltpu.VMEM((width, width), single),
            pltpu.VMEM((chunks, width, width), single),
            pltpu.VMEM((chunks, width, width), single),
            pltpu.VMEM((2, width, width), half),
            pltpu.SemaphoreType.DMA((2,)),
            pltpu.SemaphoreType.DMA((3,)),
        ],
        compiler_params=pltpu.CompilerParams(vmem_limit_bytes=VMEM_LIMIT),
        name="middle",
    )(mixed, inputs, flags, cotangent, vecs, w_out, w_up, w_down)


MESH = pl.DeviceIdType.MESH
ZS = 4


class Place:
    def __init__(self):
        self.me = lax.axis_index("dp")
        self.core = lax.axis_index("rep")
        self.z = self.me // 4
        self.y = (self.me // 2) % 2
        self.x = self.me % 2
        step_x = 1 - 2 * self.x
        step_y = 2 - 4 * self.y
        self.near = self.me + step_x + self.core * (step_y - step_x)
        self.far = self.me + step_y + self.core * (step_x - step_y)
        self.diag = self.me + step_x + step_y
        self.near_bit = self.x + self.core * (self.y - self.x)
        self.far_bit = self.y + self.core * (self.x - self.y)

    def chip(self, z, far, near):
        return z * 4 + far * (2 - self.core) + near * (1 + self.core)

    def partner(self):
        return (self.me, 1 - self.core)

    def barrier(self):
        sem = pltpu.get_barrier_semaphore()
        tell = lambda dev: pl.semaphore_signal(sem, inc=1, device_id=dev, device_id_type=MESH)
        tell(self.partner())
        tell((self.near, self.core))
        tell((self.far, self.core))

        for k in range(1, ZS):
            tell(((self.me + 4 * k) % (4 * ZS), self.core))
        return sem, 3 + ZS - 1


def send(src, dst, send_sem, recv_sem, dev):
    return pltpu.make_async_remote_copy(
        src_ref=src, dst_ref=dst, send_sem=send_sem, recv_sem=recv_sem, device_id=dev, device_id_type=MESH
    )


OWN, COLUMN, NEAR, FAR, DIAG, END = range(6)


class Gather:
    def __init__(self, place, own, full, rows, offset, cols, sends, recvs, passed):
        self.place, self.own, self.full = place, own, full
        self.rows, self.offset, self.cols = rows, offset, cols
        self.stride = full.shape[1] // 2
        self.sends, self.recvs, self.passed = sends, recvs, passed

    def window(self, h):
        return pl.ds(pl.multiple_of(h * self.stride + self.offset, 128), self.cols)

    def piece(self, q, h):
        return self.full.at[pl.ds(pl.multiple_of(q * self.rows, 16), self.rows), self.window(h)]

    def stage(self, kind, r):
        p = self.place
        yes = p.z >= 0
        up = ((p.me + 4, p.core), p.z < ZS - 1)
        down = ((p.me - 4, p.core), p.z > 0)
        near = ((p.near, p.core), yes)
        far = ((p.far, p.core), yes)
        other = (p.partner(), None)
        if kind == OWN:
            return [(p.me, yes, [up, down, near, far])]
        base = {COLUMN: p.me, NEAR: p.near, FAR: p.far, DIAG: p.diag}[kind]
        ways = [(-4 * r, p.z >= r, up), (4 * r, p.z + r < ZS, down)] if r else [(0, yes, None)]
        onward = {COLUMN: [near, far, other], NEAR: [far, other], FAR: [other], DIAG: [other]}[kind]
        return [(base + shift, there, ([way] if kind == COLUMN else []) + onward) for shift, there, way in ways]

    def copies(self, kind, q, targets):
        p = self.place
        dst = self.piece(q, p.core)
        src = self.own.at[:, self.window(p.core)] if kind == OWN else dst
        made = []
        for n, (dev, cond) in enumerate(targets):
            recv = self.passed.at[q] if cond is None else self.recvs.at[q]
            made.append((send(src, dst, self.sends.at[n, q], recv, dev), cond))
        return made

    def run(self, kind, r):
        if kind == END:
            return self.finish_partner()
        for q, there, targets in self.stage(kind, r):

            def go(q=q, targets=targets):
                if kind != OWN:
                    piece = self.piece(q, self.place.core)
                    send(piece, piece, self.sends.at[0, q], self.recvs.at[q], self.place.partner()).wait_recv()
                for copy, cond in self.copies(kind, q, targets):
                    copy.start() if cond is None else pl.when(cond)(copy.start)

            pl.when(there)(go)

    def finish_sends(self, kind, r):
        if kind == END:
            return
        for q, there, targets in self.stage(kind, r):

            def go(q=q, targets=targets):
                for copy, cond in self.copies(kind, q, targets):
                    copy.wait_send() if cond is None else pl.when(cond)(copy.wait_send)

            pl.when(there)(go)

    def finish_partner(self):
        p = self.place

        @pl.loop(0, 4 * ZS)
        def _(q):
            @pl.when(q != p.me)
            def _():
                piece = self.piece(q, 1 - p.core)
                send(piece, piece, self.sends.at[0, q], self.passed.at[q], p.partner()).wait_recv()


class Scatter:
    def __init__(self, place, grad, rows, out, mine, pair, far, near, low, high, own, got, sems):
        self.place = place
        self.grad, self.rows, self.out = grad, rows, out
        self.mine, self.pair, self.far, self.near, self.low, self.high, self.own, self.got = mine, pair, far, near, low, high, own, got
        self.sems = sems
        self.cols = grad.shape[1] // 2

    LOCAL, PAIR_S, PAIR_R, LAST_S, LAST_R, FAR_S, FAR_R = 0, 1, 2, 3, 4, 8, 16
    NEAR_S, NEAR_R, UP_S, UP_R, DOWN_S, DOWN_R = 24, 28, 32, 36, 40, 44
    COUNT = 48

    def columns(self, h):
        return pl.ds(pl.multiple_of(h * self.cols, 128), self.cols)

    def at(self, ref, q):
        return ref.at[pl.ds(pl.multiple_of(q * self.rows, 16), self.rows), :]

    def load(self, ref, q):
        return ref[pl.ds(pl.multiple_of(q * self.rows, 16), self.rows), :]

    def store(self, ref, q, value):
        ref[pl.ds(pl.multiple_of(q * self.rows, 16), self.rows), :] = value.astype(ref.dtype)

    def copy_local(self):
        return pltpu.make_async_copy(
            self.grad.at[:, self.columns(self.place.core)], self.mine, self.sems.at[self.LOCAL]
        )

    def copy_pair(self):
        p = self.place
        return send(
            self.grad.at[:, self.columns(1 - p.core)],
            self.pair,
            self.sems.at[self.PAIR_S],
            self.sems.at[self.PAIR_R],
            p.partner(),
        )

    def copy_far(self, k):
        p = self.place
        q = p.chip(k // 2, 1 - p.far_bit, k % 2)
        return send(
            self.at(self.mine, q),
            self.at(self.far, k),
            self.sems.at[self.FAR_S + k],
            self.sems.at[self.FAR_R + k],
            (p.far, p.core),
        )

    def copy_near(self, z):
        p = self.place
        return send(
            self.at(self.far, z * 2 + 1 - p.near_bit),
            self.at(self.near, z),
            self.sems.at[self.NEAR_S + z],
            self.sems.at[self.NEAR_R + z],
            (p.near, p.core),
        )

    def copy_up(self, z):
        p = self.place
        return send(
            self.at(self.near, z),
            self.at(self.low, z),
            self.sems.at[self.UP_S + z],
            self.sems.at[self.UP_R + z],
            (p.me + 4, p.core),
        )

    def copy_down(self, z):
        p = self.place
        return send(
            self.at(self.near, z),
            self.at(self.high, z),
            self.sems.at[self.DOWN_S + z],
            self.sems.at[self.DOWN_R + z],
            (p.me - 4, p.core),
        )

    def copy_last(self):
        p = self.place
        return send(
            self.own,
            self.got,
            self.sems.at[self.LAST_S],
            self.sems.at[self.LAST_R],
            p.partner(),
        )

    def start(self):
        self.copy_local().start()
        self.copy_pair().start()

    def to_far(self):
        p = self.place
        self.copy_local().wait()
        self.copy_pair().wait_recv()

        @pl.loop(0, 8)
        def _(k):
            q = p.chip(k // 2, 1 - p.far_bit, k % 2)
            self.store(self.mine, q, self.load(self.mine, q) + self.load(self.pair, q))
            self.copy_far(k).start()

    def to_near(self):
        p = self.place

        def add(k):
            q = p.chip(k // 2, p.far_bit, k % 2)
            self.copy_far(k).wait_recv()
            self.store(
                self.far, k, self.load(self.far, k) + self.load(self.mine, q) + self.load(self.pair, q)
            )

        @pl.loop(0, 4)
        def _(z):
            add(z * 2 + 1 - p.near_bit)
            self.copy_near(z).start()

        @pl.loop(0, 4)
        def _(z):
            add(z * 2 + p.near_bit)

    def to_line(self):
        p = self.place

        @pl.loop(0, 4)
        def _(z):
            self.copy_near(z).wait_recv()
            self.store(self.near, z, self.load(self.near, z) + self.load(self.far, z * 2 + p.near_bit))

        @pl.when(p.z == 0)
        def _():
            for z in (3, 2, 1):
                self.copy_up(z).start()

        @pl.when(p.z == ZS - 1)
        def _():
            for z in (0, 1, 2):
                self.copy_down(z).start()

    def along(self, step):
        p = self.place

        @pl.when(p.z == step)
        def _():
            for z in (3, 2, 1):
                if z >= step:
                    self.copy_up(z).wait_recv()
                if z > step:
                    self.store(self.near, z, self.load(self.near, z) + self.load(self.low, z))
                    self.copy_up(z).start()

        @pl.when(p.z == ZS - 1 - step)
        def _():
            for z in (0, 1, 2):
                if z <= ZS - 1 - step:
                    self.copy_down(z).wait_recv()
                if z < ZS - 1 - step:
                    self.store(self.near, z, self.load(self.near, z) + self.load(self.high, z))
                    self.copy_down(z).start()

    def to_last(self):
        p = self.place
        self.own[...] = self.load(self.near, p.z).astype(single)

        @pl.when(p.z > 0)
        def _():
            self.own[...] += self.load(self.low, p.z).astype(single)

        @pl.when(p.z < ZS - 1)
        def _():
            self.own[...] += self.load(self.high, p.z).astype(single)

        self.copy_last().start()
        self.out[:, self.columns(p.core)] = self.own[...]

    def finish(self):
        p = self.place
        self.copy_pair().wait_send()

        @pl.loop(0, 8)
        def _(k):
            self.copy_far(k).wait_send()

        @pl.loop(0, 4)
        def _(z):
            self.copy_near(z).wait_send()

            @pl.when(z > p.z)
            def _():
                self.copy_up(z).wait_send()

            @pl.when(z < p.z)
            def _():
                self.copy_down(z).wait_send()

        self.copy_last().wait()
        self.out[:, self.columns(1 - p.core)] = self.got[...]

    def stages(self):
        return [
            self.start,
            self.to_far,
            self.to_near,
            self.to_line,
            lambda: self.along(1),
            lambda: self.along(2),
            lambda: self.along(3),
            self.to_last,
            self.finish,
        ]

    @staticmethod
    def scratch(shape):
        total, cols = shape[0], shape[1] // 2
        rows = total // 16
        return [
            pltpu.VMEM((total, cols), half),
            pltpu.VMEM((total, cols), half),
            pltpu.VMEM((8 * rows, cols), half),
            pltpu.VMEM((4 * rows, cols), half),
            pltpu.VMEM((4 * rows, cols), half),
            pltpu.VMEM((4 * rows, cols), half),
            pltpu.VMEM((rows, cols), single),
            pltpu.VMEM((rows, cols), single),
            pltpu.SemaphoreType.DMA((Scatter.COUNT,)),
        ]


class Total:
    COUNT = 12

    def __init__(self, place, start, pair, result, parts, held, sems):
        self.place, self.first, self.pair, self.result = place, start, pair, result
        self.parts, self.held, self.sems = parts, held, sems

    def copy(self, n):
        p = self.place
        if n == 0:
            src, dev = self.first, p.partner()
        elif n <= 3:
            src, dev = self.held.at[0], ((p.me + 4 * n) % (4 * ZS), p.core)
        elif n == 4:
            src, dev = self.held.at[1], (p.near, p.core)
        else:
            src, dev = self.held.at[2], (p.far, p.core)
        return send(src, self.parts.at[n], self.sems.at[n], self.sems.at[6 + n], dev)

    def stages(self):
        def begin():
            if self.pair:
                self.copy(0).start()

        def column():
            value = self.first[...]
            if self.pair:
                self.copy(0).wait_recv()
                value = value + self.parts[0]
            self.held[0] = value
            for n in (1, 2, 3):
                self.copy(n).start()

        def near():
            value = self.held[0]
            for n in (1, 2, 3):
                self.copy(n).wait_recv()
                value = value + self.parts[n]
            self.held[1] = value
            self.copy(4).start()

        def far():
            self.copy(4).wait_recv()
            self.held[2] = self.held[1] + self.parts[4]
            self.copy(5).start()

        def finish():
            self.copy(5).wait_recv()
            self.result[...] = self.held[2] + self.parts[5]
            for n in range(0 if self.pair else 1, 6):
                self.copy(n).wait_send()

        return [begin, column, near, far, finish]

    @staticmethod
    def scratch(shape):
        return [
            pltpu.VMEM((6,) + shape, single),
            pltpu.VMEM((3,) + shape, single),
            pltpu.SemaphoreType.DMA((Total.COUNT,)),
        ]


PAIRS = 2


FRONT_PLAN = [
    (-1, 0, 0, 0), (-1, 1, 0, 0), (-1, 0, 2, 0), (-1, 0, 3, 0), (-1, 0, 1, 1), (-1, 1, 2, 0),
    (-1, 1, 3, 0), (-1, 1, 1, 1), (-1, 0, 4, 0), (-1, 0, 1, 2), (-1, 1, 1, 2), (-1, 0, 2, 1),
    (-1, 0, 3, 1), (-1, 1, 4, 0), (-1, 1, 2, 1), (-1, 0, 1, 3), (-1, 0, 2, 2), (-1, 1, 1, 3),
    (-1, 1, 3, 1), (-1, 1, 2, 2), (-1, 0, 3, 2), (-1, 1, 3, 2), (-1, 0, 2, 3), (-1, 0, 3, 3),
    (-1, 0, 4, 1), (-1, 1, 2, 3), (-1, 1, 4, 1), (-1, 1, 3, 3), (-1, 0, 4, 2), (-1, 1, 4, 2),
    (-1, 0, 4, 3), (-1, 1, 4, 3), (-1, 0, 5, 0), (-1, 1, 5, 0), (0, 2, 0, 0), (0, 3, 0, 0),
    (0, 4, 0, 0), (0, 2, 2, 0), (0, 2, 1, 1), (0, 2, 3, 0), (1, 3, 2, 0), (1, 3, 3, 0),
    (1, 3, 1, 1), (3, 4, 2, 0), (3, 4, 1, 1), (3, 2, 1, 2), (3, 4, 3, 0), (4, 2, 4, 0),
    (4, 2, 2, 1), (5, 2, 3, 1), (6, 3, 1, 2), (7, 3, 4, 0), (8, 2, 1, 3), (8, 3, 2, 1),
    (8, 4, 1, 2), (10, 3, 1, 3), (11, 2, 2, 3), (11, 3, 3, 1), (13, 2, 2, 2), (13, 4, 4, 0),
    (13, 4, 2, 1), (13, 4, 1, 3), (15, 3, 2, 2), (15, 3, 2, 3), (16, 2, 3, 3), (17, 2, 3, 2),
    (17, 4, 3, 1), (17, 4, 2, 2), (17, 4, 2, 3), (18, 2, 4, 1), (19, 3, 3, 2), (20, 3, 3, 3),
    (21, 2, 4, 3), (21, 3, 4, 1), (22, 2, 4, 2), (22, 4, 3, 2), (22, 4, 3, 3), (24, 2, 5, 0),
    (24, 4, 4, 1), (25, 3, 4, 3), (26, 3, 4, 2), (27, 4, 4, 2), (27, 4, 4, 3), (28, 3, 5, 0),
    (31, 4, 5, 0),
]
SMALL_AT = (2, 20, 27, 32)


def front_body(links, *refs):
    tok_ref, flag_ref, mask_ref, small_ref = refs[:4]
    step = pl.program_id(0)
    count = pl.num_programs(0)
    per_group = 1 + HEADS // (2 * PAIRS)
    actions = {}
    if links:
        shards, (inp_ref, proj_ref, mixed_ref, log_ref, vec_ref) = refs[4:8], refs[8:13]
        fulls, w_ref, own, rest = refs[13:17], refs[17], refs[18:21], refs[21:]
        place = Place()
        local = rest[0]
        sets = [rest[1 + 3 * n : 4 + 3 * n] for n in range(5)]
        total = Total(place, small_ref, False, vec_ref, *rest[16:19])
        rows = [shard.shape[0] for shard in shards]
        mine = pl.ds(pl.multiple_of(place.me * rows[0], 16), rows[0])
        cut = w_ref.shape[1] // 2
        first = cut // 2 // 128 * 128 + 128
        parts = [
            Gather(place, w_ref.at[mine], w_ref, rows[0], 0, first, *sets[0]),
            Gather(place, w_ref.at[mine], w_ref, rows[0], first, cut - first, *sets[1]),
        ]
        parts += [Gather(place, own[t], fulls[t + 1], rows[t + 1], 0, fulls[t + 1].shape[1] // 2, *sets[t + 2]) for t in range(3)]
        keep = pltpu.make_async_copy(w_ref, fulls[0], local.at[0])
        mine_to = [
            pltpu.make_async_copy(
                own[t], fulls[t + 1].at[pl.ds(pl.multiple_of(place.me * rows[t + 1], 16), rows[t + 1]), :], local.at[t + 1]
            )
            for t in range(3)
        ]

        def enter():
            sem, expect = place.barrier()
            w_ref[mine, :] = shards[0][...].astype(half)
            for t in range(3):
                own[t][...] = shards[t + 1][...].astype(half)
            pl.semaphore_wait(sem, expect)
            for copy in mine_to:
                copy.start()

        stages = total.stages()
        todo = [(-1, enter)]
        seen = 0
        for n, part, kind, r in FRONT_PLAN:
            if seen in SMALL_AT:
                todo.append((-1, stages[1 + SMALL_AT.index(seen)]))
            todo.append((n, functools.partial(parts[part].run, kind, r)))
            seen += 1
        todo.append((0, keep.start))

        def leave():
            keep.wait()
            for copy in mine_to:
                copy.wait()
            for _, part, kind, r in FRONT_PLAN:
                parts[part].finish_sends(kind, r)

        for n, action in sorted(todo, key=lambda item: item[0]):
            actions.setdefault(front_point(per_group, n), []).append(action)
        actions.setdefault((4 * per_group - 1, 2), []).append(leave)
    else:
        w_ref, (inp_ref, proj_ref, mixed_ref, log_ref, vec_ref) = refs[4], refs[5:]
        vec_ref[...] = small_ref[...]

    def talk(point):
        for (at, where), todo in sorted(actions.items(), key=lambda item: item[0]):
            if where == point:

                def run_all(todo=todo):
                    for action in todo:
                        action()

                pl.when(step == at)(run_all)

    talk(0)
    column = step % per_group - 1
    wide = 128 * PAIRS
    width = inp_ref.shape[1]

    @pl.when(column < 0)
    def _():
        masked = flag_ref[...] > 0
        low = jnp.where(masked, mask_ref[...].astype(single), tok_ref[...].astype(single)).astype(half)
        inp_ref[...] = low
        for n in range(3):
            cols = pl.ds(n * width, width)
            value = mm(low, w_ref[:, cols])
            if n != 1:
                value = value + vec_ref[pl.ds(n // 2, 1), :]
            proj_ref[:, cols] = value.astype(half)

    @pl.when(column >= 0)
    def _():
        for p in range(PAIRS):
            start = column * wide + 128 * p
            q, k, v = (proj_ref[:, pl.ds(pl.multiple_of(start + n * width, 128), 128)] for n in range(3))
            mixed, logs = attend_pair(q, k, v)
            mixed_ref[:, pl.ds(128 * p, 128)] = mixed
            for h in range(2):
                log_ref[0, 0, pl.ds(2 * p + h, 1), :] = logs[h]
            if p + 1 < PAIRS:
                talk(1)

    talk(2)


def front_point(per_group, n):
    points = 1 + (per_group - 1) * PAIRS
    if n < 0:
        return (0, 0)
    if n >= 4 * points:
        return (4 * per_group - 1, 2)
    group, n = n // points, n % points
    if n == 0:
        return (group * per_group, 0)
    return (group * per_group + 1 + (n - 1) // PAIRS, (n - 1) % PAIRS)


def front(links, tokens, flags, mask_embed, small, shards):
    count, width = tokens.shape
    groups = count // SEQ
    wide = 128 * PAIRS
    steps = width // wide
    per_group = steps + 1
    group = lambda cols: pl.BlockSpec((SEQ, cols), lambda s: (s // per_group, 0))
    whole = lambda shape: pl.BlockSpec(shape, lambda s: (0,) * len(shape), pipeline_mode=pl.Buffered(1))
    column = lambda s: jnp.maximum(s % per_group - 1, 0)
    anywhere = pl.BlockSpec(memory_space=pl.ANY)
    in_specs = [group(width), group(1), whole((1, width)), whole(small.shape)] + [whole(s.shape) for s in shards]
    out_specs = [
        group(width),
        group(3 * width),
        pl.BlockSpec((SEQ, wide), lambda s: (s // per_group, column(s))),
        pl.BlockSpec((1, 1, 8, SEQ), lambda s: (s // per_group, column(s), 0, 0)),
        whole(small.shape),
    ]
    out_shape = [
        jax.ShapeDtypeStruct((count, width), half),
        jax.ShapeDtypeStruct((count, 3 * width), half),
        jax.ShapeDtypeStruct((count, width), half),
        jax.ShapeDtypeStruct((groups, steps, 8, SEQ), single),
        jax.ShapeDtypeStruct(small.shape, single),
    ]
    scratch = []
    params = pltpu.CompilerParams(vmem_limit_bytes=VMEM_LIMIT)
    if links:
        full = [(4 * ZS * s.shape[0], s.shape[1]) for s in shards]
        out_specs += [anywhere] * 4
        out_shape += [jax.ShapeDtypeStruct(shape, half) for shape in full]
        scratch += [pltpu.VMEM(full[0], half)] + [pltpu.VMEM(s.shape, half) for s in shards[1:]]
        scratch.append(pltpu.SemaphoreType.DMA((4,)))
        for _ in range(5):
            scratch += [pltpu.SemaphoreType.DMA((4, 4 * ZS))] + [pltpu.SemaphoreType.DMA((4 * ZS,))] * 2
        scratch += Total.scratch(small.shape)
        params = pltpu.CompilerParams(collective_id=1, has_side_effects=True, vmem_limit_bytes=VMEM_LIMIT)
    return pl.pallas_call(
        functools.partial(front_body, links),
        grid=(groups * per_group,),
        in_specs=in_specs,
        out_specs=out_specs,
        out_shape=out_shape,
        scratch_shapes=scratch,
        compiler_params=params,
        name="front",
    )(tokens, flags, mask_embed, small, *shards)


def back_body(links, steps, *refs):
    q_ref, k_ref, v_ref, grad_ref, mixed_ref, log_ref, inp_ref, w_ref, dsum_ref, flag_ref, small_ref = refs[:11]
    rest = refs[11:]
    step = pl.program_id(0)
    width = inp_ref.shape[1]
    count = inp_ref.shape[0]
    wide = 128 * PAIRS
    per_group = width // wide
    attends = (count // SEQ) * per_group
    weights = 3 * (width // 256)
    actions = {}

    if links:
        grads, (out_ref, g_qkv, g_out, g_up, g_down, total_ref) = rest[:3], rest[3:9]
        parts_ref, made, sums, fixed = rest[9], rest[10], rest[11], rest[12:]
        place = Place()
        runs = []
        sources = [(grads[2], g_down), (grads[1], g_up), (grads[0], g_out)]
        sources += [(made.at[n], g_qkv.at[:, pl.ds(n * width, width)]) for n in range(3)]
        for n, (src, dst) in enumerate(sources):
            runs.append(Scatter(place, src, src.shape[0] // 16, dst, *fixed[9 * n : 9 * n + 9]))
        runs.append(Total(place, sums, True, total_ref, *fixed[9 * len(sources) :]))

        def enter():
            sem, expect = place.barrier()
            pl.semaphore_wait(sem, expect)

        actions[(0, 0)] = [enter]
        order = [(n, which, stage) for which, row in enumerate(BACK_PLAN) for stage, n in enumerate(row)]
        for n, which, stage in sorted(order):
            actions.setdefault(back_point(attends, steps, n), []).append(runs[which].stages()[stage])
    else:
        out_ref, made, total_ref = rest[:3]
        parts_ref, sums = rest[3:]

    def talk(point):
        for (at, where), todo in sorted(actions.items(), key=lambda item: item[0]):
            if where == point:

                def run_all(todo=todo):
                    for action in todo:
                        action()

                pl.when(step == at)(run_all)

    @pl.when(step == 0)
    def _():
        sums[...] = small_ref[...]

    talk(0)

    @pl.when(step < attends)
    def _():
        group = step // per_group
        column = step % per_group
        rows = pl.ds(pl.multiple_of(group * SEQ, SEQ), SEQ)
        logs = log_ref[0, 0].T
        for p in range(PAIRS):
            cols = pl.ds(128 * p, 128)
            done = attend_back_pair(
                q_ref[:, cols],
                k_ref[:, cols],
                v_ref[:, cols],
                grad_ref[:, cols],
                mixed_ref[:, cols],
                logs[:, 2 * p : 2 * p + 2],
            )
            where = pl.ds(pl.multiple_of(column * wide + 128 * p, 128), 128)
            for n in range(3):
                parts_ref[n, rows, where] = done[n]
            if p + 1 < PAIRS:
                talk(1)

    @pl.when((step >= attends) & (step < attends + weights))
    def _():
        part = (step - attends) // (width // 256)
        cols = pl.ds(pl.multiple_of((step - attends) % (width // 256) * 256, 256), 256)
        grad = parts_ref[part, :, cols]
        made[part, :, cols] = mm_ta(inp_ref[...], grad).astype(half)
        column = col_sum(grad.astype(single))

        @pl.when(part == 0)
        def _():
            sums[pl.ds(0, 1), cols] = column

        @pl.when(part == 2)
        def _():
            sums[pl.ds(1, 1), cols] = column

    @pl.when(step >= attends + weights)
    def _():
        block = out_ref.shape[0]
        rows = pl.ds(pl.multiple_of((step - attends - weights) * block, block), block)
        grad = dsum_ref[...]
        for n in range(3):
            grad = grad + mm_tb(parts_ref[n, rows, :], w_ref[:, pl.ds(n * width, width)])
        out_ref[...] = jnp.where(flag_ref[...] > 0, 0.0, grad).astype(half)

    talk(2)
    if not links:
        total_ref[...] = sums[...]


def back(links, projected, d_mixed, mixed, logs, inputs, w_qkv, d_sum, flags, small, grads):
    count, width = mixed.shape
    groups = count // SEQ
    wide = 128 * PAIRS
    per_group = width // wide
    attends = groups * per_group
    weights = 3 * (width // 256)
    block = 256
    steps = attends + weights + count // block
    last = attends - 1

    def group_of(s):
        return jnp.minimum(s, last) // per_group

    def column_of(s):
        return jnp.minimum(s, last) % per_group

    def late(s):
        return jnp.maximum(s - attends - weights, 0)

    spec = lambda part: pl.BlockSpec((SEQ, wide), lambda s: (group_of(s), part * per_group + column_of(s)))
    whole = lambda shape: pl.BlockSpec(shape, lambda s: (0,) * len(shape), pipeline_mode=pl.Buffered(1))
    anywhere = pl.BlockSpec(memory_space=pl.ANY)
    in_specs = [
        spec(0),
        spec(1),
        spec(2),
        spec(0),
        spec(0),
        pl.BlockSpec((1, 1, 8, SEQ), lambda s: (group_of(s), column_of(s), 0, 0)),
        whole(inputs.shape),
        whole(w_qkv.shape),
        pl.BlockSpec((block, width), lambda s: (late(s), 0)),
        pl.BlockSpec((block, 1), lambda s: (late(s), 0)),
        whole(small.shape),
    ]
    out_specs = [pl.BlockSpec((block, width), lambda s: (late(s), 0))]
    out_shape = [jax.ShapeDtypeStruct((count, width), half)]
    operands = [projected, projected, projected, d_mixed, mixed, logs, inputs, w_qkv, d_sum, flags, small]
    dparts = pltpu.VMEM((3, count, width), half)
    sums = pltpu.VMEM(small.shape, single)
    if links:
        in_specs += [anywhere] * 3
        operands += grads
        shapes = [(width // 16, 3 * width)] + [(g.shape[0] // 16, g.shape[1]) for g in grads] + [small.shape]
        out_specs += [whole(shape) for shape in shapes]
        out_shape += [jax.ShapeDtypeStruct(shape, single) for shape in shapes]
        scratch = [dparts, pltpu.VMEM((3, width, width), half), sums]
        for shape in [grads[2].shape, grads[1].shape, grads[0].shape] + [(width, width)] * 3:
            scratch += Scatter.scratch(shape)
        scratch += Total.scratch(small.shape)
        params = pltpu.CompilerParams(collective_id=2, has_side_effects=True, vmem_limit_bytes=VMEM_LIMIT)
    else:
        out_specs += [whole((3, width, width)), whole(small.shape)]
        out_shape += [jax.ShapeDtypeStruct((3, width, width), half), jax.ShapeDtypeStruct(small.shape, single)]
        scratch = [dparts, sums]
        params = pltpu.CompilerParams(vmem_limit_bytes=VMEM_LIMIT)
    return pl.pallas_call(
        functools.partial(back_body, links, steps),
        grid=(steps,),
        in_specs=in_specs,
        out_specs=out_specs,
        out_shape=out_shape,
        scratch_shapes=scratch,
        compiler_params=params,
        name="back",
    )(*operands)


BACK_PLAN = [
    [0, 4, 13, 22, 29, 34, 36, 36, 37],
    [0, 6, 23, 28, 34, 38, 41, 41, 45],
    [0, 6, 24, 29, 35, 38, 41, 41, 45],
    [27, 29, 33, 35, 37, 39, 41, 41, 45],
    [30, 32, 35, 37, 39, 41, 50, 50, 55],
    [33, 34, 37, 39, 41, 52, 62, 62, 67],
    [33, 35, 37, 39, 42],
]


def back_point(attends, steps, n):
    if n < 2 * attends:
        return n // 2, n % 2
    n -= attends
    return (n, 0) if n < steps else (steps - 1, 2)


def local(chips, twins, tokens, flags, mask_embed, cotangent, w_qkv, b_qv, w_out, b_out, norm_one, w_up, b_up, w_down, b_down, norm_two):
    links = chips == 4 * ZS and twins == 2
    n = b_out.shape[0]
    width = chips * n
    me = lax.axis_index("dp")
    vectors = jnp.stack([b_qv[0], b_qv[1], b_out, norm_one[0], norm_one[1], b_down, norm_two[0], norm_two[1]])
    vectors = lax.dynamic_update_slice(jnp.zeros((8, width), single), vectors, (0, me * n))
    hidden = lax.dynamic_update_slice(jnp.zeros((4 * width,), single), b_up, (me * 4 * n,)).reshape(4, width)
    small = jnp.concatenate([vectors, hidden, jnp.zeros_like(hidden)])
    small = lax.reduce_precision(small, 8, 7)
    shards = [w_qkv, w_out, w_up, w_down]
    flag_col = flags[:, None]
    if links:
        inputs, projected, mixed, logs, vecs, qkv_full, out_full, up_full, down_full = front(
            True, tokens, flag_col, mask_embed[None], small, shards
        )
    else:
        qkv_full, out_full, up_full, down_full = [
            lax.all_gather(s.astype(half), "dp", axis=0, tiled=True) for s in shards
        ]
        small = lax.psum(small, "dp")
        inputs, projected, mixed, logs, vecs = front(False, tokens, flag_col, mask_embed[None], small, [qkv_full])
    activations, d_sum, d_mixed, g_small, g_out, g_up, g_down = middle(
        mixed, inputs, flag_col, cotangent, vecs, out_full, up_full, down_full
    )
    grads = [g_out, g_up, g_down]
    input_grad, g_qkv, *summed = back(
        links, projected, d_mixed, mixed, logs, inputs, qkv_full, d_sum, flag_col, g_small, grads
    )
    if links:
        g_out, g_up, g_down, g_small = summed
    else:
        g_small = summed[0]
        grads = [jnp.concatenate([g_qkv[0], g_qkv[1], g_qkv[2]], axis=1)] + grads
        grads = [lax.psum_scatter(g.astype(single), "dp", scatter_dimension=0, tiled=True) for g in grads]
        g_qkv, g_out, g_up, g_down = [lax.psum(g.astype(half), "rep").astype(single) for g in grads]
        g_small = lax.psum(g_small, ("dp", "rep"))
    rows = lax.dynamic_slice_in_dim(g_small[:8], me * n, n, axis=1)
    g_bup = lax.dynamic_slice_in_dim(g_small[8:12].reshape(4 * width), me * 4 * n, 4 * n)
    return (
        activations,
        input_grad.astype(single),
        g_qkv,
        rows[0:2],
        g_out,
        rows[2],
        rows[3:5],
        g_up,
        g_bup,
        g_down,
        rows[5],
        rows[6:8],
    )


def solution(mesh):
    rows = P(("dp", "rep"), None)
    first = P("dp", None)
    second = P(None, "dp")
    return jax.shard_map(
        functools.partial(local, mesh.shape["dp"], mesh.shape["rep"]),
        mesh=mesh,
        in_specs=(rows, P(("dp", "rep")), P(), rows, first, second, first, P("dp"), second, first, P("dp"), first, P("dp"), second),
        out_specs=(rows, rows, first, second, first, P("dp"), second, first, P("dp"), first, P("dp"), second),
        check_vma=False,
    )
```
